32 devices in a mesh: src: 4 (over z), dst: 8 (over y, x, core).
Axes of the slice: x: 2, y: 2, z: 4, core: 2. Of those that a mesh axis runs over, the one named last changes fastest.
Arguments:
- table: float32 [65536, 400], P(('src', 'dst')), may hold values from -2 to 2
- state: float32 [65536], P(('src', 'dst')), may hold values from 0.0001 to 0.01
- relations: float32 [4096, 400], replicated, may hold values from -4 to 4
- rel_ids: int32 [65536], P(('src', 'dst')), may hold values from 0 to 4095
- block_list: int32 [32, 32], P(('src', 'dst')), may hold values from 0 to 15
- src_pos: int32 [65536], P(('src', 'dst')), may hold values from 0 to 4095, as said below
- dst_pos: int32 [65536], P(('src', 'dst')), may hold values from 0 to 4095, as said below
- neg_pos: int32 [4096], P(('src', 'dst')), may hold values from 0 to 4095, as said below
Outputs:
- new_table: float32 [65536, 400], P(('src', 'dst'))
- new_state: float32 [65536], P(('src', 'dst'))
The draws below stay inside these ranges and needn't reach their ends.
Inputs may be any that keep to these rules, and one draw needn't show every extreme that they name: Each entry is owner * 128 + row of a block the device requested; one device's src_pos, dst_pos and neg_pos name the same 16 owners, and its src_pos names each of them. `dst_pos`: rows of the same 16 owners as the device's src_pos. `neg_pos`: rows of the same 16 owners as the device's src_pos.
All inputs are finite; a program needn't handle non-finite values.
Results may differ from the reference program's by a relative error of at most 0.0004.
The reference program's roundings to bfloat16 on the way count: a program that leaves them out, or rounds other values in their place, can miss the bound.
Values may be sent and summed in bfloat16 or wider, within the bound.
No kernel may reach another device: no remote copies, remote signals or barrier semaphores. Data moves between devices by JAX's collectives and lax.ppermute only.
A program may use at most 192 MiB of HBM per device.

```python
import math
import jax
import jax.numpy as jnp
from jax import lax

D = 400
NREL = 4096
BLK = 128
BLK_DEV = 16
EDGES_DEV = 2048
NEG = 1024
ROWS_DEV = 2048
ENT = 65536
NEG_DEV = 128
LIVE = 16
N_SRC = 4
N_DST = 8
DEVICES = 32


def live_owners(key):
    keys = jax.random.split(jax.random.fold_in(key, 7), DEVICES)
    return jax.vmap(lambda one_key: jax.random.permutation(one_key, DEVICES)[:LIVE])(keys)


def draw_positions(key, salt, count, cover):
    live = live_owners(key)
    pick_key, row_key, order_key = jax.random.split(jax.random.fold_in(key, salt), 3)
    pick = jax.random.randint(pick_key, (DEVICES, count), 0, LIVE)
    if cover:
        order_keys = jax.random.split(order_key, DEVICES)
        order = jax.vmap(lambda one_key: jax.random.permutation(one_key, count))(order_keys)
        pick = jnp.where(order < LIVE, order, pick)
    owner = jnp.take_along_axis(live, pick, axis=1)
    within = jax.random.randint(row_key, (DEVICES, count), 0, BLK)
    return (owner * BLK + within).reshape(-1).astype(jnp.int32)


def draw_src_pos(key, part):
    return draw_positions(key, 11, EDGES_DEV, True)


def draw_dst_pos(key, part):
    return draw_positions(key, 13, EDGES_DEV, False)


def draw_neg_pos(key, part):
    return draw_positions(key, 17, NEG_DEV, False)


def touch_ends(result, rng, least, top_value):
    dims = result.shape
    index_at = [jax.random.randint(jax.random.fold_in(rng, axis), (), 0, dims[axis]) for axis in range(len(dims))]
    result = result.at[tuple(index_at)].set(least)
    longest = dims.index(max(dims))
    index_at[longest] = (index_at[longest] + 1) % dims[longest]
    return result.at[tuple(index_at)].set(top_value)


def shard_levels(key, shape, cuts, least, top_value):
    level, own = 1.0, jax.random.fold_in(key, 6)
    for dim, blocks in cuts:
        draws = jnp.exp(jax.random.uniform(jax.random.fold_in(own, dim), (blocks,), jnp.float32, least / len(cuts), top_value / len(cuts)))
        level = level * jnp.repeat(draws, shape[dim] // blocks).reshape([-1 if axis == dim else 1 for axis in range(len(shape))])
    return level


def gaussian(rng, dims, width, reach, pieces=(), kind=jnp.bfloat16):
    entries = jax.random.normal(rng, dims, jnp.float32) * width
    if len(pieces) > 0:
        entries = shard_levels(rng, dims, pieces, -0.22, 0.18) * entries
    return jnp.clip(entries, min=-reach, max=reach).astype(kind)


def setup_inputs(seed: int = 0) -> dict:
    key_list = jax.random.split(jax.random.key(seed), 9)
    return {
        "table": gaussian(key_list[0], (ENT, D), 0.3, 2.0, ((0, 32),), jnp.float32),
        "state": jnp.clip(jnp.exp(math.log(0.01) - 4.6051702 * jax.random.uniform(key_list[1], (ENT,), jnp.float32) ** shard_levels(key_list[1], (ENT,), ((0, 32),), -0.2, 0.2)), 0.0001, 0.01),
        "relations": gaussian(key_list[2], (NREL, D), 1.0, 4.0, (), jnp.float32),
        "rel_ids": touch_ends(jax.random.randint(key_list[3], (DEVICES * EDGES_DEV,), 0, NREL), jax.random.fold_in(key_list[3], 1), 0, NREL - 1).astype(jnp.int32),
        "block_list": touch_ends(jax.random.randint(key_list[4], (DEVICES, DEVICES), 0, BLK_DEV), jax.random.fold_in(key_list[4], 1), 0, BLK_DEV - 1).astype(jnp.int32),
        "src_pos": draw_src_pos(jax.random.fold_in(key_list[8], 71), 0),
        "dst_pos": draw_dst_pos(jax.random.fold_in(key_list[8], 71), 0),
        "neg_pos": draw_neg_pos(jax.random.fold_in(key_list[8], 71), 0),
    }


def global_rows(lists, positions):
    owner = positions // BLK
    within = positions % BLK
    block = jnp.take_along_axis(lists, owner, axis=1)
    return (owner * ROWS_DEV + block * BLK + within).astype(jnp.int32)

def reference(table, state, relations, rel_ids, block_list, src_pos, dst_pos, neg_pos):
    devices = N_SRC * N_DST
    rows = table.astype(jnp.bfloat16)
    src_ids = global_rows(block_list, src_pos.reshape(devices, EDGES_DEV))
    dst_ids = global_rows(block_list, dst_pos.reshape(devices, EDGES_DEV))
    neg_ids = global_rows(block_list, neg_pos.reshape(devices, NEG_DEV)).reshape(N_SRC, NEG)
    rel_rows = rel_ids.reshape(devices, EDGES_DEV)

    def one(device):
        source = rows[src_ids[device]].astype(jnp.float32)
        target = rows[dst_ids[device]].astype(jnp.float32)
        negs = rows[neg_ids[device // N_DST]]
        operator = relations[rel_rows[device]]
        u_full = source * operator
        u_half = u_full.astype(jnp.bfloat16)
        positive = lax.optimization_barrier(jnp.sum(u_full * target, axis=1))
        scores = jnp.dot(u_half, negs.T, preferred_element_type=jnp.float32)
        g_pos = -jax.nn.sigmoid(-positive)
        g_neg = (jax.nn.sigmoid(scores) / NEG).astype(jnp.bfloat16)
        grad_u = g_pos[:, None] * target + jnp.dot(g_neg, negs, preferred_element_type=jnp.float32)
        grad_src = grad_u * operator
        grad_dst = g_pos[:, None] * u_full
        grad_negs = jnp.dot(g_neg.T, u_half, preferred_element_type=jnp.float32)
        return (grad_src, grad_dst, grad_negs)
    grad_src, grad_dst, grad_negs = lax.map(one, jnp.arange(devices, dtype=jnp.int32))
    grad_negs = lax.optimization_barrier(jnp.sum(grad_negs.reshape(N_SRC, N_DST, NEG, D), axis=1))
    grad = jnp.zeros((table.shape[0], D), jnp.float32)
    grad = grad.at[src_ids.reshape(-1)].add(grad_src.reshape(-1, D))
    grad = grad.at[dst_ids.reshape(-1)].add(grad_dst.reshape(-1, D))
    grad = grad.at[neg_ids.reshape(-1)].add(grad_negs.reshape(-1, D))
    new_state = state + lax.optimization_barrier(jnp.mean(grad * grad, axis=1))
    new_table = table - 0.1 * grad / (jnp.sqrt(new_state)[:, None] + 1e-10)
    return (new_table, new_state)
```

```python
import jax
import jax.numpy as jnp
from jax import lax
from jax.experimental import pallas as pl
from jax.experimental.pallas import tpu as pltpu
from jax.sharding import PartitionSpec as P

BLK = 128
TAIL = 8
AXES = ("src", "dst")
VMEM_LIMIT = 40 * 1024 * 1024
F32 = jnp.float32
BF16 = jnp.bfloat16
NT = (((1,), (1,)), ((), ()))


def params():
    return pltpu.CompilerParams(vmem_limit_bytes=VMEM_LIMIT)


def whole():
    return pl.BlockSpec(memory_space=pltpu.VMEM)


def smem():
    return pl.BlockSpec(memory_space=pltpu.SMEM)


def anywhere():
    return pl.BlockSpec(memory_space=pl.ANY)


def load_live(live_ref, fetched, rows, sem):
    count = live_ref.shape[0]

    def copy(k):
        lanes = pl.ds(pl.multiple_of(k * BLK, BLK), BLK)
        return pltpu.make_async_copy(fetched.at[live_ref[k]], rows.at[:, lanes], sem)

    def start(k, _):
        copy(k).start()
        return 0

    def wait(k, _):
        copy(k).wait()
        return 0

    lax.fori_loop(0, count, start, 0)
    lax.fori_loop(0, count, wait, 0)


def pick(rows, positions):
    total = rows.shape[1]
    step = min(total, 2048)
    out = None
    for first in range(0, total, step):
        index = lax.broadcasted_iota(jnp.int32, (step, positions.shape[1]), 0) + first
        hot = jnp.where(index == positions, 1.0, 0.0).astype(BF16)
        part = jnp.dot(rows[:, first : first + step], hot, preferred_element_type=F32)
        out = part if out is None else out + part
    return out


def neg_kernel(live_ref, fetched, pos_ref, out_ref, rows, sem):
    load_live(live_ref, fetched, rows, sem)
    out_ref[...] = pick(rows, pos_ref[...]).astype(BF16)


def gather_negs(live, fetched, pos):
    width = fetched.shape[1]
    return pl.pallas_call(
        neg_kernel,
        out_shape=jax.ShapeDtypeStruct((width, pos.shape[1]), BF16),
        in_specs=[smem(), anywhere(), whole()],
        out_specs=whole(),
        scratch_shapes=[
            pltpu.VMEM((width, live.shape[0] * BLK), BF16),
            pltpu.SemaphoreType.DMA,
        ],
        compiler_params=params(),
        name="gather_negs",
    )(live, fetched, pos)


def edge_kernel(live_ref, fetched, spos, dpos, op_ref, src_ref, dst_ref, gpos_ref, rows, sem):
    @pl.when(pl.program_id(0) == 0)
    def _():
        load_live(live_ref, fetched, rows, sem)

    source = pick(rows, spos[...])
    target = pick(rows, dpos[...])
    u = source * op_ref[...]
    positive = jnp.sum(u * target, axis=0, keepdims=True)
    gpos_ref[...] = -jax.nn.sigmoid(-positive)
    src_ref[...] = source.astype(BF16)
    dst_ref[...] = target.astype(BF16)


def gather_edges(live, fetched, spos, dpos, operator, tile=256):
    width = fetched.shape[1]
    edges = spos.shape[1]
    lane = pl.BlockSpec((1, tile), lambda i: (0, i))
    column = pl.BlockSpec((width, tile), lambda i: (0, i))
    return pl.pallas_call(
        edge_kernel,
        grid=(edges // tile,),
        out_shape=(
            jax.ShapeDtypeStruct((width, edges), BF16),
            jax.ShapeDtypeStruct((width, edges), BF16),
            jax.ShapeDtypeStruct((1, edges), F32),
        ),
        in_specs=[smem(), anywhere(), lane, lane, column],
        out_specs=(column, column, lane),
        scratch_shapes=[
            pltpu.VMEM((width, live.shape[0] * BLK), BF16),
            pltpu.SemaphoreType.DMA,
        ],
        compiler_params=params(),
        name="gather_edges",
    )(live, fetched, spos, dpos, operator)


def split(x):
    high = x.astype(BF16)
    return high, (x - high.astype(F32)).astype(BF16)


def score_kernel(negs_ref, src_ref, dst_ref, op_ref, gpos_ref, gs_ref, gd_ref, gn_ref, wide, tall, acc):
    groups, width, _ = negs_ref.shape
    step = pl.program_id(0)
    count = groups * negs_ref.shape[2]
    each = negs_ref.shape[2]

    @pl.when(step == 0)
    def _():
        for g in range(groups):
            block = negs_ref[g]
            wide[:, g * each : (g + 1) * each] = block
            tall[g * each : (g + 1) * each, :] = block.T
        acc[...] = jnp.zeros_like(acc)

    operator = op_ref[...]
    u = src_ref[...].astype(F32) * operator
    u_half = u.astype(BF16)
    scores = jnp.dot(tall[...], u_half, preferred_element_type=F32)
    g_neg = (jax.nn.sigmoid(scores) / count).astype(BF16)
    g_pos = gpos_ref[...]
    grad_u = g_pos * dst_ref[...].astype(F32) + jnp.dot(wide[...], g_neg, preferred_element_type=F32)
    acc[...] += lax.dot_general(u_half, g_neg, NT, preferred_element_type=F32)
    gs_ref[0], gs_ref[1] = split(grad_u * operator)
    gd_ref[0], gd_ref[1] = split(g_pos * u)

    @pl.when(step == pl.num_programs(0) - 1)
    def _():
        for g in range(groups):
            gn_ref[g] = acc[:, g * each : (g + 1) * each].astype(BF16)


def score(negs, source, target, operator, g_pos, tile=256):
    groups, width, each = negs.shape
    edges = source.shape[1]
    lane = pl.BlockSpec((1, tile), lambda i: (0, i))
    column = pl.BlockSpec((width, tile), lambda i: (0, i))
    pair = pl.BlockSpec((2, width, tile), lambda i: (0, 0, i))
    return pl.pallas_call(
        score_kernel,
        grid=(edges // tile,),
        out_shape=(
            jax.ShapeDtypeStruct((2, width, edges), BF16),
            jax.ShapeDtypeStruct((2, width, edges), BF16),
            jax.ShapeDtypeStruct((groups, width, each), BF16),
        ),
        in_specs=[whole(), column, column, column, lane],
        out_specs=(pair, pair, pl.BlockSpec((groups, width, each), lambda i: (0, 0, 0))),
        scratch_shapes=[
            pltpu.VMEM((width, groups * each), BF16),
            pltpu.VMEM((groups * each, width), BF16),
            pltpu.VMEM((width, groups * each), F32),
        ],
        compiler_params=params(),
        name="score",
    )(negs, source, target, operator, g_pos)


def scatter_kernel(gs_ref, gd_ref, spos, dpos, out_ref):
    tile = out_ref.shape[1]
    width = gs_ref.shape[1]
    edges = gs_ref.shape[2]
    index = lax.broadcasted_iota(jnp.int32, (tile, edges), 0) + pl.program_id(0) * tile
    both = None
    for grads, pos in ((gs_ref, spos), (gd_ref, dpos)):
        hot = jnp.where(index == pos[...], 1.0, 0.0).astype(BF16)
        part = lax.dot_general(
            grads[...].reshape(2 * width, edges), hot, NT, preferred_element_type=F32
        )
        both = part if both is None else both + part
    out_ref[...] = both[:width] + both[width:]


def scatter(grads_src, grads_dst, spos, dpos, rows, tile=256):
    width = grads_src.shape[1]
    return pl.pallas_call(
        scatter_kernel,
        grid=(rows // tile,),
        out_shape=jax.ShapeDtypeStruct((width, rows), F32),
        in_specs=[whole(), whole(), whole(), whole()],
        out_specs=pl.BlockSpec((width, tile), lambda i: (0, i)),
        compiler_params=params(),
        name="scatter",
    )(grads_src, grads_dst, spos, dpos)


def encode(x, out_ref):
    width = x.shape[0]
    top = jnp.max(jnp.abs(x), axis=0, keepdims=True)
    power = jnp.ceil(jnp.log2(jnp.maximum(top, 1e-30)))
    code = jnp.clip(jnp.round(x * jnp.exp2(15.0 - power)), -32767.0, 32767.0)
    out_ref[:width, :] = code.astype(jnp.int32).astype(jnp.int16)
    tail = jnp.broadcast_to(power, (TAIL, x.shape[1]))
    out_ref[width:, :] = tail.astype(jnp.int32).astype(jnp.int16)


def decode(code, width):
    power = code[width : width + 1, :].astype(jnp.int32).astype(F32)
    return code[:width, :].astype(jnp.int32).astype(F32) * jnp.exp2(power - 15.0)


def pack_kernel(rank_ref, live_ref, slots_ref, gn_ref, npos, out_ref):
    group = out_ref.shape[0]
    first = pl.program_id(0) * group
    for k in range(group):
        alive = live_ref[first + k] > 0

        @pl.when(alive)
        def _():
            start = pl.multiple_of(rank_ref[first + k] * BLK, BLK)
            index = lax.broadcasted_iota(jnp.int32, (BLK, npos.shape[1]), 0) + start
            hot = jnp.where(index == npos[...], 1.0, 0.0).astype(BF16)
            part = lax.dot_general(gn_ref[...], hot, NT, preferred_element_type=F32)
            encode(slots_ref[:, pl.ds(start, BLK)] + part, out_ref.at[k])

        @pl.when(jnp.logical_not(alive))
        def _():
            out_ref[k] = jnp.zeros(out_ref.shape[1:], jnp.int16)


def pack(rank, live, slots, grad_negs, npos, group=8):
    devices = rank.shape[0]
    width = slots.shape[0]
    return pl.pallas_call(
        pack_kernel,
        grid=(devices // group,),
        out_shape=jax.ShapeDtypeStruct((devices, width + TAIL, BLK), jnp.int16),
        in_specs=[smem(), smem(), whole(), whole(), whole()],
        out_specs=pl.BlockSpec((group, width + TAIL, BLK), lambda i: (i, 0, 0)),
        compiler_params=params(),
        name="pack",
    )(rank, live, slots, grad_negs, npos)


def update_kernel(asked_ref, back_ref, table_ref, state_ref, table_out, state_out, grad):
    group = back_ref.shape[0]
    width = grad.shape[0]
    step = pl.program_id(0)

    @pl.when(step == 0)
    def _():
        grad[...] = jnp.zeros_like(grad)

    for k in range(group):
        lanes = pl.ds(pl.multiple_of(asked_ref[step * group + k] * BLK, BLK), BLK)
        grad[:, lanes] += decode(back_ref[k], width)

    @pl.when(step == pl.num_programs(0) - 1)
    def _():
        def block(b, _):
            lanes = pl.ds(pl.multiple_of(b * BLK, BLK), BLK)
            g = grad[:, lanes]
            new_state = state_ref[:, lanes] + jnp.sum(g * g, axis=0, keepdims=True) / width
            state_out[:, lanes] = new_state
            table_out[:, lanes] = table_ref[:, lanes] - 0.1 * g / (jnp.sqrt(new_state) + 1e-10)
            return 0

        lax.fori_loop(0, grad.shape[1] // BLK, block, 0)


def update(asked, returned, table, state, group=8):
    devices, coded, _ = returned.shape
    width, rows = table.shape
    return pl.pallas_call(
        update_kernel,
        grid=(devices // group,),
        out_shape=(
            jax.ShapeDtypeStruct((width, rows), F32),
            jax.ShapeDtypeStruct((1, rows), F32),
        ),
        in_specs=[
            smem(),
            pl.BlockSpec((group, coded, BLK), lambda i: (i, 0, 0)),
            pl.BlockSpec((width, rows), lambda i: (0, 0)),
            pl.BlockSpec((1, rows), lambda i: (0, 0)),
        ],
        out_specs=(
            pl.BlockSpec((width, rows), lambda i: (0, 0)),
            pl.BlockSpec((1, rows), lambda i: (0, 0)),
        ),
        scratch_shapes=[pltpu.VMEM((width, rows), F32)],
        compiler_params=params(),
        name="update",
    )(asked, returned, table, state)


def per_device(table, state, relations, rel_ids, block_list, src_pos, dst_pos, neg_pos):
    devices = lax.axis_size(AXES)
    named = devices // 2
    rows_dev, width = table.shape
    blocks = rows_dev // BLK
    wanted = lax.all_to_all(
        block_list.reshape(devices, 1), AXES, split_axis=0, concat_axis=0, tiled=True
    )
    asked = wanted.reshape(devices)
    outgoing = table.reshape(blocks, BLK, width).astype(BF16)[asked]
    fetched = lax.all_to_all(
        outgoing.transpose(0, 2, 1), AXES, split_axis=0, concat_axis=0, tiled=True
    )
    operator = relations[rel_ids].T

    ids = jnp.arange(devices, dtype=jnp.int32)
    alive = jnp.max((src_pos // BLK)[:, None] == ids[None, :], axis=0).astype(jnp.int32)
    rank = jnp.sum(jnp.where(ids[None, :] < ids[:, None], alive[None, :], 0), axis=1)
    slot = jnp.arange(named, dtype=jnp.int32)
    live = jnp.sum(
        jnp.where((rank[None, :] == slot[:, None]) & (alive[None, :] > 0), ids[None, :], 0), axis=1
    )

    def compact(pos):
        place = jnp.sum(jnp.where((pos // BLK)[:, None] == ids[None, :], rank[None, :], 0), axis=1)
        return (place * BLK + pos % BLK).reshape(1, -1)

    spos, dpos, npos = compact(src_pos), compact(dst_pos), compact(neg_pos)

    own_negs = gather_negs(live, fetched, npos)
    negs = lax.all_gather(own_negs, "dst", axis=0, tiled=False)
    source, target, g_pos = gather_edges(live, fetched, spos, dpos, operator)
    grads_src, grads_dst, part_negs = score(negs, source, target, operator, g_pos)
    own_grad = lax.psum_scatter(part_negs, "dst", scatter_dimension=0, tiled=False)
    slots = scatter(grads_src, grads_dst, spos, dpos, named * BLK)
    packed = pack(rank, alive, slots, own_grad, npos)
    returned = lax.all_to_all(packed, AXES, split_axis=0, concat_axis=0, tiled=True)
    new_table, new_state = update(asked, returned, table.T, state.reshape(1, rows_dev))
    return (new_table.T, new_state.reshape(rows_dev))


def solution(mesh):
    in_specs = (
        P(AXES, None),
        P(AXES),
        P(),
        P(AXES),
        P(AXES, None),
        P(AXES),
        P(AXES),
        P(AXES),
    )
    out_specs = (P(AXES, None), P(AXES))
    return jax.shard_map(
        per_device, mesh=mesh, in_specs=in_specs, out_specs=out_specs, check_vma=False
    )
```

```python
import functools

import jax
import jax.numpy as jnp
from jax import lax
from jax.experimental import pallas as pl
from jax.experimental.pallas import tpu as pltpu
from jax.sharding import PartitionSpec as P

BLK = 128
TAIL = 8
AXES = ("src", "dst")
F32 = jnp.float32
BF16 = jnp.bfloat16
NT = (((1,), (1,)), ((), ()))


def params(held):
    return pltpu.CompilerParams(vmem_limit_bytes=14 * 1024 * 1024 + held)


def whole():
    return pl.BlockSpec(memory_space=pltpu.VMEM)


def smem():
    return pl.BlockSpec(memory_space=pltpu.SMEM)


def anywhere():
    return pl.BlockSpec(memory_space=pl.ANY)


def load_live(live_ref, fetched, rows, sem):
    count = live_ref.shape[0]

    def copy(k):
        lanes = pl.ds(pl.multiple_of(k * BLK, BLK), BLK)
        return pltpu.make_async_copy(fetched.at[live_ref[k]], rows.at[:, lanes], sem)

    def start(k, _):
        copy(k).start()
        return 0

    def wait(k, _):
        copy(k).wait()
        return 0

    lax.fori_loop(0, count, start, 0)
    lax.fori_loop(0, count, wait, 0)


def pick(rows, positions):
    total = rows.shape[1]
    step = min(total, 2048)
    out = None
    for first in range(0, total, step):
        index = lax.broadcasted_iota(jnp.int32, (step, positions.shape[1]), 0) + first
        hot = jnp.where(index == positions, 1.0, 0.0).astype(BF16)
        part = jnp.dot(rows[:, first : first + step], hot, preferred_element_type=F32)
        out = part if out is None else out + part
    return out


def neg_kernel(live_ref, fetched, pos_ref, out_ref, rows, sem):
    load_live(live_ref, fetched, rows, sem)
    out_ref[...] = pick(rows, pos_ref[...]).astype(BF16)


def gather_negs(live, fetched, pos):
    width = fetched.shape[1]
    return pl.pallas_call(
        neg_kernel,
        out_shape=jax.ShapeDtypeStruct((width, pos.shape[1]), BF16),
        in_specs=[smem(), anywhere(), whole()],
        out_specs=whole(),
        scratch_shapes=[
            pltpu.VMEM((width, live.shape[0] * BLK), BF16),
            pltpu.SemaphoreType.DMA,
        ],
        compiler_params=params(4 * width * live.shape[0] * BLK),
        name="gather_negs",
    )(live, fetched, pos)


def edge_kernel(live_ref, fetched, spos, dpos, op_ref, src_ref, dst_ref, gpos_ref, rows, sem):
    @pl.when(pl.program_id(0) == 0)
    def _():
        load_live(live_ref, fetched, rows, sem)

    source = pick(rows, spos[...])
    target = pick(rows, dpos[...])
    u = source * op_ref[...]
    positive = jnp.sum(u * target, axis=0, keepdims=True)
    gpos_ref[...] = -jax.nn.sigmoid(-positive)
    src_ref[...] = source.astype(BF16)
    dst_ref[...] = target.astype(BF16)


def gather_edges(live, fetched, spos, dpos, operator, tile=256):
    width = fetched.shape[1]
    edges = spos.shape[1]
    lane = pl.BlockSpec((1, tile), lambda i: (0, i))
    column = pl.BlockSpec((width, tile), lambda i: (0, i))
    return pl.pallas_call(
        edge_kernel,
        grid=(edges // tile,),
        out_shape=(
            jax.ShapeDtypeStruct((width, edges), BF16),
            jax.ShapeDtypeStruct((width, edges), BF16),
            jax.ShapeDtypeStruct((1, edges), F32),
        ),
        in_specs=[smem(), anywhere(), lane, lane, column],
        out_specs=(column, column, lane),
        scratch_shapes=[
            pltpu.VMEM((width, live.shape[0] * BLK), BF16),
            pltpu.SemaphoreType.DMA,
        ],
        compiler_params=params(4 * width * live.shape[0] * BLK),
        name="gather_edges",
    )(live, fetched, spos, dpos, operator)


def split(x):
    high = x.astype(BF16)
    return high, (x - high.astype(F32)).astype(BF16)


def score_kernel(groups, *refs):
    negs = refs[:groups]
    src_ref, dst_ref, op_ref, gpos_ref, gs_ref, gd_ref = refs[groups : groups + 6]
    outs = refs[groups + 6 : 2 * groups + 6]
    wide, tall, acc = refs[2 * groups + 6 :]
    step = pl.program_id(0)
    each = negs[0].shape[1]
    count = groups * each

    @pl.when(step == 0)
    def _():
        for g in range(groups):
            block = negs[g][...]
            wide[:, g * each : (g + 1) * each] = block
            tall[g * each : (g + 1) * each, :] = block.T
        acc[...] = jnp.zeros_like(acc)

    operator = op_ref[...]
    u = src_ref[...].astype(F32) * operator
    u_half = u.astype(BF16)
    scores = jnp.dot(tall[...], u_half, preferred_element_type=F32)
    g_neg = (jax.nn.sigmoid(scores) / count).astype(BF16)
    g_pos = gpos_ref[...]
    grad_u = g_pos * dst_ref[...].astype(F32) + jnp.dot(wide[...], g_neg, preferred_element_type=F32)
    acc[...] += lax.dot_general(u_half, g_neg, NT, preferred_element_type=F32)
    gs_ref[0], gs_ref[1] = split(grad_u * operator)
    gd_ref[0], gd_ref[1] = split(g_pos * u)

    @pl.when(step == pl.num_programs(0) - 1)
    def _():
        for g in range(groups):
            outs[g][...] = acc[:, g * each : (g + 1) * each].astype(BF16)


def score(negs, source, target, operator, g_pos, tile=256):
    groups = len(negs)
    width, each = negs[0].shape
    edges = source.shape[1]
    lane = pl.BlockSpec((1, tile), lambda i: (0, i))
    column = pl.BlockSpec((width, tile), lambda i: (0, i))
    pair = pl.BlockSpec((2, width, tile), lambda i: (0, 0, i))
    out = pl.pallas_call(
        functools.partial(score_kernel, groups),
        grid=(edges // tile,),
        out_shape=(
            jax.ShapeDtypeStruct((2, width, edges), BF16),
            jax.ShapeDtypeStruct((2, width, edges), BF16),
            *[jax.ShapeDtypeStruct((width, each), BF16)] * groups,
        ),
        in_specs=[whole()] * groups + [column, column, column, lane],
        out_specs=(pair, pair, *[pl.BlockSpec((width, each), lambda i: (0, 0))] * groups),
        scratch_shapes=[
            pltpu.VMEM((width, groups * each), BF16),
            pltpu.VMEM((groups * each, width), BF16),
            pltpu.VMEM((width, groups * each), F32),
        ],
        compiler_params=params(0),
        name="score",
    )(*negs, source, target, operator, g_pos)
    return out[0], out[1], out[2:]


def scatter_kernel(gs_ref, gd_ref, spos, dpos, out_ref):
    tile = out_ref.shape[1]
    width = gs_ref.shape[1]
    edges = gs_ref.shape[2]
    index = lax.broadcasted_iota(jnp.int32, (tile, edges), 0) + pl.program_id(0) * tile
    both = None
    for grads, pos in ((gs_ref, spos), (gd_ref, dpos)):
        hot = jnp.where(index == pos[...], 1.0, 0.0).astype(BF16)
        part = lax.dot_general(
            grads[...].reshape(2 * width, edges), hot, NT, preferred_element_type=F32
        )
        both = part if both is None else both + part
    out_ref[...] = both[:width] + both[width:]


def scatter(grads_src, grads_dst, spos, dpos, rows, tile=256):
    width = grads_src.shape[1]
    return pl.pallas_call(
        scatter_kernel,
        grid=(rows // tile,),
        out_shape=jax.ShapeDtypeStruct((width, rows), F32),
        in_specs=[whole(), whole(), whole(), whole()],
        out_specs=pl.BlockSpec((width, tile), lambda i: (0, i)),
        compiler_params=params(8 * grads_src.size),
        name="scatter",
    )(grads_src, grads_dst, spos, dpos)


def encode(x, out_ref):
    width = x.shape[0]
    top = jnp.max(jnp.abs(x), axis=0, keepdims=True)
    power = jnp.ceil(jnp.log2(jnp.maximum(top, 1e-30)))
    code = jnp.clip(jnp.round(x * jnp.exp2(15.0 - power)), -32767.0, 32767.0)
    out_ref[:width, :] = code.astype(jnp.int32).astype(jnp.int16)
    tail = jnp.broadcast_to(power, (TAIL, x.shape[1]))
    out_ref[width:, :] = tail.astype(jnp.int32).astype(jnp.int16)


def decode(code, width):
    power = code[width : width + 1, :].astype(jnp.int32).astype(F32)
    return code[:width, :].astype(jnp.int32).astype(F32) * jnp.exp2(power - 15.0)


def pack_kernel(rank_ref, live_ref, slots_ref, npos, *refs):
    grads, out_ref, total = refs[:-2], refs[-2], refs[-1]
    group = out_ref.shape[0]
    first = pl.program_id(0) * group
    width = slots_ref.shape[0]

    @pl.when(pl.program_id(0) == 0)
    def _():
        summed = sum(g[...].astype(F32) for g in grads)
        total[:width], total[width:] = split(summed)

    for k in range(group):
        alive = live_ref[first + k] > 0

        @pl.when(alive)
        def _():
            start = pl.multiple_of(rank_ref[first + k] * BLK, BLK)
            index = lax.broadcasted_iota(jnp.int32, (BLK, npos.shape[1]), 0) + start
            hot = jnp.where(index == npos[...], 1.0, 0.0).astype(BF16)
            both = lax.dot_general(total[...], hot, NT, preferred_element_type=F32)
            part = both[:width] + both[width:]
            encode(slots_ref[:, pl.ds(start, BLK)] + part, out_ref.at[k])

        @pl.when(jnp.logical_not(alive))
        def _():
            out_ref[k] = jnp.zeros(out_ref.shape[1:], jnp.int16)


def pack(rank, live, slots, grad_negs, npos, group=8):
    devices = rank.shape[0]
    width, rows = slots.shape
    return pl.pallas_call(
        pack_kernel,
        grid=(devices // group,),
        out_shape=jax.ShapeDtypeStruct((devices, width + TAIL, BLK), jnp.int16),
        in_specs=[smem(), smem(), whole(), whole()] + [whole()] * len(grad_negs),
        out_specs=pl.BlockSpec((group, width + TAIL, BLK), lambda i: (i, 0, 0)),
        scratch_shapes=[pltpu.VMEM((2 * width, npos.shape[1]), BF16)],
        compiler_params=params(6 * width * rows),
        name="pack",
    )(rank, live, slots, npos, *grad_negs)


def update_kernel(asked_ref, back_ref, table_ref, state_ref, table_out, state_out, grad):
    group = back_ref.shape[0]
    width = grad.shape[0]
    step = pl.program_id(0)

    @pl.when(step == 0)
    def _():
        grad[...] = jnp.zeros_like(grad)

    for k in range(group):
        lanes = pl.ds(pl.multiple_of(asked_ref[step * group + k] * BLK, BLK), BLK)
        grad[:, lanes] += decode(back_ref[k], width)

    @pl.when(step == pl.num_programs(0) - 1)
    def _():
        def block(b, _):
            lanes = pl.ds(pl.multiple_of(b * BLK, BLK), BLK)
            g = grad[:, lanes]
            new_state = state_ref[:, lanes] + jnp.sum(g * g, axis=0, keepdims=True) / width
            state_out[:, lanes] = new_state
            table_out[:, lanes] = table_ref[:, lanes] - 0.1 * g / (jnp.sqrt(new_state) + 1e-10)
            return 0

        lax.fori_loop(0, grad.shape[1] // BLK, block, 0)


def update(asked, returned, table, state, group=8):
    devices, coded, _ = returned.shape
    width, rows = table.shape
    return pl.pallas_call(
        update_kernel,
        grid=(devices // group,),
        out_shape=(
            jax.ShapeDtypeStruct((width, rows), F32),
            jax.ShapeDtypeStruct((1, rows), F32),
        ),
        in_specs=[
            smem(),
            pl.BlockSpec((group, coded, BLK), lambda i: (i, 0, 0)),
            pl.BlockSpec((width, rows), lambda i: (0, 0)),
            pl.BlockSpec((1, rows), lambda i: (0, 0)),
        ],
        out_specs=(
            pl.BlockSpec((width, rows), lambda i: (0, 0)),
            pl.BlockSpec((1, rows), lambda i: (0, 0)),
        ),
        scratch_shapes=[pltpu.VMEM((width, rows), F32)],
        compiler_params=params(12 * width * rows),
        name="update",
    )(asked, returned, table, state)


def per_device(table, state, relations, rel_ids, block_list, src_pos, dst_pos, neg_pos):
    devices = lax.axis_size(AXES)
    named = devices // 2
    rows_dev, width = table.shape
    blocks = rows_dev // BLK
    wanted = lax.all_to_all(
        block_list.reshape(devices, 1), AXES, split_axis=0, concat_axis=0, tiled=True
    )
    asked = wanted.reshape(devices)
    outgoing = table.reshape(blocks, BLK, width).astype(BF16)[asked]
    fetched = lax.all_to_all(
        outgoing.transpose(0, 2, 1), AXES, split_axis=0, concat_axis=0, tiled=True
    )
    operator = relations[rel_ids].T

    ids = jnp.arange(devices, dtype=jnp.int32)
    alive = jnp.max((src_pos // BLK)[:, None] == ids[None, :], axis=0).astype(jnp.int32)
    rank = jnp.sum(jnp.where(ids[None, :] < ids[:, None], alive[None, :], 0), axis=1)
    slot = jnp.arange(named, dtype=jnp.int32)
    live = jnp.sum(
        jnp.where((rank[None, :] == slot[:, None]) & (alive[None, :] > 0), ids[None, :], 0), axis=1
    )

    def compact(pos):
        place = jnp.sum(jnp.where((pos // BLK)[:, None] == ids[None, :], rank[None, :], 0), axis=1)
        return (place * BLK + pos % BLK).reshape(1, -1)

    spos, dpos, npos = compact(src_pos), compact(dst_pos), compact(neg_pos)

    fetched, operator, live, rank, spos, dpos, npos = lax.optimization_barrier(
        (fetched, operator, live, rank, spos, dpos, npos)
    )
    own_negs = gather_negs(live, fetched, npos)
    peers = lax.axis_size("dst")
    negs = [own_negs]
    for shift in range(1, peers):
        pairs = [(i, i ^ shift) for i in range(peers)]
        negs.append(lax.ppermute(own_negs, "dst", pairs))
    source, target, g_pos = gather_edges(live, fetched, spos, dpos, operator)
    grads_src, grads_dst, part_negs = score(negs, source, target, operator, g_pos)
    own_grad = [part_negs[0]]
    for shift in range(1, peers):
        pairs = [(i, i ^ shift) for i in range(peers)]
        own_grad.append(lax.ppermute(part_negs[shift], "dst", pairs))
    slots = scatter(grads_src, grads_dst, spos, dpos, named * BLK)
    packed = pack(rank, alive, slots, own_grad, npos)
    returned = lax.all_to_all(packed, AXES, split_axis=0, concat_axis=0, tiled=True)
    new_table, new_state = update(asked, returned, table.T, state.reshape(1, rows_dev))
    return (new_table.T, new_state.reshape(rows_dev))


def solution(mesh):
    in_specs = (
        P(AXES, None),
        P(AXES),
        P(),
        P(AXES),
        P(AXES, None),
        P(AXES),
        P(AXES),
        P(AXES),
    )
    out_specs = (P(AXES, None), P(AXES))
    return jax.shard_map(
        per_device, mesh=mesh, in_specs=in_specs, out_specs=out_specs, check_vma=False
    )
```

```python
import functools

import jax
import jax.numpy as jnp
from jax import lax
from jax.experimental import pallas as pl
from jax.experimental.pallas import tpu as pltpu
from jax.sharding import PartitionSpec as P

BLK = 128
TAIL = 8
GROUPS = 4
TILE = 256
AXES = ("src", "dst")
F32 = jnp.float32
BF16 = jnp.bfloat16
NT = (((1,), (1,)), ((), ()))


def params(held):
    return pltpu.CompilerParams(vmem_limit_bytes=14 * 1024 * 1024 + held)


MIB = 1024 * 1024


def cost(flops):
    return pl.CostEstimate(flops=flops, bytes_accessed=flops // 512, transcendentals=0)


def whole():
    return pl.BlockSpec(memory_space=pltpu.VMEM)


def smem():
    return pl.BlockSpec(memory_space=pltpu.SMEM)


def anywhere():
    return pl.BlockSpec(memory_space=pl.ANY)


def load_live(live_ref, fetched, rows, sem):
    count = live_ref.shape[0]

    def copy(k):
        lanes = pl.ds(pl.multiple_of(k * BLK, BLK), BLK)
        return pltpu.make_async_copy(fetched.at[live_ref[k]], rows.at[:, lanes], sem)

    def start(k, _):
        copy(k).start()
        return 0

    def wait(k, _):
        copy(k).wait()
        return 0

    lax.fori_loop(0, count, start, 0)
    lax.fori_loop(0, count, wait, 0)


def pick(rows, positions):
    total = rows.shape[1]
    step = min(total, 2048)
    out = None
    for first in range(0, total, step):
        index = lax.broadcasted_iota(jnp.int32, (step, positions.shape[1]), 0) + first
        hot = jnp.where(index == positions, 1.0, 0.0).astype(BF16)
        part = jnp.dot(rows[:, first : first + step], hot, preferred_element_type=F32)
        out = part if out is None else out + part
    return out


def neg_kernel(live_ref, fetched, pos_ref, out_ref, rows, sem):
    load_live(live_ref, fetched, rows, sem)
    out_ref[...] = pick(rows, pos_ref[...]).astype(BF16)


def gather_negs(live, fetched, pos):
    width = fetched.shape[1]
    total = live.shape[0] * BLK
    return pl.pallas_call(
        neg_kernel,
        out_shape=(
            jax.ShapeDtypeStruct((width, pos.shape[1]), BF16),
            jax.ShapeDtypeStruct((width, total), BF16),
        ),
        in_specs=[smem(), anywhere(), whole()],
        out_specs=(whole(), whole()),
        scratch_shapes=[pltpu.SemaphoreType.DMA],
        compiler_params=params(4 * width * total),
        name="gather_negs",
    )(live, fetched, pos)


def edge_kernel(rows, spos, dpos, op_ref, src_ref, dst_ref, gpos_ref):
    source = pick(rows, spos[...])
    target = pick(rows, dpos[...])
    u = source * op_ref[...]
    positive = jnp.sum(u * target, axis=0, keepdims=True)
    gpos_ref[...] = -jax.nn.sigmoid(-positive)
    src_ref[...] = source.astype(BF16)
    dst_ref[...] = target.astype(BF16)


def gather_edges(rows, spos, dpos, operator, tile=512):
    width, total = rows.shape
    edges = spos.shape[1]
    lane = pl.BlockSpec((1, tile), lambda i: (0, i))
    column = pl.BlockSpec((width, tile), lambda i: (0, i))
    return pl.pallas_call(
        edge_kernel,
        grid=(edges // tile,),
        out_shape=(
            jax.ShapeDtypeStruct((width, edges), BF16),
            jax.ShapeDtypeStruct((width, edges), BF16),
            jax.ShapeDtypeStruct((1, edges), F32),
        ),
        in_specs=[whole(), lane, lane, column],
        out_specs=(column, column, lane),
        compiler_params=params(2 * width * total + 8 * MIB),
        cost_estimate=cost(4 * width * total * edges),
        name="gather_edges",
    )(rows, spos, dpos, operator)


def split(x):
    high = x.astype(BF16)
    return high, (x - high.astype(F32)).astype(BF16)


def score_kernel(groups, *refs):
    negs = refs[:groups]
    src_ref, dst_ref, op_ref, gpos_ref, gs_ref, gd_ref = refs[groups : groups + 6]
    outs = refs[groups + 6 : 2 * groups + 6]
    each = negs[0].shape[1]
    count = groups * each
    wide = jnp.concatenate([n[...] for n in negs], axis=1)
    tall = jnp.concatenate([n[...].T for n in negs], axis=0)
    operator = op_ref[...]
    u = src_ref[...].astype(F32) * operator
    u_half = u.astype(BF16)
    scores = jnp.dot(tall, u_half, preferred_element_type=F32)
    g_neg = (jax.nn.sigmoid(scores) / count).astype(BF16)
    sums = lax.dot_general(u_half, g_neg, NT, preferred_element_type=F32)
    for g in range(groups):
        outs[g][...] = sums[:, g * each : (g + 1) * each].astype(BF16)
    g_pos = gpos_ref[...]
    grad_u = g_pos * dst_ref[...].astype(F32) + jnp.dot(wide, g_neg, preferred_element_type=F32)
    gs_ref[0], gs_ref[1] = split(grad_u * operator)
    gd_ref[0], gd_ref[1] = split(g_pos * u)


def score(negs, source, target, operator, g_pos):
    groups = len(negs)
    width, each = negs[0].shape
    edges = source.shape[1]
    out = pl.pallas_call(
        functools.partial(score_kernel, groups),
        out_shape=(
            jax.ShapeDtypeStruct((2, width, edges), BF16),
            jax.ShapeDtypeStruct((2, width, edges), BF16),
            *[jax.ShapeDtypeStruct((width, each), BF16)] * groups,
        ),
        in_specs=[whole()] * (groups + 4),
        out_specs=(whole(),) * (groups + 2),
        compiler_params=params(20 * MIB),
        cost_estimate=cost(6 * width * edges * groups * each),
        name="score",
    )(*negs, source, target, operator, g_pos)
    return out[0], out[1], out[2:]


def scatter_kernel(base_ref, gs_ref, gd_ref, spos, dpos, out_ref):
    width, edges = gs_ref.shape[1:]
    first = base_ref[0] * BLK

    def tile(t, _):
        index = lax.broadcasted_iota(jnp.int32, (TILE, edges), 0) + (first + t * TILE)
        both = None
        for grads, pos in ((gs_ref, spos), (gd_ref, dpos)):
            hot = jnp.where(index == pos[...], 1.0, 0.0).astype(BF16)
            part = lax.dot_general(
                grads[...].reshape(2 * width, edges), hot, NT, preferred_element_type=F32
            )
            both = part if both is None else both + part
        out_ref[:, pl.ds(pl.multiple_of(t * TILE, TILE), TILE)] = both[:width] + both[width:]
        return 0

    blocks = base_ref[1] - base_ref[0]
    lax.fori_loop(0, (blocks * BLK + TILE - 1) // TILE, tile, 0)


def scatter(bases, grads_src, grads_dst, spos, dpos, blocks):
    width, edges = grads_src.shape[1:]
    rows = -(-blocks * BLK // TILE) * TILE
    return pl.pallas_call(
        scatter_kernel,
        out_shape=jax.ShapeDtypeStruct((width, rows), F32),
        in_specs=[smem(), whole(), whole(), whole(), whole()],
        out_specs=whole(),
        compiler_params=params(4 * width * rows),
        cost_estimate=cost(4 * width * rows * edges),
        name="scatter",
    )(bases, grads_src, grads_dst, spos, dpos)


def encode(x, out_ref):
    width = x.shape[0]
    top = jnp.max(jnp.abs(x), axis=0, keepdims=True)
    power = jnp.ceil(jnp.log2(jnp.maximum(top, 1e-30)))
    code = jnp.clip(jnp.round(x * jnp.exp2(15.0 - power)), -32767.0, 32767.0)
    out_ref[:width, :] = code.astype(jnp.int32).astype(jnp.int16)
    tail = jnp.broadcast_to(power, (TAIL, x.shape[1]))
    out_ref[width:, :] = tail.astype(jnp.int32).astype(jnp.int16)


def decode(code, width):
    power = code[width:, :].astype(jnp.int32).astype(F32)[:1]
    return code[:width, :].astype(jnp.int32).astype(F32) * jnp.exp2(power - 15.0)


def pack_kernel(first, rank_ref, live_ref, slots_ref, npos, *refs):
    count = len(refs) - 1
    peers = 0
    while refs[peers].shape[0] == slots_ref.shape[0]:
        peers += 1
    grads, outs, total = refs[:peers], refs[peers:count], refs[count]
    width = slots_ref.shape[0]
    total[:width], total[width:] = split(sum(g[...].astype(F32) for g in grads))
    base = rank_ref[first]
    for k, out_ref in enumerate(outs):
        alive = live_ref[first + k] > 0

        @pl.when(alive)
        def _():
            rank = rank_ref[first + k]
            index = lax.broadcasted_iota(jnp.int32, (BLK, npos.shape[1]), 0) + rank * BLK
            hot = jnp.where(index == npos[...], 1.0, 0.0).astype(BF16)
            both = lax.dot_general(total[...], hot, NT, preferred_element_type=F32)
            lanes = pl.ds(pl.multiple_of((rank - base) * BLK, BLK), BLK)
            encode(slots_ref[:, lanes] + (both[:width] + both[width:]), out_ref)

        @pl.when(jnp.logical_not(alive))
        def _():
            out_ref[...] = jnp.zeros(out_ref.shape, jnp.int16)


def pack(first, group, rank, live, slots, grad_negs, npos):
    width = slots.shape[0]
    return pl.pallas_call(
        functools.partial(pack_kernel, first),
        out_shape=(jax.ShapeDtypeStruct((width + TAIL, BLK), jnp.int16),) * group,
        in_specs=[smem(), smem(), whole(), whole()] + [whole()] * len(grad_negs),
        out_specs=(whole(),) * group,
        scratch_shapes=[pltpu.VMEM((2 * width, npos.shape[1]), BF16)],
        compiler_params=params(0),
        cost_estimate=cost(4 * width * BLK * BLK * group),
        name="pack",
    )(rank, live, slots, npos, *grad_negs)


def add_kernel(first, fresh, asked_ref, *refs):
    grad = refs[-1]
    backs = refs[: -1 if fresh else -2]
    width = grad.shape[0]
    if fresh:
        grad[...] = jnp.zeros_like(grad)
    for k, back in enumerate(backs):
        lanes = pl.ds(pl.multiple_of(asked_ref[first + k] * BLK, BLK), BLK)
        grad[:, lanes] += decode(back, width)


def add(first, asked, backs, grad, width, rows):
    fresh = grad is None
    extra = [] if fresh else [grad]
    return pl.pallas_call(
        functools.partial(add_kernel, first, fresh),
        out_shape=jax.ShapeDtypeStruct((width, rows), F32),
        in_specs=[smem()] + [whole()] * (len(backs) + len(extra)),
        out_specs=whole(),
        input_output_aliases={} if fresh else {len(backs) + 1: 0},
        compiler_params=params(0),
        cost_estimate=cost(width * BLK * len(backs) * 64),
        name="add",
    )(asked, *backs, *extra)


def update_kernel(first, asked_ref, *refs):
    backs = refs[:-7]
    grad, table_ref, state_ref, table_out, state_out, fresh, sems = refs[-7:]
    width, rows = grad.shape
    for k, back in enumerate(backs):
        lanes = pl.ds(pl.multiple_of(asked_ref[first + k] * BLK, BLK), BLK)
        grad[:, lanes] += decode(back, width)
    span = fresh.shape[1] // sems.shape[0]

    def copy(b):
        lanes = pl.ds(pl.multiple_of(b * span, span), span)
        return pltpu.make_async_copy(fresh.at[:, lanes], table_out.at[:, lanes], sems.at[b])

    for b in range(sems.shape[0]):
        for c in range(b * span, (b + 1) * span, BLK):
            lanes = slice(c, c + BLK)
            g = grad[:, lanes]
            new_state = state_ref[:, lanes] + jnp.sum(g * g, axis=0, keepdims=True) / width
            state_out[:, lanes] = new_state
            fresh[:, lanes] = table_ref[:, lanes] - 0.1 * g / (jnp.sqrt(new_state) + 1e-10)
        copy(b).start()
    for b in range(sems.shape[0]):
        copy(b).wait()


def update(first, asked, backs, grad, table, state, parts=4):
    width, rows = table.shape
    return pl.pallas_call(
        functools.partial(update_kernel, first),
        out_shape=(
            jax.ShapeDtypeStruct((width, rows), F32),
            jax.ShapeDtypeStruct((1, rows), F32),
        ),
        in_specs=[smem()] + [whole()] * (len(backs) + 3),
        out_specs=(anywhere(), whole()),
        scratch_shapes=[pltpu.VMEM((width, rows), F32), pltpu.SemaphoreType.DMA((parts,))],
        compiler_params=params(4 * width * rows),
        cost_estimate=cost(width * rows * 64),
        name="update",
    )(asked, *backs, grad, table, state)


def per_device(table, state, relations, rel_ids, block_list, src_pos, dst_pos, neg_pos):
    devices = lax.axis_size(AXES)
    named = devices // 2
    rows_dev, width = table.shape
    blocks = rows_dev // BLK
    wanted = lax.all_to_all(
        block_list.reshape(devices, 1), AXES, split_axis=0, concat_axis=0, tiled=True
    )
    asked = wanted.reshape(devices)
    outgoing = table.reshape(blocks, BLK, width).astype(BF16)[asked]
    fetched = lax.all_to_all(
        outgoing.transpose(0, 2, 1), AXES, split_axis=0, concat_axis=0, tiled=True
    )
    operator = relations[rel_ids].T

    half = devices // 2
    order = [k for pair in zip(range(devices - 1, half - 1, -1), range(half - 1, -1, -1)) for k in pair]
    partners = lax.axis_index(AXES) ^ jnp.array(order, jnp.int32)
    ids = jnp.arange(devices, dtype=jnp.int32)
    seat = partners[:, None] == ids[None, :]
    named_by = jnp.max((src_pos // BLK)[:, None] == ids[None, :], axis=0).astype(jnp.int32)
    alive = jnp.sum(jnp.where(seat, named_by[None, :], 0), axis=1)
    rank = jnp.sum(jnp.where(ids[None, :] < ids[:, None], alive[None, :], 0), axis=1)
    place = jnp.sum(jnp.where(seat, rank[:, None], 0), axis=0)
    slot = jnp.arange(named, dtype=jnp.int32)
    live = jnp.sum(
        jnp.where((rank[None, :] == slot[:, None]) & (alive[None, :] > 0), partners[None, :], 0), axis=1
    )
    asked = jnp.sum(jnp.where(seat, asked[None, :], 0), axis=1)
    group = devices // GROUPS
    starts = jnp.concatenate([rank[::group], jnp.full((1,), named, jnp.int32)])

    def compact(pos):
        where = jnp.sum(jnp.where((pos // BLK)[:, None] == ids[None, :], place[None, :], 0), axis=1)
        return (where * BLK + pos % BLK).reshape(1, -1)

    spos, dpos, npos = compact(src_pos), compact(dst_pos), compact(neg_pos)
    bases = [starts[g : g + 2] for g in range(GROUPS)]
    fetched, operator, live, rank, alive, asked, spos, dpos, npos, bases = lax.optimization_barrier(
        (fetched, operator, live, rank, alive, asked, spos, dpos, npos, bases)
    )

    def swap(x, shift, axis):
        count = lax.axis_size(axis)
        return lax.ppermute(x, axis, [(i, i ^ shift) for i in range(count)])

    peers = lax.axis_size("dst")
    own_negs, rows = gather_negs(live, fetched, npos)
    negs = [own_negs] + [swap(own_negs, shift, "dst") for shift in range(1, peers)]
    source, target, g_pos = gather_edges(rows, spos, dpos, operator)
    grads_src, grads_dst, part_negs = score(negs, source, target, operator, g_pos)
    own_grad = [part_negs[0]] + [swap(part_negs[shift], shift, "dst") for shift in range(1, peers)]
    grad = None
    for g in range(GROUPS):
        first = g * group
        slots = scatter(bases[g], grads_src, grads_dst, spos, dpos, min(group, named))
        packed = pack(first, group, rank, alive, slots, own_grad, npos)
        backs = [
            swap(x, shift, AXES) if shift else x
            for x, shift in zip(packed, order[first : first + group])
        ]
        if g < GROUPS - 1:
            grad = add(first, asked, backs, grad, width, rows_dev)
        else:
            new_table, new_state = update(
                first, asked, backs, grad, table.T, state.reshape(1, rows_dev)
            )
    return (new_table.T, new_state.reshape(rows_dev))


def solution(mesh):
    in_specs = (
        P(AXES, None),
        P(AXES),
        P(),
        P(AXES),
        P(AXES, None),
        P(AXES),
        P(AXES),
        P(AXES),
    )
    out_specs = (P(AXES, None), P(AXES))
    return jax.shard_map(
        per_device, mesh=mesh, in_specs=in_specs, out_specs=out_specs, check_vma=False
    )
```

```python
import functools

import jax
import jax.numpy as jnp
from jax import lax
from jax.experimental import pallas as pl
from jax.experimental.pallas import tpu as pltpu
from jax.sharding import PartitionSpec as P

BLK = 128
TAIL = 8
CUTS = (1, 1, 2, 2, 2)
TILE = 256
AXES = ("src", "dst")
F32 = jnp.float32
BF16 = jnp.bfloat16
NT = (((1,), (1,)), ((), ()))


def params(held):
    return pltpu.CompilerParams(vmem_limit_bytes=14 * 1024 * 1024 + held)


MIB = 1024 * 1024


def cost(flops):
    return pl.CostEstimate(flops=flops, bytes_accessed=flops // 512, transcendentals=0)


def whole():
    return pl.BlockSpec(memory_space=pltpu.VMEM)


def smem():
    return pl.BlockSpec(memory_space=pltpu.SMEM)


def anywhere():
    return pl.BlockSpec(memory_space=pl.ANY)


def load_live(live_ref, fetched, rows, sem):
    count = live_ref.shape[0]

    def copy(k):
        lanes = pl.ds(pl.multiple_of(k * BLK, BLK), BLK)
        return pltpu.make_async_copy(fetched.at[live_ref[k]], rows.at[:, lanes], sem)

    def start(k, _):
        copy(k).start()
        return 0

    def wait(k, _):
        copy(k).wait()
        return 0

    lax.fori_loop(0, count, start, 0)
    lax.fori_loop(0, count, wait, 0)


def pick(rows, positions):
    total = rows.shape[1]
    step = min(total, 2048)
    out = None
    for first in range(0, total, step):
        index = lax.broadcasted_iota(jnp.int32, (step, positions.shape[1]), 0) + first
        hot = jnp.where(index == positions, 1.0, 0.0).astype(BF16)
        part = jnp.dot(rows[:, first : first + step], hot, preferred_element_type=F32)
        out = part if out is None else out + part
    return out


def neg_kernel(live_ref, fetched, pos_ref, out_ref, rows, sem):
    load_live(live_ref, fetched, rows, sem)
    out_ref[...] = pick(rows, pos_ref[...]).astype(BF16)


def gather_negs(live, fetched, pos):
    width = fetched.shape[1]
    total = live.shape[0] * BLK
    return pl.pallas_call(
        neg_kernel,
        out_shape=(
            jax.ShapeDtypeStruct((width, pos.shape[1]), BF16),
            jax.ShapeDtypeStruct((width, total), BF16),
        ),
        in_specs=[smem(), anywhere(), whole()],
        out_specs=(whole(), whole()),
        scratch_shapes=[pltpu.SemaphoreType.DMA],
        compiler_params=params(4 * width * total),
        name="gather_negs",
    )(live, fetched, pos)


def edge_kernel(rows, spos, dpos, op_ref, src_ref, dst_ref, gpos_ref):
    source = pick(rows, spos[...])
    target = pick(rows, dpos[...])
    u = source * op_ref[...]
    positive = jnp.sum(u * target, axis=0, keepdims=True)
    gpos_ref[...] = -jax.nn.sigmoid(-positive)
    src_ref[...] = source.astype(BF16)
    dst_ref[...] = target.astype(BF16)


def gather_edges(rows, spos, dpos, operator, tile=512):
    width, total = rows.shape
    edges = spos.shape[1]
    lane = pl.BlockSpec((1, tile), lambda i: (0, i))
    column = pl.BlockSpec((width, tile), lambda i: (0, i))
    return pl.pallas_call(
        edge_kernel,
        grid=(edges // tile,),
        out_shape=(
            jax.ShapeDtypeStruct((width, edges), BF16),
            jax.ShapeDtypeStruct((width, edges), BF16),
            jax.ShapeDtypeStruct((1, edges), F32),
        ),
        in_specs=[whole(), lane, lane, column],
        out_specs=(column, column, lane),
        compiler_params=params(2 * width * total + 8 * MIB),
        cost_estimate=cost(4 * width * total * edges),
        name="gather_edges",
    )(rows, spos, dpos, operator)


def split(x):
    high = x.astype(BF16)
    return high, (x - high.astype(F32)).astype(BF16)


def score_kernel(groups, *refs):
    negs = refs[:groups]
    src_ref, dst_ref, op_ref, gpos_ref, gs_ref, gd_ref = refs[groups : groups + 6]
    outs = refs[groups + 6 : 2 * groups + 6]
    each = negs[0].shape[1]
    count = groups * each
    wide = jnp.concatenate([n[...] for n in negs], axis=1)
    tall = jnp.concatenate([n[...].T for n in negs], axis=0)
    operator = op_ref[...]
    u = src_ref[...].astype(F32) * operator
    u_half = u.astype(BF16)
    scores = jnp.dot(tall, u_half, preferred_element_type=F32)
    g_neg = (jax.nn.sigmoid(scores) / count).astype(BF16)
    sums = lax.dot_general(u_half, g_neg, NT, preferred_element_type=F32)
    for g in range(groups):
        outs[g][...] = sums[:, g * each : (g + 1) * each].astype(BF16)
    g_pos = gpos_ref[...]
    grad_u = g_pos * dst_ref[...].astype(F32) + jnp.dot(wide, g_neg, preferred_element_type=F32)
    gs_ref[0], gs_ref[1] = split(grad_u * operator)
    gd_ref[0], gd_ref[1] = split(g_pos * u)


def score(negs, source, target, operator, g_pos):
    groups = len(negs)
    width, each = negs[0].shape
    edges = source.shape[1]
    out = pl.pallas_call(
        functools.partial(score_kernel, groups),
        out_shape=(
            jax.ShapeDtypeStruct((2, width, edges), BF16),
            jax.ShapeDtypeStruct((2, width, edges), BF16),
            *[jax.ShapeDtypeStruct((width, each), BF16)] * groups,
        ),
        in_specs=[whole()] * (groups + 4),
        out_specs=(whole(),) * (groups + 2),
        compiler_params=params(20 * MIB),
        cost_estimate=cost(6 * width * edges * groups * each),
        name="score",
    )(*negs, source, target, operator, g_pos)
    return out[0], out[1], out[2:]


def scatter_kernel(base_ref, gs_ref, gd_ref, spos, dpos, out_ref):
    width, edges = gs_ref.shape[1:]
    first = base_ref[0] * BLK

    def tile(t, _):
        index = lax.broadcasted_iota(jnp.int32, (TILE, edges), 0) + (first + t * TILE)
        both = None
        for grads, pos in ((gs_ref, spos), (gd_ref, dpos)):
            hot = jnp.where(index == pos[...], 1.0, 0.0).astype(BF16)
            part = lax.dot_general(
                grads[...].reshape(2 * width, edges), hot, NT, preferred_element_type=F32
            )
            both = part if both is None else both + part
        out_ref[:, pl.ds(pl.multiple_of(t * TILE, TILE), TILE)] = both[:width] + both[width:]
        return 0

    blocks = base_ref[1] - base_ref[0]
    lax.fori_loop(0, (blocks * BLK + TILE - 1) // TILE, tile, 0)


def scatter(bases, grads_src, grads_dst, spos, dpos, blocks):
    width, edges = grads_src.shape[1:]
    rows = -(-blocks * BLK // TILE) * TILE
    return pl.pallas_call(
        scatter_kernel,
        out_shape=jax.ShapeDtypeStruct((width, rows), F32),
        in_specs=[smem(), whole(), whole(), whole(), whole()],
        out_specs=whole(),
        compiler_params=params(4 * width * rows),
        cost_estimate=cost(4 * width * rows * edges),
        name="scatter",
    )(bases, grads_src, grads_dst, spos, dpos)


def encode(x, out_ref):
    width = x.shape[0]
    top = jnp.max(jnp.abs(x), axis=0, keepdims=True)
    power = jnp.ceil(jnp.log2(jnp.maximum(top, 1e-30)))
    code = jnp.clip(jnp.round(x * jnp.exp2(15.0 - power)), -32767.0, 32767.0)
    out_ref[:width, :] = code.astype(jnp.int32).astype(jnp.int16)
    tail = jnp.broadcast_to(power, (TAIL, x.shape[1]))
    out_ref[width:, :] = tail.astype(jnp.int32).astype(jnp.int16)


def decode(code, width):
    power = code[width:, :].astype(jnp.int32).astype(F32)[:1]
    return code[:width, :].astype(jnp.int32).astype(F32) * jnp.exp2(power - 15.0)


def pack_kernel(first, rank_ref, live_ref, slots_ref, npos, *refs):
    count = len(refs) - 1
    peers = 0
    while refs[peers].shape[0] == slots_ref.shape[0]:
        peers += 1
    grads, outs, total = refs[:peers], refs[peers:count], refs[count]
    width = slots_ref.shape[0]
    total[:width], total[width:] = split(sum(g[...].astype(F32) for g in grads))
    base = rank_ref[first]
    for k, out_ref in enumerate(outs):
        alive = live_ref[first + k] > 0

        @pl.when(alive)
        def _():
            rank = rank_ref[first + k]
            index = lax.broadcasted_iota(jnp.int32, (BLK, npos.shape[1]), 0) + rank * BLK
            hot = jnp.where(index == npos[...], 1.0, 0.0).astype(BF16)
            both = lax.dot_general(total[...], hot, NT, preferred_element_type=F32)
            lanes = pl.ds(pl.multiple_of((rank - base) * BLK, BLK), BLK)
            encode(slots_ref[:, lanes] + (both[:width] + both[width:]), out_ref)

        @pl.when(jnp.logical_not(alive))
        def _():
            out_ref[...] = jnp.zeros(out_ref.shape, jnp.int16)


def pack(first, group, rank, live, slots, grad_negs, npos):
    width = slots.shape[0]
    return pl.pallas_call(
        functools.partial(pack_kernel, first),
        out_shape=(jax.ShapeDtypeStruct((width + TAIL, BLK), jnp.int16),) * group,
        in_specs=[smem(), smem(), whole(), whole()] + [whole()] * len(grad_negs),
        out_specs=(whole(),) * group,
        scratch_shapes=[pltpu.VMEM((2 * width, npos.shape[1]), BF16)],
        compiler_params=params(0),
        cost_estimate=cost(4 * width * BLK * BLK * group),
        name="pack",
    )(rank, live, slots, npos, *grad_negs)


def add_kernel(first, fresh, asked_ref, *refs):
    grad = refs[-1]
    backs = refs[: -1 if fresh else -2]
    width = grad.shape[0]
    if fresh:
        grad[...] = jnp.zeros_like(grad)
    for k, back in enumerate(backs):
        lanes = pl.ds(pl.multiple_of(asked_ref[first + k] * BLK, BLK), BLK)
        grad[:, lanes] += decode(back, width)


def add(first, asked, backs, grad, width, rows):
    fresh = grad is None
    extra = [] if fresh else [grad]
    return pl.pallas_call(
        functools.partial(add_kernel, first, fresh),
        out_shape=jax.ShapeDtypeStruct((width, rows), F32),
        in_specs=[smem()] + [whole()] * (len(backs) + len(extra)),
        out_specs=whole(),
        input_output_aliases={} if fresh else {len(backs) + 1: 0},
        compiler_params=params(0),
        cost_estimate=cost(width * BLK * len(backs) * 64),
        name="add",
    )(asked, *backs, *extra)


def update_kernel(first, asked_ref, *refs):
    backs = refs[:-7]
    grad, table_ref, state_ref, table_out, state_out, fresh, sems = refs[-7:]
    width, rows = grad.shape
    for k, back in enumerate(backs):
        lanes = pl.ds(pl.multiple_of(asked_ref[first + k] * BLK, BLK), BLK)
        grad[:, lanes] += decode(back, width)
    span = fresh.shape[1] // sems.shape[0]

    def copy(b):
        lanes = pl.ds(pl.multiple_of(b * span, span), span)
        return pltpu.make_async_copy(fresh.at[:, lanes], table_out.at[:, lanes], sems.at[b])

    for b in range(sems.shape[0]):
        for c in range(b * span, (b + 1) * span, BLK):
            lanes = slice(c, c + BLK)
            g = grad[:, lanes]
            new_state = state_ref[:, lanes] + jnp.sum(g * g, axis=0, keepdims=True) / width
            state_out[:, lanes] = new_state
            fresh[:, lanes] = table_ref[:, lanes] - 0.1 * g / (jnp.sqrt(new_state) + 1e-10)
        copy(b).start()
    for b in range(sems.shape[0]):
        copy(b).wait()


def update(first, asked, backs, grad, table, state, parts=4):
    width, rows = table.shape
    return pl.pallas_call(
        functools.partial(update_kernel, first),
        out_shape=(
            jax.ShapeDtypeStruct((width, rows), F32),
            jax.ShapeDtypeStruct((1, rows), F32),
        ),
        in_specs=[smem()] + [whole()] * (len(backs) + 3),
        out_specs=(anywhere(), whole()),
        scratch_shapes=[pltpu.VMEM((width, rows), F32), pltpu.SemaphoreType.DMA((parts,))],
        compiler_params=params(4 * width * rows),
        cost_estimate=cost(width * rows * 64),
        name="update",
    )(asked, *backs, grad, table, state)


def per_device(table, state, relations, rel_ids, block_list, src_pos, dst_pos, neg_pos):
    devices = lax.axis_size(AXES)
    named = devices // 2
    rows_dev, width = table.shape
    blocks = rows_dev // BLK
    wanted = lax.all_to_all(
        block_list.reshape(devices, 1), AXES, split_axis=0, concat_axis=0, tiled=True
    )
    asked = wanted.reshape(devices)
    outgoing = table.reshape(blocks, BLK, width).astype(BF16)[asked]
    fetched = lax.all_to_all(
        outgoing.transpose(0, 2, 1), AXES, split_axis=0, concat_axis=0, tiled=True
    )
    operator = relations[rel_ids].T

    half = devices // 2
    order = [k for pair in zip(range(devices - 1, half - 1, -1), range(half - 1, -1, -1)) for k in pair]
    partners = lax.axis_index(AXES) ^ jnp.array(order, jnp.int32)
    ids = jnp.arange(devices, dtype=jnp.int32)
    seat = partners[:, None] == ids[None, :]
    named_by = jnp.max((src_pos // BLK)[:, None] == ids[None, :], axis=0).astype(jnp.int32)
    alive = jnp.sum(jnp.where(seat, named_by[None, :], 0), axis=1)
    rank = jnp.sum(jnp.where(ids[None, :] < ids[:, None], alive[None, :], 0), axis=1)
    place = jnp.sum(jnp.where(seat, rank[:, None], 0), axis=0)
    slot = jnp.arange(named, dtype=jnp.int32)
    live = jnp.sum(
        jnp.where((rank[None, :] == slot[:, None]) & (alive[None, :] > 0), partners[None, :], 0), axis=1
    )
    asked = jnp.sum(jnp.where(seat, asked[None, :], 0), axis=1)
    sizes = [cut * devices // sum(CUTS) for cut in CUTS]
    firsts = [sum(sizes[:g]) for g in range(len(sizes))]
    starts = [rank[first] for first in firsts] + [jnp.int32(named)]

    def compact(pos):
        where = jnp.sum(jnp.where((pos // BLK)[:, None] == ids[None, :], place[None, :], 0), axis=1)
        return (where * BLK + pos % BLK).reshape(1, -1)

    spos, dpos, npos = compact(src_pos), compact(dst_pos), compact(neg_pos)
    bases = [jnp.stack(starts[g : g + 2]) for g in range(len(sizes))]
    fetched, operator, live, rank, alive, asked, spos, dpos, npos, bases = lax.optimization_barrier(
        (fetched, operator, live, rank, alive, asked, spos, dpos, npos, bases)
    )

    def swap(x, shift, axis):
        count = lax.axis_size(axis)
        return lax.ppermute(x, axis, [(i, i ^ shift) for i in range(count)])

    peers = lax.axis_size("dst")
    own_negs, rows = gather_negs(live, fetched, npos)
    negs = [own_negs] + [swap(own_negs, shift, "dst") for shift in range(1, peers)]
    source, target, g_pos = gather_edges(rows, spos, dpos, operator)
    grads_src, grads_dst, part_negs = score(negs, source, target, operator, g_pos)
    own_grad = [part_negs[0]] + [swap(part_negs[shift], shift, "dst") for shift in range(1, peers)]
    grad = None
    backs = []
    for g, (first, group) in enumerate(zip(firsts, sizes)):
        base = bases[g]
        if g:
            ahead = len(backs) // 2
            base, backs[:ahead] = lax.optimization_barrier((base, backs[:ahead]))
        if g > 1:
            base, grad = lax.optimization_barrier((base, grad))
        slots = scatter(base, grads_src, grads_dst, spos, dpos, min(group, named))
        packed = pack(first, group, rank, alive, slots, own_grad, npos)
        if g:
            grad = add(firsts[g - 1], asked, backs, grad, width, rows_dev)
        backs = [
            swap(x, shift, AXES) if shift else x
            for x, shift in zip(packed, order[first : first + group])
        ]
    new_table, new_state = update(
        firsts[-1], asked, backs, grad, table.T, state.reshape(1, rows_dev)
    )
    return (new_table.T, new_state.reshape(rows_dev))


def solution(mesh):
    in_specs = (
        P(AXES, None),
        P(AXES),
        P(),
        P(AXES),
        P(AXES, None),
        P(AXES),
        P(AXES),
        P(AXES),
    )
    out_specs = (P(AXES, None), P(AXES))
    return jax.shard_map(
        per_device, mesh=mesh, in_specs=in_specs, out_specs=out_specs, check_vma=False
    )
```

```python
import functools

import jax
import jax.numpy as jnp
from jax import lax
from jax.experimental import pallas as pl
from jax.experimental.pallas import tpu as pltpu
from jax.sharding import PartitionSpec as P

BLK = 128
TAIL = 8
CUTS = (1, 2, 2, 2, 1)
STEPS = (1, 3, 4)
TILE = 256
AXES = ("src", "dst")
F32 = jnp.float32
BF16 = jnp.bfloat16
NT = (((1,), (1,)), ((), ()))


def params(held):
    return pltpu.CompilerParams(vmem_limit_bytes=14 * 1024 * 1024 + held)


MIB = 1024 * 1024


def cost(flops):
    return pl.CostEstimate(flops=flops, bytes_accessed=flops // 512, transcendentals=0)


def whole():
    return pl.BlockSpec(memory_space=pltpu.VMEM)


def smem():
    return pl.BlockSpec(memory_space=pltpu.SMEM)


def anywhere():
    return pl.BlockSpec(memory_space=pl.ANY)


def load_live(live_ref, fetched, rows, sem):
    count = live_ref.shape[0]

    def copy(k):
        lanes = pl.ds(pl.multiple_of(k * BLK, BLK), BLK)
        return pltpu.make_async_copy(fetched.at[live_ref[k]], rows.at[:, lanes], sem)

    def start(k, _):
        copy(k).start()
        return 0

    def wait(k, _):
        copy(k).wait()
        return 0

    lax.fori_loop(0, count, start, 0)
    lax.fori_loop(0, count, wait, 0)


def pick(rows, positions):
    total = rows.shape[1]
    step = min(total, 2048)
    out = None
    for first in range(0, total, step):
        index = lax.broadcasted_iota(jnp.int32, (step, positions.shape[1]), 0) + first
        hot = jnp.where(index == positions, 1.0, 0.0).astype(BF16)
        part = jnp.dot(rows[:, first : first + step], hot, preferred_element_type=F32)
        out = part if out is None else out + part
    return out


def neg_kernel(live_ref, fetched, pos_ref, out_ref, rows, sem):
    load_live(live_ref, fetched, rows, sem)
    out_ref[...] = pick(rows, pos_ref[...]).astype(BF16)


def gather_negs(live, fetched, pos):
    width = fetched.shape[1]
    total = live.shape[0] * BLK
    return pl.pallas_call(
        neg_kernel,
        out_shape=(
            jax.ShapeDtypeStruct((width, pos.shape[1]), BF16),
            jax.ShapeDtypeStruct((width, total), BF16),
        ),
        in_specs=[smem(), anywhere(), whole()],
        out_specs=(whole(), whole()),
        scratch_shapes=[pltpu.SemaphoreType.DMA],
        compiler_params=params(4 * width * total),
        name="gather_negs",
    )(live, fetched, pos)


def edge_kernel(rows, spos, dpos, op_ref, src_ref, dst_ref, gpos_ref):
    source = pick(rows, spos[...])
    target = pick(rows, dpos[...])
    u = source * op_ref[...]
    positive = jnp.sum(u * target, axis=0, keepdims=True)
    gpos_ref[...] = -jax.nn.sigmoid(-positive)
    src_ref[...] = source.astype(BF16)
    dst_ref[...] = target.astype(BF16)


def gather_edges(rows, spos, dpos, operator, tile=512):
    width, total = rows.shape
    edges = spos.shape[1]
    lane = pl.BlockSpec((1, tile), lambda i: (0, i))
    column = pl.BlockSpec((width, tile), lambda i: (0, i))
    return pl.pallas_call(
        edge_kernel,
        grid=(edges // tile,),
        out_shape=(
            jax.ShapeDtypeStruct((width, edges), BF16),
            jax.ShapeDtypeStruct((width, edges), BF16),
            jax.ShapeDtypeStruct((1, edges), F32),
        ),
        in_specs=[whole(), lane, lane, column],
        out_specs=(column, column, lane),
        compiler_params=params(2 * width * total + 8 * MIB),
        cost_estimate=cost(4 * width * total * edges),
        name="gather_edges",
    )(rows, spos, dpos, operator)


def split(x):
    high = x.astype(BF16)
    return high, (x - high.astype(F32)).astype(BF16)


def score_kernel(groups, *refs):
    negs = refs[:groups]
    src_ref, dst_ref, op_ref, gpos_ref, gs_ref, gd_ref = refs[groups : groups + 6]
    outs = refs[groups + 6 : 2 * groups + 6]
    each = negs[0].shape[1]
    count = groups * each
    wide = jnp.concatenate([n[...] for n in negs], axis=1)
    tall = jnp.concatenate([n[...].T for n in negs], axis=0)
    operator = op_ref[...]
    u = src_ref[...].astype(F32) * operator
    u_half = u.astype(BF16)
    scores = jnp.dot(tall, u_half, preferred_element_type=F32)
    g_neg = (jax.nn.sigmoid(scores) / count).astype(BF16)
    sums = lax.dot_general(u_half, g_neg, NT, preferred_element_type=F32)
    for g in range(groups):
        outs[g][...] = sums[:, g * each : (g + 1) * each].astype(BF16)
    g_pos = gpos_ref[...]
    grad_u = g_pos * dst_ref[...].astype(F32) + jnp.dot(wide, g_neg, preferred_element_type=F32)
    gs_ref[0], gs_ref[1] = split(grad_u * operator)
    gd_ref[0], gd_ref[1] = split(g_pos * u)


def score(negs, source, target, operator, g_pos):
    groups = len(negs)
    width, each = negs[0].shape
    edges = source.shape[1]
    out = pl.pallas_call(
        functools.partial(score_kernel, groups),
        out_shape=(
            jax.ShapeDtypeStruct((2, width, edges), BF16),
            jax.ShapeDtypeStruct((2, width, edges), BF16),
            *[jax.ShapeDtypeStruct((width, each), BF16)] * groups,
        ),
        in_specs=[whole()] * (groups + 4),
        out_specs=(whole(),) * (groups + 2),
        compiler_params=params(20 * MIB),
        cost_estimate=cost(6 * width * edges * groups * each),
        name="score",
    )(*negs, source, target, operator, g_pos)
    return out[0], out[1], out[2:]


def scatter_kernel(first, gs_ref, gd_ref, spos, dpos, out_ref):
    width, edges = gs_ref.shape[1:]

    def tile(t, _):
        index = lax.broadcasted_iota(jnp.int32, (TILE, edges), 0) + (first + t * TILE)
        both = None
        for grads, pos in ((gs_ref, spos), (gd_ref, dpos)):
            hot = jnp.where(index == pos[...], 1.0, 0.0).astype(BF16)
            part = lax.dot_general(
                grads[...].reshape(2 * width, edges), hot, NT, preferred_element_type=F32
            )
            both = part if both is None else both + part
        out_ref[:, pl.ds(pl.multiple_of(t * TILE, TILE), TILE)] = both[:width] + both[width:]
        return 0

    lax.fori_loop(0, out_ref.shape[1] // TILE, tile, 0)


def scatter(first, after, grads_src, grads_dst, spos, dpos):
    width, edges = grads_src.shape[1:]
    rows = (after - first) * BLK
    return pl.pallas_call(
        functools.partial(scatter_kernel, first * BLK),
        out_shape=jax.ShapeDtypeStruct((width, rows), F32),
        in_specs=[whole(), whole(), whole(), whole()],
        out_specs=whole(),
        compiler_params=params(4 * width * rows),
        cost_estimate=cost(4 * width * rows * edges),
        name="scatter",
    )(grads_src, grads_dst, spos, dpos)


def encode(x, out_ref):
    width = x.shape[0]
    top = jnp.max(jnp.abs(x), axis=0, keepdims=True)
    power = jnp.ceil(jnp.log2(jnp.maximum(top, 1e-30)))
    code = jnp.clip(jnp.round(x * jnp.exp2(15.0 - power)), -32767.0, 32767.0)
    out_ref[:width, :] = code.astype(jnp.int32).astype(jnp.int16)
    tail = jnp.broadcast_to(power, (TAIL, x.shape[1]))
    out_ref[width:, :] = tail.astype(jnp.int32).astype(jnp.int16)


def decode(code, width):
    power = code[width:, :].astype(jnp.int32).astype(F32)[:1]
    return code[:width, :].astype(jnp.int32).astype(F32) * jnp.exp2(power - 15.0)


def pack_kernel(first, bounds, peers, rank_ref, live_ref, npos, *refs):
    chunks, grads = refs[: len(bounds)], refs[len(bounds) : len(bounds) + peers]
    outs, total, slot = refs[len(bounds) + peers : -2], refs[-2], refs[-1]
    width = slot.shape[0]
    total[:width], total[width:] = split(sum(g[...].astype(F32) for g in grads))
    for k, out_ref in enumerate(outs):
        alive = live_ref[first + k] > 0
        rank = rank_ref[first + k]

        for chunk, (low, high) in zip(chunks, bounds):

            @pl.when(alive & (rank >= low) & (rank < high))
            def _():
                lanes = pl.ds(pl.multiple_of((rank - low) * BLK, BLK), BLK)
                slot[...] = chunk[:, lanes]

        @pl.when(alive)
        def _():
            index = lax.broadcasted_iota(jnp.int32, (BLK, npos.shape[1]), 0) + rank * BLK
            hot = jnp.where(index == npos[...], 1.0, 0.0).astype(BF16)
            both = lax.dot_general(total[...], hot, NT, preferred_element_type=F32)
            encode(slot[...] + (both[:width] + both[width:]), out_ref)

        @pl.when(jnp.logical_not(alive))
        def _():
            out_ref[...] = jnp.zeros(out_ref.shape, jnp.int16)


def pack(first, group, rank, live, chunks, bounds, grad_negs, npos):
    width = chunks[0].shape[0]
    return pl.pallas_call(
        functools.partial(pack_kernel, first, tuple(bounds), len(grad_negs)),
        out_shape=(jax.ShapeDtypeStruct((width + TAIL, BLK), jnp.int16),) * group,
        in_specs=[smem(), smem()] + [whole()] * (1 + len(chunks) + len(grad_negs)),
        out_specs=(whole(),) * group,
        scratch_shapes=[
            pltpu.VMEM((2 * width, npos.shape[1]), BF16),
            pltpu.VMEM((width, BLK), F32),
        ],
        compiler_params=params(0),
        cost_estimate=cost(4 * width * BLK * BLK * group),
        name="pack",
    )(rank, live, npos, *chunks, *grad_negs)


def add_kernel(first, fresh, asked_ref, *refs):
    grad = refs[-1]
    backs = refs[: -1 if fresh else -2]
    width = grad.shape[0]
    if fresh:
        grad[...] = jnp.zeros_like(grad)
    for k, back in enumerate(backs):
        lanes = pl.ds(pl.multiple_of(asked_ref[first + k] * BLK, BLK), BLK)
        grad[:, lanes] += decode(back, width)


def add(first, asked, backs, grad, width, rows):
    fresh = grad is None
    extra = [] if fresh else [grad]
    return pl.pallas_call(
        functools.partial(add_kernel, first, fresh),
        out_shape=jax.ShapeDtypeStruct((width, rows), F32),
        in_specs=[smem()] + [whole()] * (len(backs) + len(extra)),
        out_specs=whole(),
        input_output_aliases={} if fresh else {len(backs) + 1: 0},
        compiler_params=params(0),
        cost_estimate=cost(width * BLK * len(backs) * 64),
        name="add",
    )(asked, *backs, *extra)


def update_kernel(first, asked_ref, *refs):
    backs = refs[:-7]
    grad, table_ref, state_ref, table_out, state_out, fresh, sems = refs[-7:]
    width, rows = grad.shape
    for k, back in enumerate(backs):
        lanes = pl.ds(pl.multiple_of(asked_ref[first + k] * BLK, BLK), BLK)
        grad[:, lanes] += decode(back, width)
    span = fresh.shape[1] // sems.shape[0]

    def copy(b):
        lanes = pl.ds(pl.multiple_of(b * span, span), span)
        return pltpu.make_async_copy(fresh.at[:, lanes], table_out.at[:, lanes], sems.at[b])

    for b in range(sems.shape[0]):
        for c in range(b * span, (b + 1) * span, BLK):
            lanes = slice(c, c + BLK)
            g = grad[:, lanes]
            new_state = state_ref[:, lanes] + jnp.sum(g * g, axis=0, keepdims=True) / width
            state_out[:, lanes] = new_state
            fresh[:, lanes] = table_ref[:, lanes] - 0.1 * g / (jnp.sqrt(new_state) + 1e-10)
        copy(b).start()
    for b in range(sems.shape[0]):
        copy(b).wait()


def update(first, asked, backs, grad, table, state, parts=4):
    width, rows = table.shape
    return pl.pallas_call(
        functools.partial(update_kernel, first),
        out_shape=(
            jax.ShapeDtypeStruct((width, rows), F32),
            jax.ShapeDtypeStruct((1, rows), F32),
        ),
        in_specs=[smem()] + [whole()] * (len(backs) + 3),
        out_specs=(anywhere(), whole()),
        scratch_shapes=[pltpu.VMEM((width, rows), F32), pltpu.SemaphoreType.DMA((parts,))],
        compiler_params=params(4 * width * rows),
        cost_estimate=cost(width * rows * 64),
        name="update",
    )(asked, *backs, grad, table, state)


def per_device(table, state, relations, rel_ids, block_list, src_pos, dst_pos, neg_pos):
    devices = lax.axis_size(AXES)
    named = devices // 2
    rows_dev, width = table.shape
    blocks = rows_dev // BLK
    wanted = lax.all_to_all(
        block_list.reshape(devices, 1), AXES, split_axis=0, concat_axis=0, tiled=True
    )
    asked = wanted.reshape(devices)
    outgoing = table.reshape(blocks, BLK, width).astype(BF16)[asked]
    fetched = lax.all_to_all(
        outgoing.transpose(0, 2, 1), AXES, split_axis=0, concat_axis=0, tiled=True
    )
    operator = relations[rel_ids].T

    half = devices // 2
    order = [k for pair in zip(range(devices - 1, half - 1, -1), range(half - 1, -1, -1)) for k in pair]
    partners = lax.axis_index(AXES) ^ jnp.array(order, jnp.int32)
    ids = jnp.arange(devices, dtype=jnp.int32)
    seat = partners[:, None] == ids[None, :]
    named_by = jnp.max((src_pos // BLK)[:, None] == ids[None, :], axis=0).astype(jnp.int32)
    alive = jnp.sum(jnp.where(seat, named_by[None, :], 0), axis=1)
    rank = jnp.sum(jnp.where(ids[None, :] < ids[:, None], alive[None, :], 0), axis=1)
    place = jnp.sum(jnp.where(seat, rank[:, None], 0), axis=0)
    slot = jnp.arange(named, dtype=jnp.int32)
    live = jnp.sum(
        jnp.where((rank[None, :] == slot[:, None]) & (alive[None, :] > 0), partners[None, :], 0), axis=1
    )
    asked = jnp.sum(jnp.where(seat, asked[None, :], 0), axis=1)
    sizes = [cut * devices // sum(CUTS) for cut in CUTS]
    firsts = [sum(sizes[:g]) for g in range(len(sizes))]
    steps = [0] + [named * step // STEPS[-1] for step in STEPS]
    bounds = list(zip(steps[:-1], steps[1:]))

    def compact(pos):
        where = jnp.sum(jnp.where((pos // BLK)[:, None] == ids[None, :], place[None, :], 0), axis=1)
        return (where * BLK + pos % BLK).reshape(1, -1)

    spos, dpos, npos = compact(src_pos), compact(dst_pos), compact(neg_pos)
    fetched, operator, live, rank, alive, asked, spos, dpos, npos = lax.optimization_barrier(
        (fetched, operator, live, rank, alive, asked, spos, dpos, npos)
    )

    def swap(x, shift, axis):
        count = lax.axis_size(axis)
        return lax.ppermute(x, axis, [(i, i ^ shift) for i in range(count)])

    peers = lax.axis_size("dst")
    own_negs, rows = gather_negs(live, fetched, npos)
    negs = [own_negs] + [swap(own_negs, shift, "dst") for shift in range(1, peers)]
    source, target, g_pos = gather_edges(rows, spos, dpos, operator)
    grads_src, grads_dst, part_negs = score(negs, source, target, operator, g_pos)
    own_grad = [part_negs[0]] + [swap(part_negs[shift], shift, "dst") for shift in range(1, peers)]
    grad = None
    backs, chunks = [], []
    for g, (first, group) in enumerate(zip(firsts, sizes)):
        if g < len(bounds):
            edges_at = (spos, dpos)
            if g:
                edges_at, backs[:1] = lax.optimization_barrier((edges_at, backs[:1]))
            chunks.append(scatter(*bounds[g], grads_src, grads_dst, *edges_at))
        packed = list(pack(first, group, rank, alive, chunks, bounds[: len(chunks)], own_grad, npos))
        if g:
            ahead = len(backs) // 2
            if grad is None:
                packed, backs[:ahead] = lax.optimization_barrier((packed, backs[:ahead]))
            else:
                packed, backs[:ahead], grad = lax.optimization_barrier((packed, backs[:ahead], grad))
            grad = add(firsts[g - 1], asked, backs, grad, width, rows_dev)
        backs = [
            swap(x, shift, AXES) if shift else x
            for x, shift in zip(packed, order[first : first + group])
        ]
    new_table, new_state = update(
        firsts[-1], asked, backs, grad, table.T, state.reshape(1, rows_dev)
    )
    return (new_table.T, new_state.reshape(rows_dev))


def solution(mesh):
    in_specs = (
        P(AXES, None),
        P(AXES),
        P(),
        P(AXES),
        P(AXES, None),
        P(AXES),
        P(AXES),
        P(AXES),
    )
    out_specs = (P(AXES, None), P(AXES))
    return jax.shard_map(
        per_device, mesh=mesh, in_specs=in_specs, out_specs=out_specs, check_vma=False
    )
```

```python
import functools

import jax
import jax.numpy as jnp
from jax import lax
from jax.experimental import pallas as pl
from jax.experimental.pallas import tpu as pltpu
from jax.sharding import PartitionSpec as P

BLK = 128
TAIL = 8
CUTS = (1, 2, 2, 2, 1)
STEPS = (2, 3, 6, 8)
TILE = 256
AXES = ("src", "dst")
F32 = jnp.float32
BF16 = jnp.bfloat16
NT = (((1,), (1,)), ((), ()))


def params(held):
    return pltpu.CompilerParams(vmem_limit_bytes=14 * 1024 * 1024 + held)


MIB = 1024 * 1024


def cost(flops):
    return pl.CostEstimate(flops=flops, bytes_accessed=flops // 512, transcendentals=0)


def whole():
    return pl.BlockSpec(memory_space=pltpu.VMEM)


def smem():
    return pl.BlockSpec(memory_space=pltpu.SMEM)


def anywhere():
    return pl.BlockSpec(memory_space=pl.ANY)


def load_live(live_ref, fetched, rows, sem):
    count = live_ref.shape[0]

    def copy(k):
        lanes = pl.ds(pl.multiple_of(k * BLK, BLK), BLK)
        return pltpu.make_async_copy(fetched.at[live_ref[k]], rows.at[:, lanes], sem)

    def start(k, _):
        copy(k).start()
        return 0

    def wait(k, _):
        copy(k).wait()
        return 0

    lax.fori_loop(0, count, start, 0)
    lax.fori_loop(0, count, wait, 0)


def pick(rows, positions):
    total = rows.shape[1]
    step = min(total, 2048)
    out = None
    for first in range(0, total, step):
        index = lax.broadcasted_iota(jnp.int32, (step, positions.shape[1]), 0) + first
        hot = jnp.where(index == positions, 1.0, 0.0).astype(BF16)
        part = jnp.dot(rows[:, first : first + step], hot, preferred_element_type=F32)
        out = part if out is None else out + part
    return out


def neg_kernel(live_ref, fetched, pos_ref, out_ref, rows, sem):
    load_live(live_ref, fetched, rows, sem)
    out_ref[...] = pick(rows, pos_ref[...]).astype(BF16)


def gather_negs(live, fetched, pos):
    width = fetched.shape[1]
    total = live.shape[0] * BLK
    return pl.pallas_call(
        neg_kernel,
        out_shape=(
            jax.ShapeDtypeStruct((width, pos.shape[1]), BF16),
            jax.ShapeDtypeStruct((width, total), BF16),
        ),
        in_specs=[smem(), anywhere(), whole()],
        out_specs=(whole(), whole()),
        scratch_shapes=[pltpu.SemaphoreType.DMA],
        compiler_params=params(4 * width * total),
        name="gather_negs",
    )(live, fetched, pos)


def edge_kernel(rows, spos, dpos, op_ref, src_ref, dst_ref, gpos_ref):
    source = pick(rows, spos[...])
    target = pick(rows, dpos[...])
    u = source * op_ref[...]
    positive = jnp.sum(u * target, axis=0, keepdims=True)
    gpos_ref[...] = -jax.nn.sigmoid(-positive)
    src_ref[...] = source.astype(BF16)
    dst_ref[...] = target.astype(BF16)


def gather_edges(rows, spos, dpos, operator, tile=512):
    width, total = rows.shape
    edges = spos.shape[1]
    lane = pl.BlockSpec((1, tile), lambda i: (0, i))
    column = pl.BlockSpec((width, tile), lambda i: (0, i))
    return pl.pallas_call(
        edge_kernel,
        grid=(edges // tile,),
        out_shape=(
            jax.ShapeDtypeStruct((width, edges), BF16),
            jax.ShapeDtypeStruct((width, edges), BF16),
            jax.ShapeDtypeStruct((1, edges), F32),
        ),
        in_specs=[whole(), lane, lane, column],
        out_specs=(column, column, lane),
        compiler_params=params(2 * width * total + 8 * MIB),
        cost_estimate=cost(4 * width * total * edges),
        name="gather_edges",
    )(rows, spos, dpos, operator)


def split(x):
    high = x.astype(BF16)
    return high, (x - high.astype(F32)).astype(BF16)


def score_kernel(groups, *refs):
    negs = refs[:groups]
    src_ref, dst_ref, op_ref, gpos_ref, gs_ref, gd_ref = refs[groups : groups + 6]
    outs = refs[groups + 6 :]
    each = negs[0].shape[1]
    count = groups * each
    wide = jnp.concatenate([n[...] for n in negs], axis=1)
    tall = jnp.concatenate([n[...].T for n in negs], axis=0)
    operator = op_ref[...]
    u = src_ref[...].astype(F32) * operator
    u_half = u.astype(BF16)
    scores = jnp.dot(tall, u_half, preferred_element_type=F32)
    g_neg = (jax.nn.sigmoid(scores) / count).astype(BF16)
    sums = lax.dot_general(u_half, g_neg, NT, preferred_element_type=F32)
    for g in range(groups):
        outs[g // 2][g % 2] = sums[:, g * each : (g + 1) * each].astype(BF16)
    g_pos = gpos_ref[...]
    grad_u = g_pos * dst_ref[...].astype(F32) + jnp.dot(wide, g_neg, preferred_element_type=F32)
    gs_ref[0], gs_ref[1] = split(grad_u * operator)
    gd_ref[0], gd_ref[1] = split(g_pos * u)


def score(negs, source, target, operator, g_pos):
    groups = len(negs)
    width, each = negs[0].shape
    edges = source.shape[1]
    out = pl.pallas_call(
        functools.partial(score_kernel, groups),
        out_shape=(
            jax.ShapeDtypeStruct((2, width, edges), BF16),
            jax.ShapeDtypeStruct((2, width, edges), BF16),
            *[jax.ShapeDtypeStruct((2, width, each), BF16)] * (groups // 2),
        ),
        in_specs=[whole()] * (groups + 4),
        out_specs=(whole(),) * (groups // 2 + 2),
        compiler_params=params(20 * MIB),
        cost_estimate=cost(6 * width * edges * groups * each),
        name="score",
    )(*negs, source, target, operator, g_pos)
    return out[0], out[1], out[2:]


def mix_kernel(*refs):
    parts, own_ref, other_ref = refs[:-2], refs[-2], refs[-1]
    own_ref[...] = sum(p[0].astype(F32) for p in parts)
    other_ref[...] = sum(p[1].astype(F32) for p in parts).astype(BF16)


def mix(parts):
    shape = parts[0].shape[1:]
    return pl.pallas_call(
        mix_kernel,
        out_shape=(jax.ShapeDtypeStruct(shape, F32), jax.ShapeDtypeStruct(shape, BF16)),
        in_specs=[whole()] * len(parts),
        out_specs=(whole(), whole()),
        compiler_params=params(0),
        cost_estimate=cost(MIB),
        name="mix",
    )(*parts)


def scatter_kernel(first, gs_ref, gd_ref, spos, dpos, out_ref):
    width, edges = gs_ref.shape[1:]

    def tile(t, _):
        index = lax.broadcasted_iota(jnp.int32, (TILE, edges), 0) + (first + t * TILE)
        both = None
        for grads, pos in ((gs_ref, spos), (gd_ref, dpos)):
            hot = jnp.where(index == pos[...], 1.0, 0.0).astype(BF16)
            part = lax.dot_general(
                grads[...].reshape(2 * width, edges), hot, NT, preferred_element_type=F32
            )
            both = part if both is None else both + part
        out_ref[:, pl.ds(pl.multiple_of(t * TILE, TILE), TILE)] = both[:width] + both[width:]
        return 0

    lax.fori_loop(0, out_ref.shape[1] // TILE, tile, 0)


def scatter(first, after, grads_src, grads_dst, spos, dpos):
    width, edges = grads_src.shape[1:]
    rows = (after - first) * BLK
    return pl.pallas_call(
        functools.partial(scatter_kernel, first * BLK),
        out_shape=jax.ShapeDtypeStruct((width, rows), F32),
        in_specs=[whole(), whole(), whole(), whole()],
        out_specs=whole(),
        compiler_params=params(4 * width * rows),
        cost_estimate=cost(4 * width * rows * edges),
        name="scatter",
    )(grads_src, grads_dst, spos, dpos)


def encode(x, out_ref):
    width = x.shape[0]
    top = jnp.max(jnp.abs(x), axis=0, keepdims=True)
    power = jnp.ceil(jnp.log2(jnp.maximum(top, 1e-30)))
    code = jnp.clip(jnp.round(x * jnp.exp2(15.0 - power)), -32767.0, 32767.0)
    out_ref[:width, :] = code.astype(jnp.int32).astype(jnp.int16)
    tail = jnp.broadcast_to(power, (TAIL, x.shape[1]))
    out_ref[width:, :] = tail.astype(jnp.int32).astype(jnp.int16)


def decode(code, width):
    power = code[width:, :].astype(jnp.int32).astype(F32)[:1]
    return code[:width, :].astype(jnp.int32).astype(F32) * jnp.exp2(power - 15.0)


def pack_kernel(first, bounds, peers, rank_ref, live_ref, npos, *refs):
    chunks, grads = refs[: len(bounds)], refs[len(bounds) : len(bounds) + peers]
    outs, total, slot = refs[len(bounds) + peers : -2], refs[-2], refs[-1]
    width = slot.shape[0]
    total[:width], total[width:] = split(sum(g[...].astype(F32) for g in grads))
    seats = []
    for out in outs:
        seats += [out.at[0], out.at[1]] if len(out.shape) == 3 else [out]
    for k, out_ref in enumerate(seats):
        alive = live_ref[first + k] > 0
        rank = rank_ref[first + k]

        for chunk, (low, high) in zip(chunks, bounds):

            @pl.when(alive & (rank >= low) & (rank < high))
            def _():
                lanes = pl.ds(pl.multiple_of((rank - low) * BLK, BLK), BLK)
                slot[...] = chunk[:, lanes]

        @pl.when(alive)
        def _():
            index = lax.broadcasted_iota(jnp.int32, (BLK, npos.shape[1]), 0) + rank * BLK
            hot = jnp.where(index == npos[...], 1.0, 0.0).astype(BF16)
            both = lax.dot_general(total[...], hot, NT, preferred_element_type=F32)
            encode(slot[...] + (both[:width] + both[width:]), out_ref)

        @pl.when(jnp.logical_not(alive))
        def _():
            out_ref[...] = jnp.zeros(out_ref.shape, jnp.int16)


def pack(first, group, paired, rank, live, chunks, bounds, grad_negs, npos):
    width = chunks[0].shape[0]
    block = (width + TAIL, BLK)
    shape, outs = ((2,) + block, group // 2) if paired else (block, group)
    return pl.pallas_call(
        functools.partial(pack_kernel, first, tuple(bounds), len(grad_negs)),
        out_shape=(jax.ShapeDtypeStruct(shape, jnp.int16),) * outs,
        in_specs=[smem(), smem()] + [whole()] * (1 + len(chunks) + len(grad_negs)),
        out_specs=(whole(),) * outs,
        scratch_shapes=[
            pltpu.VMEM((2 * width, npos.shape[1]), BF16),
            pltpu.VMEM((width, BLK), F32),
        ],
        compiler_params=params(0),
        cost_estimate=cost(4 * width * BLK * BLK * group),
        name="pack",
    )(rank, live, npos, *chunks, *grad_negs)


def add_blocks(grad, asked_ref, places, blocks):
    for place, block in zip(places, blocks):
        lanes = pl.ds(pl.multiple_of(asked_ref[place] * BLK, BLK), BLK)
        grad[:, lanes] += decode(block[...], grad.shape[0])


def add_kernel(first, count, before, fresh, asked_ref, *refs):
    backs, grad, on_ref = refs[:count], refs[-2], refs[-1]
    if fresh:
        grad[...] = jnp.zeros_like(grad)
    for k, back in enumerate(backs):
        on_ref[k] = back[1]
    add_blocks(grad, asked_ref, range(first, first + 2 * count, 2), [b.at[0] for b in backs])
    if before:
        handed = refs[count]
        add_blocks(
            grad,
            asked_ref,
            range(before[0] + 1, before[0] + 2 * before[1], 2),
            [handed.at[k] for k in range(before[1])],
        )


def add(first, asked, backs, before, handed, grad, width, rows):
    fresh = grad is None
    more = [] if handed is None else [handed]
    if not fresh:
        more.append(grad)
    return pl.pallas_call(
        functools.partial(add_kernel, first, len(backs), before, fresh),
        out_shape=(
            jax.ShapeDtypeStruct((width, rows), F32),
            jax.ShapeDtypeStruct((len(backs),) + backs[0].shape[1:], backs[0].dtype),
        ),
        in_specs=[smem()] + [whole()] * (len(backs) + len(more)),
        out_specs=(whole(), whole()),
        input_output_aliases={} if fresh else {len(backs) + len(more): 0},
        compiler_params=params(0),
        cost_estimate=cost(width * BLK * len(backs) * 64),
        name="add",
    )(asked, *backs, *more)


def update_kernel(first, before, asked_ref, *refs):
    backs, handed = refs[:-8], refs[-8]
    grad, table_ref, state_ref, table_out, state_out, fresh, sems = refs[-7:]
    width, rows = grad.shape
    places = range(before[0] + 1, before[0] + 2 * before[1], 2)
    add_blocks(grad, asked_ref, places, [handed.at[k] for k in range(before[1])])
    add_blocks(grad, asked_ref, range(first, first + len(backs)), backs)
    span = fresh.shape[1] // sems.shape[0]

    def copy(b):
        lanes = pl.ds(pl.multiple_of(b * span, span), span)
        return pltpu.make_async_copy(fresh.at[:, lanes], table_out.at[:, lanes], sems.at[b])

    for b in range(sems.shape[0]):
        for c in range(b * span, (b + 1) * span, BLK):
            lanes = slice(c, c + BLK)
            g = grad[:, lanes]
            new_state = state_ref[:, lanes] + jnp.sum(g * g, axis=0, keepdims=True) / width
            state_out[:, lanes] = new_state
            fresh[:, lanes] = table_ref[:, lanes] - 0.1 * g / (jnp.sqrt(new_state) + 1e-10)
        copy(b).start()
    for b in range(sems.shape[0]):
        copy(b).wait()


def update(first, asked, backs, before, handed, grad, table, state, parts=4):
    width, rows = table.shape
    return pl.pallas_call(
        functools.partial(update_kernel, first, before),
        out_shape=(
            jax.ShapeDtypeStruct((width, rows), F32),
            jax.ShapeDtypeStruct((1, rows), F32),
        ),
        in_specs=[smem()] + [whole()] * (len(backs) + 4),
        out_specs=(anywhere(), whole()),
        scratch_shapes=[pltpu.VMEM((width, rows), F32), pltpu.SemaphoreType.DMA((parts,))],
        compiler_params=params(4 * width * rows),
        cost_estimate=cost(width * rows * 64),
        name="update",
    )(asked, *backs, handed, grad, table, state)


def per_device(table, state, relations, rel_ids, block_list, src_pos, dst_pos, neg_pos):
    devices = lax.axis_size(AXES)
    named = devices // 2
    rows_dev, width = table.shape
    blocks = rows_dev // BLK
    wanted = lax.all_to_all(
        block_list.reshape(devices, 1), AXES, split_axis=0, concat_axis=0, tiled=True
    )
    asked = wanted.reshape(devices)
    outgoing = table.reshape(blocks, BLK, width).astype(BF16)[asked]
    fetched = lax.all_to_all(
        outgoing.transpose(0, 2, 1), AXES, split_axis=0, concat_axis=0, tiled=True
    )
    operator = relations[rel_ids].T

    pairs = devices // 2
    far, near = list(range(pairs - 1, pairs // 2 - 1, -1)), list(range(pairs // 2 - 1, -1, -1))
    lead = pairs // sum(CUTS)
    chips = far[:lead]
    for f, n in zip(far[lead:], near):
        chips += [f, n]
    chips += near[len(far) - lead :]
    order = [2 * chip + side for chip in chips for side in range(2)]
    partners = lax.axis_index(AXES) ^ jnp.array(order, jnp.int32)
    ids = jnp.arange(devices, dtype=jnp.int32)
    seat = partners[:, None] == ids[None, :]
    named_by = jnp.max((src_pos // BLK)[:, None] == ids[None, :], axis=0).astype(jnp.int32)
    alive = jnp.sum(jnp.where(seat, named_by[None, :], 0), axis=1)
    rank = jnp.sum(jnp.where(ids[None, :] < ids[:, None], alive[None, :], 0), axis=1)
    place = jnp.sum(jnp.where(seat, rank[:, None], 0), axis=0)
    slot = jnp.arange(named, dtype=jnp.int32)
    live = jnp.sum(
        jnp.where((rank[None, :] == slot[:, None]) & (alive[None, :] > 0), partners[None, :], 0), axis=1
    )
    asked = jnp.sum(jnp.where(seat, asked[None, :], 0), axis=1)
    sizes = [cut * devices // sum(CUTS) for cut in CUTS]
    firsts = [sum(sizes[:g]) for g in range(len(sizes))]
    steps = [0] + [named * step // STEPS[-1] for step in STEPS]
    bounds = list(zip(steps[:-1], steps[1:]))

    def compact(pos):
        where = jnp.sum(jnp.where((pos // BLK)[:, None] == ids[None, :], place[None, :], 0), axis=1)
        return (where * BLK + pos % BLK).reshape(1, -1)

    spos, dpos, npos = compact(src_pos), compact(dst_pos), compact(neg_pos)
    fetched, operator, live, rank, alive, asked, spos, dpos, npos = lax.optimization_barrier(
        (fetched, operator, live, rank, alive, asked, spos, dpos, npos)
    )

    def swap(x, shift, axis):
        count = lax.axis_size(axis)
        return lax.ppermute(x, axis, [(i, i ^ shift) for i in range(count)])

    peers = lax.axis_size("dst")
    own_negs, rows = gather_negs(live, fetched, npos)
    negs = [own_negs] + [swap(own_negs, shift, "dst") for shift in range(1, peers)]
    source, target, g_pos = gather_edges(rows, spos, dpos, operator)
    grads_src, grads_dst, part_negs = score(negs, source, target, operator, g_pos)
    parts = [part_negs[0]]
    parts += [swap(part_negs[pair], 2 * pair, "dst") for pair in range(1, peers // 2)]
    chunks = [scatter(*bounds[0], grads_src, grads_dst, spos, dpos)]
    parts, chunks = lax.optimization_barrier((parts, chunks))
    mine, other = mix(parts)
    own_grad = [mine, swap(other, 1, "dst")]
    grad, handed, before, backs = None, None, None, []
    for g, (first, group) in enumerate(zip(firsts, sizes)):
        last = g == len(sizes) - 1
        if len(chunks) < len(bounds):
            edges_at = (spos, dpos)
            if g > 1:
                edges_at, backs[:1] = lax.optimization_barrier((edges_at, backs[:1]))
            chunks.append(scatter(*bounds[len(chunks)], grads_src, grads_dst, *edges_at))
        packed = list(
            pack(first, group, not last, rank, alive, chunks, bounds[: len(chunks)], own_grad, npos)
        )
        if g:
            ahead = len(backs) // 2
            packed, backs[:ahead], grad = lax.optimization_barrier((packed, backs[:ahead], grad))
        shifts = order[first : first + group : 1 if last else 2]
        sent = [swap(x, shift, AXES) if shift else x for x, shift in zip(packed, shifts)]
        if g:
            backs, sent[:1] = lax.optimization_barrier((backs, sent[:1]))
            now = (firsts[g - 1], len(backs))
            grad, hand = add(now[0], asked, backs, before, handed, grad, width, rows_dev)
            before, handed = now, swap(hand, 1, AXES)
        backs = sent
    new_table, new_state = update(
        firsts[-1], asked, backs, before, handed, grad, table.T, state.reshape(1, rows_dev)
    )
    return (new_table.T, new_state.reshape(rows_dev))


def solution(mesh):
    in_specs = (
        P(AXES, None),
        P(AXES),
        P(),
        P(AXES),
        P(AXES, None),
        P(AXES),
        P(AXES),
        P(AXES),
    )
    out_specs = (P(AXES, None), P(AXES))
    return jax.shard_map(
        per_device, mesh=mesh, in_specs=in_specs, out_specs=out_specs, check_vma=False
    )
```

```python
import functools

import jax
import jax.numpy as jnp
from jax import lax
from jax.experimental import pallas as pl
from jax.experimental.pallas import tpu as pltpu
from jax.sharding import PartitionSpec as P

BLK = 128
TAIL = 8
CUTS = (1, 2, 2, 2, 1)
STEPS = (3, 6, 8)
WINDOW = 5
TILE = 256
AXES = ("src", "dst")
F32 = jnp.float32
BF16 = jnp.bfloat16
NT = (((1,), (1,)), ((), ()))


def params(held):
    return pltpu.CompilerParams(vmem_limit_bytes=14 * 1024 * 1024 + held)


MIB = 1024 * 1024


def cost(flops):
    return pl.CostEstimate(flops=flops // 64, bytes_accessed=flops // 32768, transcendentals=0)


def whole():
    return pl.BlockSpec(memory_space=pltpu.VMEM)


def smem():
    return pl.BlockSpec(memory_space=pltpu.SMEM)


def anywhere():
    return pl.BlockSpec(memory_space=pl.ANY)


def load_live(live_ref, fetched, rows, sem):
    count = live_ref.shape[0]

    def copy(k):
        lanes = pl.ds(pl.multiple_of(k * BLK, BLK), BLK)
        return pltpu.make_async_copy(fetched.at[live_ref[k]], rows.at[:, lanes], sem)

    def start(k, _):
        copy(k).start()
        return 0

    def wait(k, _):
        copy(k).wait()
        return 0

    lax.fori_loop(0, count, start, 0)
    lax.fori_loop(0, count, wait, 0)


def pick(rows, positions):
    total = rows.shape[1]
    step = min(total, 2048)
    out = None
    for first in range(0, total, step):
        index = lax.broadcasted_iota(jnp.int32, (step, positions.shape[1]), 0) + first
        hot = jnp.where(index == positions, 1.0, 0.0).astype(BF16)
        part = jnp.dot(rows[:, first : first + step], hot, preferred_element_type=F32)
        out = part if out is None else out + part
    return out


def neg_kernel(live_ref, fetched, pos_ref, out_ref, rows, sem):
    load_live(live_ref, fetched, rows, sem)
    out_ref[...] = pick(rows, pos_ref[...]).astype(BF16)


def gather_negs(live, fetched, pos):
    width = fetched.shape[1]
    total = live.shape[0] * BLK
    return pl.pallas_call(
        neg_kernel,
        out_shape=(
            jax.ShapeDtypeStruct((width, pos.shape[1]), BF16),
            jax.ShapeDtypeStruct((width, total), BF16),
        ),
        in_specs=[smem(), anywhere(), whole()],
        out_specs=(whole(), whole()),
        scratch_shapes=[pltpu.SemaphoreType.DMA],
        compiler_params=params(4 * width * total),
        name="gather_negs",
    )(live, fetched, pos)


def edge_kernel(rows, spos, dpos, op_ref, src_ref, dst_ref, gpos_ref):
    source = pick(rows, spos[...])
    target = pick(rows, dpos[...])
    u = source * op_ref[...]
    positive = jnp.sum(u * target, axis=0, keepdims=True)
    gpos_ref[...] = -jax.nn.sigmoid(-positive)
    src_ref[...] = source.astype(BF16)
    dst_ref[...] = target.astype(BF16)


def gather_edges(rows, spos, dpos, operator, tile=512):
    width, total = rows.shape
    edges = spos.shape[1]
    lane = pl.BlockSpec((1, tile), lambda i: (0, i))
    column = pl.BlockSpec((width, tile), lambda i: (0, i))
    return pl.pallas_call(
        edge_kernel,
        grid=(edges // tile,),
        out_shape=(
            jax.ShapeDtypeStruct((width, edges), BF16),
            jax.ShapeDtypeStruct((width, edges), BF16),
            jax.ShapeDtypeStruct((1, edges), F32),
        ),
        in_specs=[whole(), lane, lane, column],
        out_specs=(column, column, lane),
        compiler_params=params(2 * width * total + 8 * MIB),
        cost_estimate=cost(4 * width * total * edges),
        name="gather_edges",
    )(rows, spos, dpos, operator)


def split(x):
    high = x.astype(BF16)
    return high, (x - high.astype(F32)).astype(BF16)


def score_kernel(groups, *refs):
    negs = refs[:groups]
    src_ref, dst_ref, op_ref, gpos_ref, gs_ref, gd_ref = refs[groups : groups + 6]
    outs = refs[groups + 6 : 2 * groups + 6]
    each = negs[0].shape[1]
    count = groups * each
    wide = jnp.concatenate([n[...] for n in negs], axis=1)
    tall = jnp.concatenate([n[...].T for n in negs], axis=0)
    operator = op_ref[...]
    u = src_ref[...].astype(F32) * operator
    u_half = u.astype(BF16)
    scores = jnp.dot(tall, u_half, preferred_element_type=F32)
    g_neg = (jax.nn.sigmoid(scores) / count).astype(BF16)
    sums = lax.dot_general(u_half, g_neg, NT, preferred_element_type=F32)
    for g in range(groups):
        outs[g][...] = sums[:, g * each : (g + 1) * each].astype(BF16)
    g_pos = gpos_ref[...]
    grad_u = g_pos * dst_ref[...].astype(F32) + jnp.dot(wide, g_neg, preferred_element_type=F32)
    gs_ref[0], gs_ref[1] = split(grad_u * operator)
    gd_ref[0], gd_ref[1] = split(g_pos * u)


def score(negs, source, target, operator, g_pos):
    groups = len(negs)
    width, each = negs[0].shape
    edges = source.shape[1]
    out = pl.pallas_call(
        functools.partial(score_kernel, groups),
        out_shape=(
            jax.ShapeDtypeStruct((2, width, edges), BF16),
            jax.ShapeDtypeStruct((2, width, edges), BF16),
            *[jax.ShapeDtypeStruct((width, each), BF16)] * groups,
        ),
        in_specs=[whole()] * (groups + 4),
        out_specs=(whole(),) * (groups + 2),
        compiler_params=params(20 * MIB),
        cost_estimate=cost(6 * width * edges * groups * each),
        name="score",
    )(*negs, source, target, operator, g_pos)
    return out[0], out[1], out[2:]


def scatter_kernel(first, gs_ref, gd_ref, spos, dpos, out_ref):
    width, edges = gs_ref.shape[1:]

    def tile(t, _):
        index = lax.broadcasted_iota(jnp.int32, (TILE, edges), 0) + (first + t * TILE)
        both = None
        for grads, pos in ((gs_ref, spos), (gd_ref, dpos)):
            hot = jnp.where(index == pos[...], 1.0, 0.0).astype(BF16)
            part = lax.dot_general(
                grads[...].reshape(2 * width, edges), hot, NT, preferred_element_type=F32
            )
            both = part if both is None else both + part
        out_ref[:, pl.ds(pl.multiple_of(t * TILE, TILE), TILE)] = both[:width] + both[width:]
        return 0

    lax.fori_loop(0, out_ref.shape[1] // TILE, tile, 0)


def scatter(first, after, grads_src, grads_dst, spos, dpos):
    width, edges = grads_src.shape[1:]
    rows = (after - first) * BLK
    return pl.pallas_call(
        functools.partial(scatter_kernel, first * BLK),
        out_shape=jax.ShapeDtypeStruct((width, rows), F32),
        in_specs=[whole(), whole(), whole(), whole()],
        out_specs=whole(),
        compiler_params=params(4 * width * rows),
        cost_estimate=cost(4 * width * rows * edges),
        name="scatter",
    )(grads_src, grads_dst, spos, dpos)


def encode(x, out_ref):
    width = x.shape[0]
    top = jnp.max(jnp.abs(x), axis=0, keepdims=True)
    power = jnp.ceil(jnp.log2(jnp.maximum(top, 1e-30)))
    code = jnp.clip(jnp.round(x * jnp.exp2(15.0 - power)), -32767.0, 32767.0)
    out_ref[:width, :] = code.astype(jnp.int32).astype(jnp.int16)
    tail = jnp.broadcast_to(power, (TAIL, x.shape[1]))
    out_ref[width:, :] = tail.astype(jnp.int32).astype(jnp.int16)


def decode(code, width):
    power = code[width:, :].astype(jnp.int32).astype(F32)[:1]
    return code[:width, :].astype(jnp.int32).astype(F32) * jnp.exp2(power - 15.0)


def pack_kernel(first, bounds, peers, rank_ref, live_ref, npos, *refs):
    chunks, grads = refs[: len(bounds)], refs[len(bounds) : len(bounds) + peers]
    outs, total, slot = refs[len(bounds) + peers : -2], refs[-2], refs[-1]
    width = slot.shape[0]
    total[:width], total[width:] = split(sum(g[...].astype(F32) for g in grads))
    for k, out_ref in enumerate(outs):
        alive = live_ref[first + k] > 0
        rank = rank_ref[first + k]

        for chunk, (low, high) in zip(chunks, bounds):

            @pl.when(alive & (rank >= low) & (rank < high))
            def _():
                lanes = pl.ds(pl.multiple_of((rank - low) * BLK, BLK), BLK)
                slot[...] = chunk[:, lanes]

        @pl.when(alive)
        def _():
            index = lax.broadcasted_iota(jnp.int32, (BLK, npos.shape[1]), 0) + rank * BLK
            hot = jnp.where(index == npos[...], 1.0, 0.0).astype(BF16)
            both = lax.dot_general(total[...], hot, NT, preferred_element_type=F32)
            encode(slot[...] + (both[:width] + both[width:]), out_ref)

        @pl.when(jnp.logical_not(alive))
        def _():
            out_ref[...] = jnp.zeros(out_ref.shape, jnp.int16)


def pack(first, group, rank, live, chunks, bounds, grad_negs, npos):
    width = chunks[0].shape[0]
    return pl.pallas_call(
        functools.partial(pack_kernel, first, tuple(bounds), len(grad_negs)),
        out_shape=(jax.ShapeDtypeStruct((width + TAIL, BLK), jnp.int16),) * group,
        in_specs=[smem(), smem()] + [whole()] * (1 + len(chunks) + len(grad_negs)),
        out_specs=(whole(),) * group,
        scratch_shapes=[
            pltpu.VMEM((2 * width, npos.shape[1]), BF16),
            pltpu.VMEM((width, BLK), F32),
        ],
        compiler_params=params(0),
        cost_estimate=cost(4 * width * BLK * BLK * group),
        name="pack",
    )(rank, live, npos, *chunks, *grad_negs)


def add_kernel(first, fresh, asked_ref, *refs):
    grad = refs[-1]
    backs = refs[: -1 if fresh else -2]
    width = grad.shape[0]
    if fresh:
        grad[...] = jnp.zeros_like(grad)
    for k, back in enumerate(backs):
        lanes = pl.ds(pl.multiple_of(asked_ref[first + k] * BLK, BLK), BLK)
        grad[:, lanes] += decode(back, width)


def add(first, asked, backs, grad, width, rows):
    fresh = grad is None
    extra = [] if fresh else [grad]
    return pl.pallas_call(
        functools.partial(add_kernel, first, fresh),
        out_shape=jax.ShapeDtypeStruct((width, rows), F32),
        in_specs=[smem()] + [whole()] * (len(backs) + len(extra)),
        out_specs=whole(),
        input_output_aliases={} if fresh else {len(backs) + 1: 0},
        compiler_params=params(0),
        cost_estimate=cost(width * BLK * len(backs) * 64),
        name="add",
    )(asked, *backs, *extra)


def update_kernel(first, asked_ref, *refs):
    backs = refs[:-7]
    grad, table_ref, state_ref, table_out, state_out, fresh, sems = refs[-7:]
    width, rows = grad.shape
    for k, back in enumerate(backs):
        lanes = pl.ds(pl.multiple_of(asked_ref[first + k] * BLK, BLK), BLK)
        grad[:, lanes] += decode(back, width)
    span = fresh.shape[1] // sems.shape[0]

    def copy(b):
        lanes = pl.ds(pl.multiple_of(b * span, span), span)
        return pltpu.make_async_copy(fresh.at[:, lanes], table_out.at[:, lanes], sems.at[b])

    for b in range(sems.shape[0]):
        for c in range(b * span, (b + 1) * span, BLK):
            lanes = slice(c, c + BLK)
            g = grad[:, lanes]
            new_state = state_ref[:, lanes] + jnp.sum(g * g, axis=0, keepdims=True) / width
            state_out[:, lanes] = new_state
            fresh[:, lanes] = table_ref[:, lanes] - 0.1 * g / (jnp.sqrt(new_state) + 1e-10)
        copy(b).start()
    for b in range(sems.shape[0]):
        copy(b).wait()


def update(first, asked, backs, grad, table, state, parts=4):
    width, rows = table.shape
    return pl.pallas_call(
        functools.partial(update_kernel, first),
        out_shape=(
            jax.ShapeDtypeStruct((width, rows), F32),
            jax.ShapeDtypeStruct((1, rows), F32),
        ),
        in_specs=[smem()] + [whole()] * (len(backs) + 3),
        out_specs=(anywhere(), whole()),
        scratch_shapes=[pltpu.VMEM((width, rows), F32), pltpu.SemaphoreType.DMA((parts,))],
        compiler_params=params(4 * width * rows),
        cost_estimate=cost(width * rows * 64),
        name="update",
    )(asked, *backs, grad, table, state)


def per_device(table, state, relations, rel_ids, block_list, src_pos, dst_pos, neg_pos):
    devices = lax.axis_size(AXES)
    named = devices // 2
    rows_dev, width = table.shape
    blocks = rows_dev // BLK
    wanted = lax.all_to_all(
        block_list.reshape(devices, 1), AXES, split_axis=0, concat_axis=0, tiled=True
    )
    asked = wanted.reshape(devices)
    outgoing = table.reshape(blocks, BLK, width).astype(BF16)[asked]
    fetched = lax.all_to_all(
        outgoing.transpose(0, 2, 1), AXES, split_axis=0, concat_axis=0, tiled=True
    )
    operator = relations[rel_ids].T

    half = devices // 2
    far, near = list(range(devices - 1, half - 1, -1)), list(range(half - 1, -1, -1))
    lead = devices // 8
    order = far[:lead]
    for f, n in zip(far[lead:], near):
        order += [f, n]
    order += near[half - lead :]
    partners = lax.axis_index(AXES) ^ jnp.array(order, jnp.int32)
    ids = jnp.arange(devices, dtype=jnp.int32)
    seat = partners[:, None] == ids[None, :]
    named_by = jnp.max((src_pos // BLK)[:, None] == ids[None, :], axis=0).astype(jnp.int32)
    alive = jnp.sum(jnp.where(seat, named_by[None, :], 0), axis=1)
    rank = jnp.sum(jnp.where(ids[None, :] < ids[:, None], alive[None, :], 0), axis=1)
    place = jnp.sum(jnp.where(seat, rank[:, None], 0), axis=0)
    slot = jnp.arange(named, dtype=jnp.int32)
    live = jnp.sum(
        jnp.where((rank[None, :] == slot[:, None]) & (alive[None, :] > 0), partners[None, :], 0), axis=1
    )
    asked = jnp.sum(jnp.where(seat, asked[None, :], 0), axis=1)
    sizes = [cut * devices // sum(CUTS) for cut in CUTS]
    firsts = [sum(sizes[:g]) for g in range(len(sizes))]
    steps = [0] + [named * step // STEPS[-1] for step in STEPS]
    bounds = list(zip(steps[:-1], steps[1:]))

    def compact(pos):
        where = jnp.sum(jnp.where((pos // BLK)[:, None] == ids[None, :], place[None, :], 0), axis=1)
        return (where * BLK + pos % BLK).reshape(1, -1)

    spos, dpos, npos = compact(src_pos), compact(dst_pos), compact(neg_pos)
    fetched, operator, live, rank, alive, asked, spos, dpos, npos = lax.optimization_barrier(
        (fetched, operator, live, rank, alive, asked, spos, dpos, npos)
    )

    def swap(x, shift, axis):
        count = lax.axis_size(axis)
        return lax.ppermute(x, axis, [(i, i ^ shift) for i in range(count)])

    peers = lax.axis_size("dst")
    own_negs, rows = gather_negs(live, fetched, npos)
    negs = [own_negs] + [swap(own_negs, shift, "dst") for shift in range(1, peers)]
    source, target, g_pos = gather_edges(rows, spos, dpos, operator)
    grads_src, grads_dst, part_negs = score(negs, source, target, operator, g_pos)
    own_grad = [part_negs[0]] + [swap(part_negs[shift], shift, "dst") for shift in range(1, peers)]
    grad, chunks, flight, queue = None, [], [], []
    for g, (first, group) in enumerate(zip(firsts, sizes)):
        if g < len(bounds):
            edges_at = (spos, dpos)
            if g > 1:
                edges_at, flight[-group] = lax.optimization_barrier((edges_at, flight[-group]))
            chunks.append(scatter(*bounds[g], grads_src, grads_dst, *edges_at))
        packed = pack(first, group, rank, alive, chunks, bounds[: len(chunks)], own_grad, npos)
        for k, (x, shift) in enumerate(zip(packed, order[first : first + group])):
            i = first + k
            if i >= WINDOW:
                x, flight[i - WINDOW] = lax.optimization_barrier((x, flight[i - WINDOW]))
            if k == WINDOW and g > 1:
                x, grad = lax.optimization_barrier((x, grad))
            flight.append(swap(x, shift, AXES) if shift else x)
        if g:
            before = firsts[g - 1]
            grad = add(before, asked, flight[before:first], grad, width, rows_dev)
    backs = flight[firsts[-1] :]
    new_table, new_state = update(
        firsts[-1], asked, backs, grad, table.T, state.reshape(1, rows_dev)
    )
    return (new_table.T, new_state.reshape(rows_dev))


def solution(mesh):
    in_specs = (
        P(AXES, None),
        P(AXES),
        P(),
        P(AXES),
        P(AXES, None),
        P(AXES),
        P(AXES),
        P(AXES),
    )
    out_specs = (P(AXES, None), P(AXES))
    return jax.shard_map(
        per_device, mesh=mesh, in_specs=in_specs, out_specs=out_specs, check_vma=False
    )
```

```python
import functools

import jax
import jax.numpy as jnp
from jax import lax
from jax.experimental import pallas as pl
from jax.experimental.pallas import tpu as pltpu
from jax.sharding import PartitionSpec as P

BLK = 128
TAIL = 8
STEPS = (3, 8)
WINDOW = 5
TILE = 256
AXES = ("far", "near", "dst")
F32 = jnp.float32
BF16 = jnp.bfloat16
NT = (((1,), (1,)), ((), ()))


def params(held):
    return pltpu.CompilerParams(vmem_limit_bytes=14 * 1024 * 1024 + held)


MIB = 1024 * 1024


def cost(flops):
    return pl.CostEstimate(flops=flops // 64, bytes_accessed=flops // 32768, transcendentals=0)


def whole():
    return pl.BlockSpec(memory_space=pltpu.VMEM)


def smem():
    return pl.BlockSpec(memory_space=pltpu.SMEM)


def anywhere():
    return pl.BlockSpec(memory_space=pl.ANY)


def load_live(live_ref, fetched, rows, sem):
    count = live_ref.shape[0]

    def copy(k):
        lanes = pl.ds(pl.multiple_of(k * BLK, BLK), BLK)
        return pltpu.make_async_copy(fetched.at[live_ref[k]], rows.at[:, lanes], sem)

    def start(k, _):
        copy(k).start()
        return 0

    def wait(k, _):
        copy(k).wait()
        return 0

    lax.fori_loop(0, count, start, 0)
    lax.fori_loop(0, count, wait, 0)


def pick(rows, positions):
    total = rows.shape[1]
    step = min(total, 2048)
    out = None
    for first in range(0, total, step):
        index = lax.broadcasted_iota(jnp.int32, (step, positions.shape[1]), 0) + first
        hot = jnp.where(index == positions, 1.0, 0.0).astype(BF16)
        part = jnp.dot(rows[:, first : first + step], hot, preferred_element_type=F32)
        out = part if out is None else out + part
    return out


def neg_kernel(live_ref, fetched, pos_ref, out_ref, rows, sem):
    load_live(live_ref, fetched, rows, sem)
    out_ref[...] = pick(rows, pos_ref[...]).astype(BF16)


def gather_negs(live, fetched, pos):
    width = fetched.shape[1]
    total = live.shape[0] * BLK
    return pl.pallas_call(
        neg_kernel,
        out_shape=(
            jax.ShapeDtypeStruct((width, pos.shape[1]), BF16),
            jax.ShapeDtypeStruct((width, total), BF16),
        ),
        in_specs=[smem(), anywhere(), whole()],
        out_specs=(whole(), whole()),
        scratch_shapes=[pltpu.SemaphoreType.DMA],
        compiler_params=params(4 * width * total),
        name="gather_negs",
    )(live, fetched, pos)


def edge_kernel(rows, spos, dpos, op_ref, src_ref, dst_ref, gpos_ref):
    source = pick(rows, spos[...])
    target = pick(rows, dpos[...])
    u = source * op_ref[...]
    positive = jnp.sum(u * target, axis=0, keepdims=True)
    gpos_ref[...] = -jax.nn.sigmoid(-positive)
    src_ref[...] = source.astype(BF16)
    dst_ref[...] = target.astype(BF16)


def gather_edges(rows, spos, dpos, operator, tile=512):
    width, total = rows.shape
    edges = spos.shape[1]
    lane = pl.BlockSpec((1, tile), lambda i: (0, i))
    column = pl.BlockSpec((width, tile), lambda i: (0, i))
    return pl.pallas_call(
        edge_kernel,
        grid=(edges // tile,),
        out_shape=(
            jax.ShapeDtypeStruct((width, edges), BF16),
            jax.ShapeDtypeStruct((width, edges), BF16),
            jax.ShapeDtypeStruct((1, edges), F32),
        ),
        in_specs=[whole(), lane, lane, column],
        out_specs=(column, column, lane),
        compiler_params=params(2 * width * total + 8 * MIB),
        cost_estimate=cost(4 * width * total * edges),
        name="gather_edges",
    )(rows, spos, dpos, operator)


def split(x):
    high = x.astype(BF16)
    return high, (x - high.astype(F32)).astype(BF16)


def score_kernel(groups, *refs):
    negs = refs[:groups]
    src_ref, dst_ref, op_ref, gpos_ref, gs_ref, gd_ref = refs[groups : groups + 6]
    outs = refs[groups + 6 : 2 * groups + 6]
    each = negs[0].shape[1]
    count = groups * each
    wide = jnp.concatenate([n[...] for n in negs], axis=1)
    tall = jnp.concatenate([n[...].T for n in negs], axis=0)
    operator = op_ref[...]
    u = src_ref[...].astype(F32) * operator
    u_half = u.astype(BF16)
    scores = jnp.dot(tall, u_half, preferred_element_type=F32)
    g_neg = (jax.nn.sigmoid(scores) / count).astype(BF16)
    sums = lax.dot_general(u_half, g_neg, NT, preferred_element_type=F32)
    for g in range(groups):
        outs[g][...] = sums[:, g * each : (g + 1) * each].astype(BF16)
    g_pos = gpos_ref[...]
    grad_u = g_pos * dst_ref[...].astype(F32) + jnp.dot(wide, g_neg, preferred_element_type=F32)
    gs_ref[0], gs_ref[1] = split(grad_u * operator)
    gd_ref[0], gd_ref[1] = split(g_pos * u)


def score(negs, source, target, operator, g_pos):
    groups = len(negs)
    width, each = negs[0].shape
    edges = source.shape[1]
    out = pl.pallas_call(
        functools.partial(score_kernel, groups),
        out_shape=(
            jax.ShapeDtypeStruct((2, width, edges), BF16),
            jax.ShapeDtypeStruct((2, width, edges), BF16),
            *[jax.ShapeDtypeStruct((width, each), BF16)] * groups,
        ),
        in_specs=[whole()] * (groups + 4),
        out_specs=(whole(),) * (groups + 2),
        compiler_params=params(20 * MIB),
        cost_estimate=cost(6 * width * edges * groups * each),
        name="score",
    )(*negs, source, target, operator, g_pos)
    return out[0], out[1], out[2:]


def scatter_kernel(first, gs_ref, gd_ref, spos, dpos, out_ref):
    width, edges = gs_ref.shape[1:]

    def tile(t, _):
        index = lax.broadcasted_iota(jnp.int32, (TILE, edges), 0) + (first + t * TILE)
        both = None
        for grads, pos in ((gs_ref, spos), (gd_ref, dpos)):
            hot = jnp.where(index == pos[...], 1.0, 0.0).astype(BF16)
            part = lax.dot_general(
                grads[...].reshape(2 * width, edges), hot, NT, preferred_element_type=F32
            )
            both = part if both is None else both + part
        out_ref[:, pl.ds(pl.multiple_of(t * TILE, TILE), TILE)] = both[:width] + both[width:]
        return 0

    lax.fori_loop(0, out_ref.shape[1] // TILE, tile, 0)


def scatter(first, after, grads_src, grads_dst, spos, dpos):
    width, edges = grads_src.shape[1:]
    rows = (after - first) * BLK
    return pl.pallas_call(
        functools.partial(scatter_kernel, first * BLK),
        out_shape=jax.ShapeDtypeStruct((width, rows), F32),
        in_specs=[whole(), whole(), whole(), whole()],
        out_specs=whole(),
        compiler_params=params(4 * width * rows),
        cost_estimate=cost(4 * width * rows * edges),
        name="scatter",
    )(grads_src, grads_dst, spos, dpos)


def encode(x, out_ref):
    width = x.shape[0]
    top = jnp.max(jnp.abs(x), axis=0, keepdims=True)
    power = jnp.ceil(jnp.log2(jnp.maximum(top, 1e-30)))
    code = jnp.clip(jnp.round(x * jnp.exp2(15.0 - power)), -32767.0, 32767.0)
    out_ref[:width, :] = code.astype(jnp.int32).astype(jnp.int16)
    tail = jnp.broadcast_to(power, (TAIL, x.shape[1]))
    out_ref[width:, :] = tail.astype(jnp.int32).astype(jnp.int16)


def decode(code, width):
    power = code[width:, :].astype(jnp.int32).astype(F32)[:1]
    return code[:width, :].astype(jnp.int32).astype(F32) * jnp.exp2(power - 15.0)


def pack_kernel(first, bounds, peers, rank_ref, live_ref, npos, *refs):
    chunks, grads = refs[: len(bounds)], refs[len(bounds) : len(bounds) + peers]
    outs, total, slot = refs[len(bounds) + peers : -2], refs[-2], refs[-1]
    width = slot.shape[0]
    total[:width], total[width:] = split(sum(g[...].astype(F32) for g in grads))
    seats = outs if len(outs[0].shape) == 2 else [outs[0].at[k] for k in range(outs[0].shape[0])]
    for k, out_ref in enumerate(seats):
        alive = live_ref[first + k] > 0
        rank = rank_ref[first + k]

        for chunk, (low, high) in zip(chunks, bounds):

            @pl.when(alive & (rank >= low) & (rank < high))
            def _():
                lanes = pl.ds(pl.multiple_of((rank - low) * BLK, BLK), BLK)
                slot[...] = chunk[:, lanes]

        @pl.when(alive)
        def _():
            index = lax.broadcasted_iota(jnp.int32, (BLK, npos.shape[1]), 0) + rank * BLK
            hot = jnp.where(index == npos[...], 1.0, 0.0).astype(BF16)
            both = lax.dot_general(total[...], hot, NT, preferred_element_type=F32)
            encode(slot[...] + (both[:width] + both[width:]), out_ref)

        @pl.when(jnp.logical_not(alive))
        def _():
            out_ref[...] = jnp.zeros(out_ref.shape, jnp.int16)


def pack(first, group, joined, rank, live, chunks, bounds, grad_negs, npos):
    width = chunks[0].shape[0]
    block = (width + TAIL, BLK)
    shape, outs = ((group,) + block, 1) if joined else (block, group)
    return pl.pallas_call(
        functools.partial(pack_kernel, first, tuple(bounds), len(grad_negs)),
        out_shape=(pltpu.HBM(shape, jnp.int16),) * outs,
        in_specs=[smem(), smem()] + [whole()] * (1 + len(chunks) + len(grad_negs)),
        out_specs=(pl.BlockSpec(shape, lambda: (0,) * len(shape)),) * outs,
        scratch_shapes=[
            pltpu.VMEM((2 * width, npos.shape[1]), BF16),
            pltpu.VMEM((width, BLK), F32),
        ],
        compiler_params=params(0),
        cost_estimate=cost(4 * width * BLK * BLK * group),
        name="pack",
    )(rank, live, npos, *chunks, *grad_negs)


def add_kernel(first, fresh, asked_ref, *refs):
    grad = refs[-1]
    backs = refs[: -1 if fresh else -2]
    if len(backs[0].shape) == 3:
        backs = [backs[0].at[k] for k in range(backs[0].shape[0])]
    width = grad.shape[0]
    if fresh:
        grad[...] = jnp.zeros_like(grad)
    for k, back in enumerate(backs):
        lanes = pl.ds(pl.multiple_of(asked_ref[first + k] * BLK, BLK), BLK)
        grad[:, lanes] += decode(back[...], width)


def add(first, asked, backs, grad, width, rows):
    fresh = grad is None
    extra = [] if fresh else [grad]
    return pl.pallas_call(
        functools.partial(add_kernel, first, fresh),
        out_shape=jax.ShapeDtypeStruct((width, rows), F32),
        in_specs=[smem()] + [whole()] * (len(backs) + len(extra)),
        out_specs=whole(),
        input_output_aliases={} if fresh else {len(backs) + 1: 0},
        compiler_params=params(0),
        cost_estimate=cost(width * BLK * len(backs) * 64),
        name="add",
    )(asked, *backs, *extra)


def update_kernel(first, asked_ref, *refs):
    backs = refs[:-7]
    grad, table_ref, state_ref, table_out, state_out, fresh, sems = refs[-7:]
    width, rows = grad.shape
    for k, back in enumerate(backs):
        lanes = pl.ds(pl.multiple_of(asked_ref[first + k] * BLK, BLK), BLK)
        grad[:, lanes] += decode(back[...], width)
    span = fresh.shape[1] // sems.shape[0]

    def copy(b):
        lanes = pl.ds(pl.multiple_of(b * span, span), span)
        return pltpu.make_async_copy(fresh.at[:, lanes], table_out.at[:, lanes], sems.at[b])

    for b in range(sems.shape[0]):
        for c in range(b * span, (b + 1) * span, BLK):
            lanes = slice(c, c + BLK)
            g = grad[:, lanes]
            new_state = state_ref[:, lanes] + jnp.sum(g * g, axis=0, keepdims=True) / width
            state_out[:, lanes] = new_state
            fresh[:, lanes] = table_ref[:, lanes] - 0.1 * g / (jnp.sqrt(new_state) + 1e-10)
        copy(b).start()
    for b in range(sems.shape[0]):
        copy(b).wait()


def update(first, asked, backs, grad, table, state, parts=4):
    width, rows = table.shape
    return pl.pallas_call(
        functools.partial(update_kernel, first),
        out_shape=(
            jax.ShapeDtypeStruct((width, rows), F32),
            jax.ShapeDtypeStruct((1, rows), F32),
        ),
        in_specs=[smem()] + [whole()] * (len(backs) + 3),
        out_specs=(anywhere(), whole()),
        scratch_shapes=[pltpu.VMEM((width, rows), F32), pltpu.SemaphoreType.DMA((parts,))],
        compiler_params=params(4 * width * rows),
        cost_estimate=cost(width * rows * 64),
        name="update",
    )(asked, *backs, grad, table, state)


def per_device(table, state, relations, rel_ids, block_list, src_pos, dst_pos, neg_pos):
    devices = lax.axis_size(AXES)
    named = devices // 2
    rows_dev, width = table.shape
    blocks = rows_dev // BLK
    wanted = lax.all_to_all(
        block_list.reshape(devices, 1), AXES, split_axis=0, concat_axis=0, tiled=True
    )
    asked = wanted.reshape(devices)
    outgoing = table.reshape(blocks, BLK, width).astype(BF16)[asked]
    fetched = lax.all_to_all(
        outgoing.transpose(0, 2, 1), AXES, split_axis=0, concat_axis=0, tiled=True
    )
    operator = relations[rel_ids].T

    half = devices // 2
    order = list(range(devices - 1, half - 1, -1))
    me = lax.axis_index(AXES)
    partners = jnp.concatenate(
        [me ^ jnp.array(order, jnp.int32), me // half * half + jnp.arange(half, dtype=jnp.int32)]
    )
    ids = jnp.arange(devices, dtype=jnp.int32)
    seat = partners[:, None] == ids[None, :]
    named_by = jnp.max((src_pos // BLK)[:, None] == ids[None, :], axis=0).astype(jnp.int32)
    alive = jnp.sum(jnp.where(seat, named_by[None, :], 0), axis=1)
    rank = jnp.sum(jnp.where(ids[None, :] < ids[:, None], alive[None, :], 0), axis=1)
    place = jnp.sum(jnp.where(seat, rank[:, None], 0), axis=0)
    slot = jnp.arange(named, dtype=jnp.int32)
    live = jnp.sum(
        jnp.where((rank[None, :] == slot[:, None]) & (alive[None, :] > 0), partners[None, :], 0), axis=1
    )
    asked = jnp.sum(jnp.where(seat, asked[None, :], 0), axis=1)
    steps = [0] + [named * step // STEPS[-1] for step in STEPS]
    bounds = list(zip(steps[:-1], steps[1:]))

    def compact(pos):
        where = jnp.sum(jnp.where((pos // BLK)[:, None] == ids[None, :], place[None, :], 0), axis=1)
        return (where * BLK + pos % BLK).reshape(1, -1)

    spos, dpos, npos = compact(src_pos), compact(dst_pos), compact(neg_pos)
    fetched, operator, live, rank, alive, asked, spos, dpos, npos = lax.optimization_barrier(
        (fetched, operator, live, rank, alive, asked, spos, dpos, npos)
    )

    def swap(x, shift, axis):
        count = lax.axis_size(axis)
        return lax.ppermute(x, axis, [(i, i ^ shift) for i in range(count)])

    peers = lax.axis_size("dst")
    own_negs, rows = gather_negs(live, fetched, npos)
    negs = [own_negs] + [swap(own_negs, shift, "dst") for shift in range(1, peers)]
    source, target, g_pos = gather_edges(rows, spos, dpos, operator)
    grads_src, grads_dst, part_negs = score(negs, source, target, operator, g_pos)
    own_grad = [part_negs[0]] + [swap(part_negs[shift], shift, "dst") for shift in range(1, peers)]
    def packs(first, group, joined, chunks):
        return pack(
            first, group, joined, rank, alive, chunks, bounds[: len(chunks)], own_grad, npos
        )

    lead = steps[1]
    chunks = [scatter(*bounds[0], grads_src, grads_dst, spos, dpos)]
    leaving = list(packs(0, lead, False, chunks))
    flight = [swap(x, shift, AXES) for x, shift in zip(leaving, order)]
    chunks.append(scatter(*bounds[1], grads_src, grads_dst, spos, dpos))
    leaving += packs(lead, half - lead, False, chunks)
    near = packs(half, half, True, chunks)[0]
    near, leaving, flight = lax.optimization_barrier((near, leaving, flight))
    near = lax.all_to_all(near, AXES[1:], split_axis=0, concat_axis=0, tiled=True)
    part = half // 2
    for i in range(lead, half):
        x = leaving[i]
        if i >= WINDOW:
            x, flight[i - WINDOW] = lax.optimization_barrier((x, flight[i - WINDOW]))
        if i == part + WINDOW:
            grad = add(0, asked, flight[:part], None, width, rows_dev)
            x, grad = lax.optimization_barrier((x, grad))
        flight.append(swap(x, order[i], AXES))
    grad = add(half, asked, [near], grad, width, rows_dev)
    firsts, backs = [part], flight[part:]
    new_table, new_state = update(
        firsts[-1], asked, backs, grad, table.T, state.reshape(1, rows_dev)
    )
    return (new_table.T, new_state.reshape(rows_dev))


def solution(mesh):
    across, along = mesh.devices.shape
    mesh = jax.sharding.Mesh(mesh.devices.reshape(2, across // 2, along), AXES)
    in_specs = (
        P(AXES, None),
        P(AXES),
        P(),
        P(AXES),
        P(AXES, None),
        P(AXES),
        P(AXES),
        P(AXES),
    )
    out_specs = (P(AXES, None), P(AXES))
    return jax.shard_map(
        per_device, mesh=mesh, in_specs=in_specs, out_specs=out_specs, check_vma=False
    )
```

```python
import functools

import jax
import jax.numpy as jnp
from jax import lax
from jax.experimental import pallas as pl
from jax.experimental.pallas import tpu as pltpu
from jax.sharding import PartitionSpec as P

BLK = 128
TAIL = 8
CUTS = (1, 2, 2, 2, 1)
STEPS = (3, 6, 8)
WINDOW = 5
TILE = 256
AXES = ("src", "dst")
F32 = jnp.float32
BF16 = jnp.bfloat16
NT = (((1,), (1,)), ((), ()))


def params(held):
    return pltpu.CompilerParams(vmem_limit_bytes=14 * 1024 * 1024 + held)


MIB = 1024 * 1024


def cost(flops):
    return pl.CostEstimate(flops=flops // 64, bytes_accessed=flops // 32768, transcendentals=0)


def whole():
    return pl.BlockSpec(memory_space=pltpu.VMEM)


def smem():
    return pl.BlockSpec(memory_space=pltpu.SMEM)


def anywhere():
    return pl.BlockSpec(memory_space=pl.ANY)


def select_kernel(asked_ref, blocks_ref, out_ref, sem):
    count = out_ref.shape[0]

    def copy(k):
        return pltpu.make_async_copy(blocks_ref.at[asked_ref[k, 0, 0]], out_ref.at[k], sem)

    def start(k, _):
        copy(k).start()
        return 0

    def wait(k, _):
        copy(k).wait()
        return 0

    lax.fori_loop(0, count, start, 0)
    lax.fori_loop(0, count, wait, 0)


def select(asked, blocks):
    devices = asked.shape[0]
    return pl.pallas_call(
        select_kernel,
        out_shape=jax.ShapeDtypeStruct((devices,) + blocks.shape[1:], blocks.dtype),
        in_specs=[smem(), anywhere()],
        out_specs=anywhere(),
        scratch_shapes=[pltpu.SemaphoreType.DMA],
        compiler_params=params(0),
        name="select",
    )(asked, blocks)


def load_live(live_ref, fetched, rows, sem):
    count = live_ref.shape[0]

    def copy(k):
        lanes = pl.ds(pl.multiple_of(k * BLK, BLK), BLK)
        return pltpu.make_async_copy(fetched.at[live_ref[k]], rows.at[:, lanes], sem)

    def start(k, _):
        copy(k).start()
        return 0

    def wait(k, _):
        copy(k).wait()
        return 0

    lax.fori_loop(0, count, start, 0)
    lax.fori_loop(0, count, wait, 0)


def pick(rows, positions):
    total = rows.shape[1]
    step = min(total, 2048)
    out = None
    for first in range(0, total, step):
        index = lax.broadcasted_iota(jnp.int32, (step, positions.shape[1]), 0) + first
        hot = jnp.where(index == positions, 1.0, 0.0).astype(BF16)
        part = jnp.dot(rows[:, first : first + step], hot, preferred_element_type=F32)
        out = part if out is None else out + part
    return out


def neg_kernel(live_ref, fetched, pos_ref, out_ref, rows, sem):
    load_live(live_ref, fetched, rows, sem)
    out_ref[...] = pick(rows, pos_ref[...]).astype(BF16)


def gather_negs(live, fetched, pos):
    width = fetched.shape[1]
    total = live.shape[0] * BLK
    return pl.pallas_call(
        neg_kernel,
        out_shape=(
            jax.ShapeDtypeStruct((width, pos.shape[1]), BF16),
            jax.ShapeDtypeStruct((width, total), BF16),
        ),
        in_specs=[smem(), anywhere(), whole()],
        out_specs=(whole(), whole()),
        scratch_shapes=[pltpu.SemaphoreType.DMA],
        compiler_params=params(4 * width * total),
        name="gather_negs",
    )(live, fetched, pos)


def edge_kernel(rows, spos, dpos, op_ref, src_ref, dst_ref, gpos_ref):
    source = pick(rows, spos[...])
    target = pick(rows, dpos[...])
    u = source * op_ref[...]
    positive = jnp.sum(u * target, axis=0, keepdims=True)
    gpos_ref[...] = -jax.nn.sigmoid(-positive)
    src_ref[...] = source.astype(BF16)
    dst_ref[...] = target.astype(BF16)


def gather_edges(rows, spos, dpos, operator, tile=512):
    width, total = rows.shape
    edges = spos.shape[1]
    lane = pl.BlockSpec((1, tile), lambda i: (0, i))
    column = pl.BlockSpec((width, tile), lambda i: (0, i))
    return pl.pallas_call(
        edge_kernel,
        grid=(edges // tile,),
        out_shape=(
            jax.ShapeDtypeStruct((width, edges), BF16),
            jax.ShapeDtypeStruct((width, edges), BF16),
            jax.ShapeDtypeStruct((1, edges), F32),
        ),
        in_specs=[whole(), lane, lane, column],
        out_specs=(column, column, lane),
        compiler_params=params(2 * width * total + 8 * MIB),
        cost_estimate=cost(4 * width * total * edges),
        name="gather_edges",
    )(rows, spos, dpos, operator)


def split(x):
    high = x.astype(BF16)
    return high, (x - high.astype(F32)).astype(BF16)


def score_kernel(groups, *refs):
    negs = refs[:groups]
    src_ref, dst_ref, op_ref, gpos_ref, gs_ref, gd_ref = refs[groups : groups + 6]
    outs = refs[groups + 6 : 2 * groups + 6]
    each = negs[0].shape[1]
    count = groups * each
    wide = jnp.concatenate([n[...] for n in negs], axis=1)
    tall = jnp.concatenate([n[...].T for n in negs], axis=0)
    operator = op_ref[...]
    u = src_ref[...].astype(F32) * operator
    u_half = u.astype(BF16)
    scores = jnp.dot(tall, u_half, preferred_element_type=F32)
    g_neg = (jax.nn.sigmoid(scores) / count).astype(BF16)
    sums = lax.dot_general(u_half, g_neg, NT, preferred_element_type=F32)
    for g in range(groups):
        outs[g][...] = sums[:, g * each : (g + 1) * each].astype(BF16)
    g_pos = gpos_ref[...]
    grad_u = g_pos * dst_ref[...].astype(F32) + jnp.dot(wide, g_neg, preferred_element_type=F32)
    gs_ref[0], gs_ref[1] = split(grad_u * operator)
    gd_ref[0], gd_ref[1] = split(g_pos * u)


def score(negs, source, target, operator, g_pos):
    groups = len(negs)
    width, each = negs[0].shape
    edges = source.shape[1]
    out = pl.pallas_call(
        functools.partial(score_kernel, groups),
        out_shape=(
            jax.ShapeDtypeStruct((2, width, edges), BF16),
            jax.ShapeDtypeStruct((2, width, edges), BF16),
            *[jax.ShapeDtypeStruct((width, each), BF16)] * groups,
        ),
        in_specs=[whole()] * (groups + 4),
        out_specs=(whole(),) * (groups + 2),
        compiler_params=params(20 * MIB),
        cost_estimate=cost(6 * width * edges * groups * each),
        name="score",
    )(*negs, source, target, operator, g_pos)
    return out[0], out[1], out[2:]


def scatter_kernel(first, gs_ref, gd_ref, spos, dpos, out_ref):
    width, edges = gs_ref.shape[1:]

    def tile(t, _):
        index = lax.broadcasted_iota(jnp.int32, (TILE, edges), 0) + (first + t * TILE)
        both = None
        for grads, pos in ((gs_ref, spos), (gd_ref, dpos)):
            hot = jnp.where(index == pos[...], 1.0, 0.0).astype(BF16)
            part = lax.dot_general(
                grads[...].reshape(2 * width, edges), hot, NT, preferred_element_type=F32
            )
            both = part if both is None else both + part
        out_ref[:, pl.ds(pl.multiple_of(t * TILE, TILE), TILE)] = both[:width] + both[width:]
        return 0

    lax.fori_loop(0, out_ref.shape[1] // TILE, tile, 0)


def scatter(first, after, grads_src, grads_dst, spos, dpos):
    width, edges = grads_src.shape[1:]
    rows = (after - first) * BLK
    return pl.pallas_call(
        functools.partial(scatter_kernel, first * BLK),
        out_shape=jax.ShapeDtypeStruct((width, rows), F32),
        in_specs=[whole(), whole(), whole(), whole()],
        out_specs=whole(),
        compiler_params=params(4 * width * rows),
        cost_estimate=cost(4 * width * rows * edges),
        name="scatter",
    )(grads_src, grads_dst, spos, dpos)


def encode(x, out_ref):
    width = x.shape[0]
    top = jnp.max(jnp.abs(x), axis=0, keepdims=True)
    power = jnp.ceil(jnp.log2(jnp.maximum(top, 1e-30)) + 1e-3)
    code = jnp.round(x * (jnp.exp2(-power) * 32767.0))
    out_ref[:width, :] = code.astype(jnp.int32).astype(jnp.int16)
    tail = jnp.broadcast_to(power, (TAIL, x.shape[1]))
    out_ref[width:, :] = tail.astype(jnp.int32).astype(jnp.int16)


def decode(code, width):
    power = code[width:, :].astype(jnp.int32).astype(F32)[:1]
    return code[:width, :].astype(jnp.int32).astype(F32) * (jnp.exp2(power) * (1.0 / 32767.0))


def pack_kernel(first, bounds, peers, rank_ref, live_ref, npos, *refs):
    chunks, grads = refs[: len(bounds)], refs[len(bounds) : len(bounds) + peers]
    outs, total, slot = refs[len(bounds) + peers : -2], refs[-2], refs[-1]
    width = slot.shape[0]
    total[:width], total[width:] = split(sum(g[...].astype(F32) for g in grads))
    for k, out_ref in enumerate(outs):
        alive = live_ref[first + k] > 0
        rank = rank_ref[first + k]

        for chunk, (low, high) in zip(chunks, bounds):

            @pl.when(alive & (rank >= low) & (rank < high))
            def _():
                lanes = pl.ds(pl.multiple_of((rank - low) * BLK, BLK), BLK)
                slot[...] = chunk[:, lanes]

        @pl.when(alive)
        def _():
            index = lax.broadcasted_iota(jnp.int32, (BLK, npos.shape[1]), 0) + rank * BLK
            hot = jnp.where(index == npos[...], 1.0, 0.0).astype(BF16)
            both = lax.dot_general(total[...], hot, NT, preferred_element_type=F32)
            encode(slot[...] + (both[:width] + both[width:]), out_ref)

        @pl.when(jnp.logical_not(alive))
        def _():
            out_ref[...] = jnp.zeros(out_ref.shape, jnp.int16)


def pack(first, group, rank, live, chunks, bounds, grad_negs, npos):
    width = chunks[0].shape[0]
    return pl.pallas_call(
        functools.partial(pack_kernel, first, tuple(bounds), len(grad_negs)),
        out_shape=(jax.ShapeDtypeStruct((width + TAIL, BLK), jnp.int16),) * group,
        in_specs=[smem(), smem()] + [whole()] * (1 + len(chunks) + len(grad_negs)),
        out_specs=(whole(),) * group,
        scratch_shapes=[
            pltpu.VMEM((2 * width, npos.shape[1]), BF16),
            pltpu.VMEM((width, BLK), F32),
        ],
        compiler_params=params(0),
        cost_estimate=cost(4 * width * BLK * BLK * group),
        name="pack",
    )(rank, live, npos, *chunks, *grad_negs)


def add_kernel(first, fresh, asked_ref, *refs):
    grad = refs[-1]
    backs = refs[: -1 if fresh else -2]
    width = grad.shape[0]
    if fresh:
        grad[...] = jnp.zeros_like(grad)
    for k, back in enumerate(backs):
        lanes = pl.ds(pl.multiple_of(asked_ref[first + k] * BLK, BLK), BLK)
        grad[:, lanes] += decode(back, width)


def add(first, asked, backs, grad, width, rows):
    fresh = grad is None
    extra = [] if fresh else [grad]
    return pl.pallas_call(
        functools.partial(add_kernel, first, fresh),
        out_shape=jax.ShapeDtypeStruct((width, rows), F32),
        in_specs=[smem()] + [whole()] * (len(backs) + len(extra)),
        out_specs=whole(),
        input_output_aliases={} if fresh else {len(backs) + 1: 0},
        compiler_params=params(0),
        cost_estimate=cost(width * BLK * len(backs) * 64),
        name="add",
    )(asked, *backs, *extra)


def update_kernel(first, asked_ref, *refs):
    backs = refs[:-7]
    grad, table_ref, state_ref, table_out, state_out, fresh, sems = refs[-7:]
    width, rows = grad.shape
    for k, back in enumerate(backs):
        lanes = pl.ds(pl.multiple_of(asked_ref[first + k] * BLK, BLK), BLK)
        grad[:, lanes] += decode(back, width)
    span = fresh.shape[1] // sems.shape[0]

    def copy(b):
        lanes = pl.ds(pl.multiple_of(b * span, span), span)
        return pltpu.make_async_copy(fresh.at[:, lanes], table_out.at[:, lanes], sems.at[b])

    for b in range(sems.shape[0]):
        for c in range(b * span, (b + 1) * span, BLK):
            lanes = slice(c, c + BLK)
            g = grad[:, lanes]
            new_state = state_ref[:, lanes] + jnp.sum(g * g, axis=0, keepdims=True) / width
            state_out[:, lanes] = new_state
            fresh[:, lanes] = table_ref[:, lanes] - 0.1 * g / (jnp.sqrt(new_state) + 1e-10)
        copy(b).start()
    for b in range(sems.shape[0]):
        copy(b).wait()


def update(first, asked, backs, grad, table, state, parts=4):
    width, rows = table.shape
    return pl.pallas_call(
        functools.partial(update_kernel, first),
        out_shape=(
            jax.ShapeDtypeStruct((width, rows), F32),
            jax.ShapeDtypeStruct((1, rows), F32),
        ),
        in_specs=[smem()] + [whole()] * (len(backs) + 3),
        out_specs=(anywhere(), whole()),
        scratch_shapes=[pltpu.VMEM((width, rows), F32), pltpu.SemaphoreType.DMA((parts,))],
        compiler_params=params(4 * width * rows),
        cost_estimate=cost(width * rows * 64),
        name="update",
    )(asked, *backs, grad, table, state)


def per_device(table, state, relations, rel_ids, block_list, src_pos, dst_pos, neg_pos):
    devices = lax.axis_size(AXES)
    named = devices // 2
    rows_dev, width = table.shape
    blocks = rows_dev // BLK
    wanted = lax.all_to_all(
        block_list.reshape(devices, 1, 1), AXES, split_axis=0, concat_axis=0, tiled=True
    )
    asked = wanted.reshape(devices)
    own_blocks = table.reshape(blocks, BLK, width).transpose(0, 2, 1).astype(BF16)
    outgoing = select(wanted, own_blocks)
    fetched = lax.all_to_all(outgoing, AXES, split_axis=0, concat_axis=0, tiled=True)
    operator = relations[rel_ids].T

    half = devices // 2
    far, near = list(range(devices - 1, half - 1, -1)), list(range(half - 1, -1, -1))
    lead = devices // 8
    order = far[:lead]
    for f, n in zip(far[lead:], near):
        order += [f, n]
    order += near[half - lead :]
    partners = lax.axis_index(AXES) ^ jnp.array(order, jnp.int32)
    ids = jnp.arange(devices, dtype=jnp.int32)
    seat = partners[:, None] == ids[None, :]
    named_by = jnp.max((src_pos // BLK)[:, None] == ids[None, :], axis=0).astype(jnp.int32)
    alive = jnp.sum(jnp.where(seat, named_by[None, :], 0), axis=1)
    rank = jnp.sum(jnp.where(ids[None, :] < ids[:, None], alive[None, :], 0), axis=1)
    place = jnp.sum(jnp.where(seat, rank[:, None], 0), axis=0)
    slot = jnp.arange(named, dtype=jnp.int32)
    live = jnp.sum(
        jnp.where((rank[None, :] == slot[:, None]) & (alive[None, :] > 0), partners[None, :], 0), axis=1
    )
    asked = jnp.sum(jnp.where(seat, asked[None, :], 0), axis=1)
    sizes = [cut * devices // sum(CUTS) for cut in CUTS]
    firsts = [sum(sizes[:g]) for g in range(len(sizes))]
    steps = [0] + [named * step // STEPS[-1] for step in STEPS]
    bounds = list(zip(steps[:-1], steps[1:]))

    def compact(pos):
        where = jnp.sum(jnp.where((pos // BLK)[:, None] == ids[None, :], place[None, :], 0), axis=1)
        return (where * BLK + pos % BLK).reshape(1, -1)

    spos, dpos, npos = compact(src_pos), compact(dst_pos), compact(neg_pos)
    fetched, operator, live, rank, alive, asked, spos, dpos, npos = lax.optimization_barrier(
        (fetched, operator, live, rank, alive, asked, spos, dpos, npos)
    )

    def swap(x, shift, axis):
        count = lax.axis_size(axis)
        return lax.ppermute(x, axis, [(i, i ^ shift) for i in range(count)])

    peers = lax.axis_size("dst")
    own_negs, rows = gather_negs(live, fetched, npos)
    negs = [own_negs] + [swap(own_negs, shift, "dst") for shift in range(1, peers)]
    source, target, g_pos = gather_edges(rows, spos, dpos, operator)
    grads_src, grads_dst, part_negs = score(negs, source, target, operator, g_pos)
    own_grad = [part_negs[0]] + [swap(part_negs[shift], shift, "dst") for shift in range(1, peers)]
    grad, chunks, flight, queue = None, [], [], []
    for g, (first, group) in enumerate(zip(firsts, sizes)):
        if g < len(bounds):
            edges_at = (spos, dpos)
            if g > 1:
                edges_at, flight[-group] = lax.optimization_barrier((edges_at, flight[-group]))
            chunks.append(scatter(*bounds[g], grads_src, grads_dst, *edges_at))
        packed = pack(first, group, rank, alive, chunks, bounds[: len(chunks)], own_grad, npos)
        for k, (x, shift) in enumerate(zip(packed, order[first : first + group])):
            i = first + k
            if i >= WINDOW:
                x, flight[i - WINDOW] = lax.optimization_barrier((x, flight[i - WINDOW]))
            if k == WINDOW and g > 1:
                x, grad = lax.optimization_barrier((x, grad))
            flight.append(swap(x, shift, AXES) if shift else x)
        if g:
            before = firsts[g - 1]
            grad = add(before, asked, flight[before:first], grad, width, rows_dev)
    backs = flight[firsts[-1] :]
    new_table, new_state = update(
        firsts[-1], asked, backs, grad, table.T, state.reshape(1, rows_dev)
    )
    return (new_table.T, new_state.reshape(rows_dev))


def solution(mesh):
    in_specs = (
        P(AXES, None),
        P(AXES),
        P(),
        P(AXES),
        P(AXES, None),
        P(AXES),
        P(AXES),
        P(AXES),
    )
    out_specs = (P(AXES, None), P(AXES))
    return jax.shard_map(
        per_device, mesh=mesh, in_specs=in_specs, out_specs=out_specs, check_vma=False
    )
```

```python
import functools

import jax
import jax.numpy as jnp
from jax import lax
from jax.experimental import pallas as pl
from jax.experimental.pallas import tpu as pltpu
from jax.sharding import PartitionSpec as P

BLK = 128
TAIL = 8
CUTS = (1, 2, 2, 2, 1)
STEPS = (3, 6, 8)
WINDOW = 4
TILE = 256
AXES = ("src", "dst")
F32 = jnp.float32
BF16 = jnp.bfloat16
NT = (((1,), (1,)), ((), ()))


def params(held):
    return pltpu.CompilerParams(vmem_limit_bytes=14 * 1024 * 1024 + held)


MIB = 1024 * 1024


def cost(flops):
    return pl.CostEstimate(flops=flops // 64, bytes_accessed=flops // 32768, transcendentals=0)


def whole():
    return pl.BlockSpec(memory_space=pltpu.VMEM)


def smem():
    return pl.BlockSpec(memory_space=pltpu.SMEM)


def anywhere():
    return pl.BlockSpec(memory_space=pl.ANY)


def select_kernel(asked_ref, blocks_ref, out_ref, sem):
    count = out_ref.shape[0]

    def copy(k):
        return pltpu.make_async_copy(blocks_ref.at[asked_ref[k, 0, 0]], out_ref.at[k], sem)

    def start(k, _):
        copy(k).start()
        return 0

    def wait(k, _):
        copy(k).wait()
        return 0

    lax.fori_loop(0, count, start, 0)
    lax.fori_loop(0, count, wait, 0)


def select(asked, blocks):
    devices = asked.shape[0]
    return pl.pallas_call(
        select_kernel,
        out_shape=jax.ShapeDtypeStruct((devices,) + blocks.shape[1:], blocks.dtype),
        in_specs=[smem(), anywhere()],
        out_specs=anywhere(),
        scratch_shapes=[pltpu.SemaphoreType.DMA],
        compiler_params=params(0),
        name="select",
    )(asked, blocks)


def load_live(live_ref, fetched, rows, sem):
    count = live_ref.shape[0]

    def copy(k):
        lanes = pl.ds(pl.multiple_of(k * BLK, BLK), BLK)
        return pltpu.make_async_copy(fetched.at[live_ref[k]], rows.at[:, lanes], sem)

    def start(k, _):
        copy(k).start()
        return 0

    def wait(k, _):
        copy(k).wait()
        return 0

    lax.fori_loop(0, count, start, 0)
    lax.fori_loop(0, count, wait, 0)


def pick(rows, positions):
    total = rows.shape[1]
    step = min(total, 2048)
    out = None
    for first in range(0, total, step):
        index = lax.broadcasted_iota(jnp.int32, (step, positions.shape[1]), 0) + first
        hot = jnp.where(index == positions, 1.0, 0.0).astype(BF16)
        part = jnp.dot(rows[:, first : first + step], hot, preferred_element_type=F32)
        out = part if out is None else out + part
    return out


def neg_kernel(live_ref, fetched, pos_ref, out_ref, rows, sem):
    load_live(live_ref, fetched, rows, sem)
    out_ref[...] = pick(rows, pos_ref[...]).astype(BF16)


def gather_negs(live, fetched, pos):
    width = fetched.shape[1]
    total = live.shape[0] * BLK
    return pl.pallas_call(
        neg_kernel,
        out_shape=(
            jax.ShapeDtypeStruct((width, pos.shape[1]), BF16),
            jax.ShapeDtypeStruct((width, total), BF16),
        ),
        in_specs=[smem(), anywhere(), whole()],
        out_specs=(whole(), whole()),
        scratch_shapes=[pltpu.SemaphoreType.DMA],
        compiler_params=params(4 * width * total),
        name="gather_negs",
    )(live, fetched, pos)


def edge_kernel(rows, spos, dpos, op_ref, src_ref, dst_ref, gpos_ref):
    source = pick(rows, spos[...])
    target = pick(rows, dpos[...])
    u = source * op_ref[...]
    positive = jnp.sum(u * target, axis=0, keepdims=True)
    gpos_ref[...] = -jax.nn.sigmoid(-positive)
    src_ref[...] = source.astype(BF16)
    dst_ref[...] = target.astype(BF16)


def gather_edges(rows, spos, dpos, operator, tile=512):
    width, total = rows.shape
    edges = spos.shape[1]
    lane = pl.BlockSpec((1, tile), lambda i: (0, i))
    column = pl.BlockSpec((width, tile), lambda i: (0, i))
    return pl.pallas_call(
        edge_kernel,
        grid=(edges // tile,),
        out_shape=(
            jax.ShapeDtypeStruct((width, edges), BF16),
            jax.ShapeDtypeStruct((width, edges), BF16),
            jax.ShapeDtypeStruct((1, edges), F32),
        ),
        in_specs=[whole(), lane, lane, column],
        out_specs=(column, column, lane),
        compiler_params=params(2 * width * total + 8 * MIB),
        cost_estimate=cost(4 * width * total * edges),
        name="gather_edges",
    )(rows, spos, dpos, operator)


def split(x):
    high = x.astype(BF16)
    return high, (x - high.astype(F32)).astype(BF16)


def score_kernel(groups, *refs):
    negs = refs[:groups]
    src_ref, dst_ref, op_ref, gpos_ref, gs_ref, gd_ref = refs[groups : groups + 6]
    outs = refs[groups + 6 : 2 * groups + 6]
    each = negs[0].shape[1]
    count = groups * each
    wide = jnp.concatenate([n[...] for n in negs], axis=1)
    tall = jnp.concatenate([n[...].T for n in negs], axis=0)
    operator = op_ref[...]
    u = src_ref[...].astype(F32) * operator
    u_half = u.astype(BF16)
    scores = jnp.dot(tall, u_half, preferred_element_type=F32)
    g_neg = (jax.nn.sigmoid(scores) / count).astype(BF16)
    sums = lax.dot_general(u_half, g_neg, NT, preferred_element_type=F32)
    for g in range(groups):
        outs[g][...] = sums[:, g * each : (g + 1) * each].astype(BF16)
    g_pos = gpos_ref[...]
    grad_u = g_pos * dst_ref[...].astype(F32) + jnp.dot(wide, g_neg, preferred_element_type=F32)
    gs_ref[0], gs_ref[1] = split(grad_u * operator)
    gd_ref[0], gd_ref[1] = split(g_pos * u)


def score(negs, source, target, operator, g_pos):
    groups = len(negs)
    width, each = negs[0].shape
    edges = source.shape[1]
    out = pl.pallas_call(
        functools.partial(score_kernel, groups),
        out_shape=(
            jax.ShapeDtypeStruct((2, width, edges), BF16),
            jax.ShapeDtypeStruct((2, width, edges), BF16),
            *[jax.ShapeDtypeStruct((width, each), BF16)] * groups,
        ),
        in_specs=[whole()] * (groups + 4),
        out_specs=(whole(),) * (groups + 2),
        compiler_params=params(20 * MIB),
        cost_estimate=cost(6 * width * edges * groups * each),
        name="score",
    )(*negs, source, target, operator, g_pos)
    return out[0], out[1], out[2:]


def scatter_kernel(first, gs_ref, gd_ref, spos, dpos, out_ref):
    width, edges = gs_ref.shape[1:]

    def tile(t, _):
        index = lax.broadcasted_iota(jnp.int32, (TILE, edges), 0) + (first + t * TILE)
        both = None
        for grads, pos in ((gs_ref, spos), (gd_ref, dpos)):
            hot = jnp.where(index == pos[...], 1.0, 0.0).astype(BF16)
            part = lax.dot_general(
                grads[...].reshape(2 * width, edges), hot, NT, preferred_element_type=F32
            )
            both = part if both is None else both + part
        out_ref[:, pl.ds(pl.multiple_of(t * TILE, TILE), TILE)] = both[:width] + both[width:]
        return 0

    lax.fori_loop(0, out_ref.shape[1] // TILE, tile, 0)


def scatter(first, after, grads_src, grads_dst, spos, dpos):
    width, edges = grads_src.shape[1:]
    rows = (after - first) * BLK
    return pl.pallas_call(
        functools.partial(scatter_kernel, first * BLK),
        out_shape=jax.ShapeDtypeStruct((width, rows), F32),
        in_specs=[whole(), whole(), whole(), whole()],
        out_specs=whole(),
        compiler_params=params(4 * width * rows),
        cost_estimate=cost(4 * width * rows * edges),
        name="scatter",
    )(grads_src, grads_dst, spos, dpos)


def encode(x, out_ref):
    width = x.shape[0]
    top = jnp.max(jnp.abs(x), axis=0, keepdims=True)
    power = jnp.ceil(jnp.log2(jnp.maximum(top, 1e-30)) + 1e-3)
    code = jnp.round(x * (jnp.exp2(-power) * 32767.0))
    out_ref[:width, :] = code.astype(jnp.int32).astype(jnp.int16)
    tail = jnp.broadcast_to(power, (TAIL, x.shape[1]))
    out_ref[width:, :] = tail.astype(jnp.int32).astype(jnp.int16)


def decode(code, width):
    power = code[width:, :].astype(jnp.int32).astype(F32)[:1]
    return code[:width, :].astype(jnp.int32).astype(F32) * (jnp.exp2(power) * (1.0 / 32767.0))


def pack_kernel(first, bounds, peers, rank_ref, live_ref, npos, *refs):
    chunks, grads = refs[: len(bounds)], refs[len(bounds) : len(bounds) + peers]
    outs, total, slot = refs[len(bounds) + peers : -2], refs[-2], refs[-1]
    width = slot.shape[0]
    total[:width], total[width:] = split(sum(g[...].astype(F32) for g in grads))
    seats = []
    for out in outs:
        seats += [out.at[0], out.at[1]] if len(out.shape) == 3 else [out]
    for k, out_ref in enumerate(seats):
        alive = live_ref[first + k] > 0
        rank = rank_ref[first + k]

        for chunk, (low, high) in zip(chunks, bounds):

            @pl.when(alive & (rank >= low) & (rank < high))
            def _():
                lanes = pl.ds(pl.multiple_of((rank - low) * BLK, BLK), BLK)
                slot[...] = chunk[:, lanes]

        @pl.when(alive)
        def _():
            index = lax.broadcasted_iota(jnp.int32, (BLK, npos.shape[1]), 0) + rank * BLK
            hot = jnp.where(index == npos[...], 1.0, 0.0).astype(BF16)
            both = lax.dot_general(total[...], hot, NT, preferred_element_type=F32)
            encode(slot[...] + (both[:width] + both[width:]), out_ref)

        @pl.when(jnp.logical_not(alive))
        def _():
            out_ref[...] = jnp.zeros(out_ref.shape, jnp.int16)


def pack(first, group, paired, rank, live, chunks, bounds, grad_negs, npos):
    width = chunks[0].shape[0]
    block = (width + TAIL, BLK)
    shape, outs = ((2,) + block, group // 2) if paired else (block, group)
    return pl.pallas_call(
        functools.partial(pack_kernel, first, tuple(bounds), len(grad_negs)),
        out_shape=(jax.ShapeDtypeStruct(shape, jnp.int16),) * outs,
        in_specs=[smem(), smem()] + [whole()] * (1 + len(chunks) + len(grad_negs)),
        out_specs=(whole(),) * outs,
        scratch_shapes=[
            pltpu.VMEM((2 * width, npos.shape[1]), BF16),
            pltpu.VMEM((width, BLK), F32),
        ],
        compiler_params=params(0),
        cost_estimate=cost(4 * width * BLK * BLK * group),
        name="pack",
    )(rank, live, npos, *chunks, *grad_negs)


def add_kernel(first, fresh, asked_ref, *refs):
    grad = refs[-1]
    backs = []
    for ref in refs[: -1 if fresh else -2]:
        backs.append(ref.at[0] if len(ref.shape) == 3 else ref)
    width = grad.shape[0]
    if fresh:
        grad[...] = jnp.zeros_like(grad)
    for k, back in enumerate(backs):
        lanes = pl.ds(pl.multiple_of(asked_ref[first + k] * BLK, BLK), BLK)
        grad[:, lanes] += decode(back[...], width)


def add(first, asked, backs, grad, width, rows):
    fresh = grad is None
    extra = [] if fresh else [grad]
    return pl.pallas_call(
        functools.partial(add_kernel, first, fresh),
        out_shape=jax.ShapeDtypeStruct((width, rows), F32),
        in_specs=[smem()] + [whole()] * (len(backs) + len(extra)),
        out_specs=whole(),
        input_output_aliases={} if fresh else {len(backs) + 1: 0},
        compiler_params=params(0),
        cost_estimate=cost(width * BLK * len(backs) * 64),
        name="add",
    )(asked, *backs, *extra)


def update_kernel(first, asked_ref, *refs):
    backs = refs[:-7]
    grad, table_ref, state_ref, table_out, state_out, fresh, sems = refs[-7:]
    width, rows = grad.shape
    for k, back in enumerate(backs):
        lanes = pl.ds(pl.multiple_of(asked_ref[first + k] * BLK, BLK), BLK)
        grad[:, lanes] += decode(back, width)
    span = fresh.shape[1] // sems.shape[0]

    def copy(b):
        lanes = pl.ds(pl.multiple_of(b * span, span), span)
        return pltpu.make_async_copy(fresh.at[:, lanes], table_out.at[:, lanes], sems.at[b])

    for b in range(sems.shape[0]):
        for c in range(b * span, (b + 1) * span, BLK):
            lanes = slice(c, c + BLK)
            g = grad[:, lanes]
            new_state = state_ref[:, lanes] + jnp.sum(g * g, axis=0, keepdims=True) / width
            state_out[:, lanes] = new_state
            fresh[:, lanes] = table_ref[:, lanes] - 0.1 * g / (jnp.sqrt(new_state) + 1e-10)
        copy(b).start()
    for b in range(sems.shape[0]):
        copy(b).wait()


def update(first, asked, backs, grad, table, state, parts=4):
    width, rows = table.shape
    return pl.pallas_call(
        functools.partial(update_kernel, first),
        out_shape=(
            jax.ShapeDtypeStruct((width, rows), F32),
            jax.ShapeDtypeStruct((1, rows), F32),
        ),
        in_specs=[smem()] + [whole()] * (len(backs) + 3),
        out_specs=(anywhere(), whole()),
        scratch_shapes=[pltpu.VMEM((width, rows), F32), pltpu.SemaphoreType.DMA((parts,))],
        compiler_params=params(4 * width * rows),
        cost_estimate=cost(width * rows * 64),
        name="update",
    )(asked, *backs, grad, table, state)


def per_device(table, state, relations, rel_ids, block_list, src_pos, dst_pos, neg_pos):
    devices = lax.axis_size(AXES)
    named = devices // 2
    rows_dev, width = table.shape
    blocks = rows_dev // BLK
    wanted = lax.all_to_all(
        block_list.reshape(devices, 1, 1), AXES, split_axis=0, concat_axis=0, tiled=True
    )
    asked = wanted.reshape(devices)
    own_blocks = table.reshape(blocks, BLK, width).transpose(0, 2, 1).astype(BF16)
    outgoing = select(wanted, own_blocks)
    fetched = lax.all_to_all(outgoing, AXES, split_axis=0, concat_axis=0, tiled=True)
    operator = relations[rel_ids].T

    pairs = devices // 2
    far, near = list(range(pairs - 1, pairs // 2 - 1, -1)), list(range(pairs // 2 - 1, -1, -1))
    lead = pairs // sum(CUTS)
    chips = far[:lead]
    for f, n in zip(far[lead:], near):
        chips += [f, n]
    chips += near[len(far) - lead :]
    order = [2 * chip + side for chip in chips for side in range(2)]
    partners = lax.axis_index(AXES) ^ jnp.array(order, jnp.int32)
    ids = jnp.arange(devices, dtype=jnp.int32)
    seat = partners[:, None] == ids[None, :]
    named_by = jnp.max((src_pos // BLK)[:, None] == ids[None, :], axis=0).astype(jnp.int32)
    alive = jnp.sum(jnp.where(seat, named_by[None, :], 0), axis=1)
    rank = jnp.sum(jnp.where(ids[None, :] < ids[:, None], alive[None, :], 0), axis=1)
    place = jnp.sum(jnp.where(seat, rank[:, None], 0), axis=0)
    slot = jnp.arange(named, dtype=jnp.int32)
    live = jnp.sum(
        jnp.where((rank[None, :] == slot[:, None]) & (alive[None, :] > 0), partners[None, :], 0), axis=1
    )
    asked = jnp.sum(jnp.where(seat, asked[None, :], 0), axis=1)
    sizes = [cut * devices // sum(CUTS) for cut in CUTS]
    firsts = [sum(sizes[:g]) for g in range(len(sizes))]
    steps = [0] + [named * step // STEPS[-1] for step in STEPS]
    bounds = list(zip(steps[:-1], steps[1:]))

    def compact(pos):
        where = jnp.sum(jnp.where((pos // BLK)[:, None] == ids[None, :], place[None, :], 0), axis=1)
        return (where * BLK + pos % BLK).reshape(1, -1)

    spos, dpos, npos = compact(src_pos), compact(dst_pos), compact(neg_pos)
    fetched, operator, live, rank, alive, asked, spos, dpos, npos = lax.optimization_barrier(
        (fetched, operator, live, rank, alive, asked, spos, dpos, npos)
    )

    def swap(x, shift, axis):
        count = lax.axis_size(axis)
        return lax.ppermute(x, axis, [(i, i ^ shift) for i in range(count)])

    peers = lax.axis_size("dst")
    own_negs, rows = gather_negs(live, fetched, npos)
    negs = [own_negs] + [swap(own_negs, shift, "dst") for shift in range(1, peers)]
    source, target, g_pos = gather_edges(rows, spos, dpos, operator)
    grads_src, grads_dst, part_negs = score(negs, source, target, operator, g_pos)
    own_grad = [part_negs[0]] + [swap(part_negs[shift], shift, "dst") for shift in range(1, peers)]
    grad, chunks, flight, arrived = None, [], [], []
    for g, (first, group) in enumerate(zip(firsts, sizes)):
        last = g == len(sizes) - 1
        if g < len(bounds):
            edges_at = (spos, dpos)
            if g > 1:
                edges_at, flight[-2] = lax.optimization_barrier((edges_at, flight[-2]))
            chunks.append(scatter(*bounds[g], grads_src, grads_dst, *edges_at))
        packed = pack(
            first, group, not last, rank, alive, chunks, bounds[: len(chunks)], own_grad, npos
        )
        shifts = order[first : first + group : 1 if last else 2]
        for k, (x, shift) in enumerate(zip(packed, shifts)):
            i = len(flight)
            if i >= WINDOW:
                x, flight[i - WINDOW] = lax.optimization_barrier((x, flight[i - WINDOW]))
            if k == len(shifts) // 2 and g > 1:
                x, grad = lax.optimization_barrier((x, grad))
            flight.append(swap(x, shift, AXES) if shift else x)
        if g:
            grad = add(firsts[g - 1], asked, arrived, grad, width, rows_dev)
        arrived = []
        for x in flight[-len(shifts) :]:
            arrived += [x] if last else [x, swap(x[1], 1, AXES)]
    new_table, new_state = update(
        firsts[-1], asked, arrived, grad, table.T, state.reshape(1, rows_dev)
    )
    return (new_table.T, new_state.reshape(rows_dev))


def solution(mesh):
    in_specs = (
        P(AXES, None),
        P(AXES),
        P(),
        P(AXES),
        P(AXES, None),
        P(AXES),
        P(AXES),
        P(AXES),
    )
    out_specs = (P(AXES, None), P(AXES))
    return jax.shard_map(
        per_device, mesh=mesh, in_specs=in_specs, out_specs=out_specs, check_vma=False
    )
```

```python
import functools

import jax
import jax.numpy as jnp
from jax import lax
from jax.experimental import pallas as pl
from jax.experimental.pallas import tpu as pltpu
from jax.sharding import PartitionSpec as P

BLK = 128
TAIL = 8
CUTS = (1, 2, 2, 2, 1)
STEPS = (3, 6, 8)
WINDOW = 5
TILE = 256
AXES = ("src", "dst")
F32 = jnp.float32
BF16 = jnp.bfloat16
NT = (((1,), (1,)), ((), ()))


def params(held):
    return pltpu.CompilerParams(vmem_limit_bytes=14 * 1024 * 1024 + held)


MIB = 1024 * 1024


def cost(flops):
    return pl.CostEstimate(flops=flops // 64, bytes_accessed=flops // 32768, transcendentals=0)


def whole():
    return pl.BlockSpec(memory_space=pltpu.VMEM)


def smem():
    return pl.BlockSpec(memory_space=pltpu.SMEM)


def anywhere():
    return pl.BlockSpec(memory_space=pl.ANY)


def select_kernel(asked_ref, blocks_ref, out_ref, sem):
    count = out_ref.shape[0]

    def copy(k):
        return pltpu.make_async_copy(blocks_ref.at[asked_ref[k, 0, 0]], out_ref.at[k], sem)

    def start(k, _):
        copy(k).start()
        return 0

    def wait(k, _):
        copy(k).wait()
        return 0

    lax.fori_loop(0, count, start, 0)
    lax.fori_loop(0, count, wait, 0)


def select(asked, blocks):
    devices = asked.shape[0]
    return pl.pallas_call(
        select_kernel,
        out_shape=jax.ShapeDtypeStruct((devices,) + blocks.shape[1:], blocks.dtype),
        in_specs=[smem(), anywhere()],
        out_specs=anywhere(),
        scratch_shapes=[pltpu.SemaphoreType.DMA],
        compiler_params=params(0),
        name="select",
    )(asked, blocks)


def load_live(live_ref, fetched, rows, sem):
    count = live_ref.shape[0]

    def copy(k):
        lanes = pl.ds(pl.multiple_of(k * BLK, BLK), BLK)
        return pltpu.make_async_copy(fetched.at[live_ref[k]], rows.at[:, lanes], sem)

    def start(k, _):
        copy(k).start()
        return 0

    def wait(k, _):
        copy(k).wait()
        return 0

    lax.fori_loop(0, count, start, 0)
    lax.fori_loop(0, count, wait, 0)


def pick(rows, positions):
    total = rows.shape[1]
    step = min(total, 2048)
    out = None
    for first in range(0, total, step):
        index = lax.broadcasted_iota(jnp.int32, (step, positions.shape[1]), 0) + first
        hot = jnp.where(index == positions, 1.0, 0.0).astype(BF16)
        part = jnp.dot(rows[:, first : first + step], hot, preferred_element_type=F32)
        out = part if out is None else out + part
    return out


def neg_kernel(live_ref, fetched, pos_ref, out_ref, rows, sem):
    load_live(live_ref, fetched, rows, sem)
    out_ref[...] = pick(rows, pos_ref[...]).astype(BF16)


def gather_negs(live, fetched, pos):
    width = fetched.shape[1]
    total = live.shape[0] * BLK
    return pl.pallas_call(
        neg_kernel,
        out_shape=(
            jax.ShapeDtypeStruct((width, pos.shape[1]), BF16),
            jax.ShapeDtypeStruct((width, total), BF16),
        ),
        in_specs=[smem(), anywhere(), whole()],
        out_specs=(whole(), whole()),
        scratch_shapes=[pltpu.SemaphoreType.DMA],
        compiler_params=params(4 * width * total),
        name="gather_negs",
    )(live, fetched, pos)


def edge_kernel(rows, spos, dpos, op_ref, src_ref, dst_ref, gpos_ref):
    source = pick(rows, spos[...])
    target = pick(rows, dpos[...])
    u = source * op_ref[...]
    positive = jnp.sum(u * target, axis=0, keepdims=True)
    gpos_ref[...] = -jax.nn.sigmoid(-positive)
    src_ref[...] = source.astype(BF16)
    dst_ref[...] = target.astype(BF16)


def gather_edges(rows, spos, dpos, operator, tile=1024):
    width, total = rows.shape
    edges = spos.shape[1]
    lane = pl.BlockSpec((1, tile), lambda i: (0, i))
    column = pl.BlockSpec((width, tile), lambda i: (0, i))
    return pl.pallas_call(
        edge_kernel,
        grid=(edges // tile,),
        out_shape=(
            jax.ShapeDtypeStruct((width, edges), BF16),
            jax.ShapeDtypeStruct((width, edges), BF16),
            jax.ShapeDtypeStruct((1, edges), F32),
        ),
        in_specs=[whole(), lane, lane, column],
        out_specs=(column, column, lane),
        compiler_params=params(2 * width * total + 8 * MIB),
        cost_estimate=cost(4 * width * total * edges),
        name="gather_edges",
    )(rows, spos, dpos, operator)


def split(x):
    high = x.astype(BF16)
    return high, (x - high.astype(F32)).astype(BF16)


def score_kernel(groups, *refs):
    negs = refs[:groups]
    src_ref, dst_ref, op_ref, gpos_ref, gs_ref, gd_ref = refs[groups : groups + 6]
    outs = refs[groups + 6 : 2 * groups + 6]
    each = negs[0].shape[1]
    count = groups * each
    wide = jnp.concatenate([n[...] for n in negs], axis=1)
    tall = jnp.concatenate([n[...].T for n in negs], axis=0)
    operator = op_ref[...]
    u = src_ref[...].astype(F32) * operator
    u_half = u.astype(BF16)
    scores = jnp.dot(tall, u_half, preferred_element_type=F32)
    g_neg = (jax.nn.sigmoid(scores) * (1.0 / count)).astype(BF16)
    sums = lax.dot_general(u_half, g_neg, NT, preferred_element_type=F32)
    for g in range(groups):
        outs[g][...] = sums[:, g * each : (g + 1) * each].astype(BF16)
    g_pos = gpos_ref[...]
    grad_u = g_pos * dst_ref[...].astype(F32) + jnp.dot(wide, g_neg, preferred_element_type=F32)
    gs_ref[0], gs_ref[1] = split(grad_u * operator)
    gd_ref[0], gd_ref[1] = split(g_pos * u)


def score(negs, source, target, operator, g_pos):
    groups = len(negs)
    width, each = negs[0].shape
    edges = source.shape[1]
    out = pl.pallas_call(
        functools.partial(score_kernel, groups),
        out_shape=(
            jax.ShapeDtypeStruct((2, width, edges), BF16),
            jax.ShapeDtypeStruct((2, width, edges), BF16),
            *[jax.ShapeDtypeStruct((width, each), BF16)] * groups,
        ),
        in_specs=[whole()] * (groups + 4),
        out_specs=(whole(),) * (groups + 2),
        compiler_params=params(20 * MIB),
        cost_estimate=cost(6 * width * edges * groups * each),
        name="score",
    )(*negs, source, target, operator, g_pos)
    return out[0], out[1], out[2:]


def scatter_kernel(first, gs_ref, gd_ref, spos, dpos, out_ref):
    width, edges = gs_ref.shape[1:]

    def tile(t, _):
        index = lax.broadcasted_iota(jnp.int32, (TILE, edges), 0) + (first + t * TILE)
        both = None
        for grads, pos in ((gs_ref, spos), (gd_ref, dpos)):
            hot = jnp.where(index == pos[...], 1.0, 0.0).astype(BF16)
            part = lax.dot_general(
                grads[...].reshape(2 * width, edges), hot, NT, preferred_element_type=F32
            )
            both = part if both is None else both + part
        out_ref[:, pl.ds(pl.multiple_of(t * TILE, TILE), TILE)] = both[:width] + both[width:]
        return 0

    lax.fori_loop(0, out_ref.shape[1] // TILE, tile, 0)


def scatter(first, after, grads_src, grads_dst, spos, dpos):
    width, edges = grads_src.shape[1:]
    rows = (after - first) * BLK
    return pl.pallas_call(
        functools.partial(scatter_kernel, first * BLK),
        out_shape=jax.ShapeDtypeStruct((width, rows), F32),
        in_specs=[whole(), whole(), whole(), whole()],
        out_specs=whole(),
        compiler_params=params(4 * width * rows),
        cost_estimate=cost(4 * width * rows * edges),
        name="scatter",
    )(grads_src, grads_dst, spos, dpos)


def encode(x, out_ref):
    width = x.shape[0]
    top = jnp.max(jnp.abs(x), axis=0, keepdims=True)
    power = jnp.ceil(jnp.log2(jnp.maximum(top, 1e-30)) + 1e-3)
    code = jnp.round(x * (jnp.exp2(-power) * 32767.0))
    out_ref[:width, :] = code.astype(jnp.int32).astype(jnp.int16)
    tail = jnp.broadcast_to(power, (TAIL, x.shape[1]))
    out_ref[width:, :] = tail.astype(jnp.int32).astype(jnp.int16)


def decode(code, width):
    power = code[width:, :].astype(jnp.int32).astype(F32)[:1]
    return code[:width, :].astype(jnp.int32).astype(F32) * (jnp.exp2(power) * (1.0 / 32767.0))


def pack_kernel(first, bounds, peers, rank_ref, live_ref, npos, *refs):
    chunks, grads = refs[: len(bounds)], refs[len(bounds) : len(bounds) + peers]
    outs, total, slot = refs[len(bounds) + peers : -2], refs[-2], refs[-1]
    width = slot.shape[0]
    total[:width], total[width:] = split(sum(g[...].astype(F32) for g in grads))
    for k, out_ref in enumerate(outs):
        alive = live_ref[first + k] > 0
        rank = rank_ref[first + k]

        for chunk, (low, high) in zip(chunks, bounds):

            @pl.when(alive & (rank >= low) & (rank < high))
            def _():
                lanes = pl.ds(pl.multiple_of((rank - low) * BLK, BLK), BLK)
                slot[...] = chunk[:, lanes]

        @pl.when(alive)
        def _():
            index = lax.broadcasted_iota(jnp.int32, (BLK, npos.shape[1]), 0) + rank * BLK
            hot = jnp.where(index == npos[...], 1.0, 0.0).astype(BF16)
            both = lax.dot_general(total[...], hot, NT, preferred_element_type=F32)
            encode(slot[...] + (both[:width] + both[width:]), out_ref)

        @pl.when(jnp.logical_not(alive))
        def _():
            out_ref[...] = jnp.zeros(out_ref.shape, jnp.int16)


def pack(first, group, rank, live, chunks, bounds, grad_negs, npos):
    width = chunks[0].shape[0]
    return pl.pallas_call(
        functools.partial(pack_kernel, first, tuple(bounds), len(grad_negs)),
        out_shape=(jax.ShapeDtypeStruct((width + TAIL, BLK), jnp.int16),) * group,
        in_specs=[smem(), smem()] + [whole()] * (1 + len(chunks) + len(grad_negs)),
        out_specs=(whole(),) * group,
        scratch_shapes=[
            pltpu.VMEM((2 * width, npos.shape[1]), BF16),
            pltpu.VMEM((width, BLK), F32),
        ],
        compiler_params=params(0),
        cost_estimate=cost(4 * width * BLK * BLK * group),
        name="pack",
    )(rank, live, npos, *chunks, *grad_negs)


def add_kernel(first, fresh, asked_ref, *refs):
    grad = refs[-1]
    backs = refs[: -1 if fresh else -2]
    width = grad.shape[0]
    if fresh:
        grad[...] = jnp.zeros_like(grad)
    for k, back in enumerate(backs):
        lanes = pl.ds(pl.multiple_of(asked_ref[first + k] * BLK, BLK), BLK)
        grad[:, lanes] += decode(back, width)


def add(first, asked, backs, grad, width, rows):
    fresh = grad is None
    extra = [] if fresh else [grad]
    return pl.pallas_call(
        functools.partial(add_kernel, first, fresh),
        out_shape=jax.ShapeDtypeStruct((width, rows), F32),
        in_specs=[smem()] + [whole()] * (len(backs) + len(extra)),
        out_specs=whole(),
        input_output_aliases={} if fresh else {len(backs) + 1: 0},
        compiler_params=params(0),
        cost_estimate=cost(width * BLK * len(backs) * 64),
        name="add",
    )(asked, *backs, *extra)


def update_kernel(first, asked_ref, *refs):
    backs = refs[:-7]
    grad, table_ref, state_ref, table_out, state_out, fresh, sems = refs[-7:]
    width, rows = grad.shape
    for k, back in enumerate(backs):
        lanes = pl.ds(pl.multiple_of(asked_ref[first + k] * BLK, BLK), BLK)
        grad[:, lanes] += decode(back, width)
    span = fresh.shape[1] // sems.shape[0]

    def copy(b):
        lanes = pl.ds(pl.multiple_of(b * span, span), span)
        return pltpu.make_async_copy(fresh.at[:, lanes], table_out.at[:, lanes], sems.at[b])

    for b in range(sems.shape[0]):
        for c in range(b * span, (b + 1) * span, BLK):
            lanes = slice(c, c + BLK)
            g = grad[:, lanes]
            new_state = state_ref[:, lanes] + jnp.sum(g * g, axis=0, keepdims=True) / width
            state_out[:, lanes] = new_state
            fresh[:, lanes] = table_ref[:, lanes] - g * (0.1 / (jnp.sqrt(new_state) + 1e-10))
        copy(b).start()
    for b in range(sems.shape[0]):
        copy(b).wait()


def update(first, asked, backs, grad, table, state, parts=4):
    width, rows = table.shape
    return pl.pallas_call(
        functools.partial(update_kernel, first),
        out_shape=(
            jax.ShapeDtypeStruct((width, rows), F32),
            jax.ShapeDtypeStruct((1, rows), F32),
        ),
        in_specs=[smem()] + [whole()] * (len(backs) + 3),
        out_specs=(anywhere(), whole()),
        scratch_shapes=[pltpu.VMEM((width, rows), F32), pltpu.SemaphoreType.DMA((parts,))],
        compiler_params=params(4 * width * rows),
        cost_estimate=cost(width * rows * 64),
        name="update",
    )(asked, *backs, grad, table, state)


def per_device(table, state, relations, rel_ids, block_list, src_pos, dst_pos, neg_pos):
    devices = lax.axis_size(AXES)
    named = devices // 2
    rows_dev, width = table.shape
    blocks = rows_dev // BLK
    wanted = lax.all_to_all(
        block_list.reshape(devices, 1, 1), AXES, split_axis=0, concat_axis=0, tiled=True
    )
    asked = wanted.reshape(devices)
    own_blocks = table.reshape(blocks, BLK, width).transpose(0, 2, 1).astype(BF16)
    outgoing = select(wanted, own_blocks)
    fetched = lax.all_to_all(outgoing, AXES, split_axis=0, concat_axis=0, tiled=True)
    operator = relations[rel_ids].T

    half = devices // 2
    far, near = list(range(devices - 1, half - 1, -1)), list(range(half - 1, -1, -1))
    lead = devices // 8
    order = far[:lead]
    for f, n in zip(far[lead:], near):
        order += [f, n]
    order += near[half - lead :]
    partners = lax.axis_index(AXES) ^ jnp.array(order, jnp.int32)
    ids = jnp.arange(devices, dtype=jnp.int32)
    seat = partners[:, None] == ids[None, :]
    named_by = jnp.max((src_pos // BLK)[:, None] == ids[None, :], axis=0).astype(jnp.int32)
    alive = jnp.sum(jnp.where(seat, named_by[None, :], 0), axis=1)
    rank = jnp.sum(jnp.where(ids[None, :] < ids[:, None], alive[None, :], 0), axis=1)
    place = jnp.sum(jnp.where(seat, rank[:, None], 0), axis=0)
    slot = jnp.arange(named, dtype=jnp.int32)
    live = jnp.sum(
        jnp.where((rank[None, :] == slot[:, None]) & (alive[None, :] > 0), partners[None, :], 0), axis=1
    )
    asked = jnp.sum(jnp.where(seat, asked[None, :], 0), axis=1)
    sizes = [cut * devices // sum(CUTS) for cut in CUTS]
    firsts = [sum(sizes[:g]) for g in range(len(sizes))]
    steps = [0] + [named * step // STEPS[-1] for step in STEPS]
    bounds = list(zip(steps[:-1], steps[1:]))

    def compact(pos):
        where = jnp.sum(jnp.where((pos // BLK)[:, None] == ids[None, :], place[None, :], 0), axis=1)
        return (where * BLK + pos % BLK).reshape(1, -1)

    spos, dpos, npos = compact(src_pos), compact(dst_pos), compact(neg_pos)
    fetched, operator, live, rank, alive, asked, spos, dpos, npos = lax.optimization_barrier(
        (fetched, operator, live, rank, alive, asked, spos, dpos, npos)
    )

    def swap(x, shift, axis):
        count = lax.axis_size(axis)
        return lax.ppermute(x, axis, [(i, i ^ shift) for i in range(count)])

    peers = lax.axis_size("dst")
    own_negs, rows = gather_negs(live, fetched, npos)
    negs = [own_negs] + [swap(own_negs, shift, "dst") for shift in range(1, peers)]
    source, target, g_pos = gather_edges(rows, spos, dpos, operator)
    grads_src, grads_dst, part_negs = score(negs, source, target, operator, g_pos)
    own_grad = [part_negs[0]] + [swap(part_negs[shift], shift, "dst") for shift in range(1, peers)]
    grad, chunks, flight, queue = None, [], [], []
    for g, (first, group) in enumerate(zip(firsts, sizes)):
        if g < len(bounds):
            edges_at = (spos, dpos)
            if g > 1:
                edges_at, flight[-group] = lax.optimization_barrier((edges_at, flight[-group]))
            chunks.append(scatter(*bounds[g], grads_src, grads_dst, *edges_at))
        packed = pack(first, group, rank, alive, chunks, bounds[: len(chunks)], own_grad, npos)
        for k, (x, shift) in enumerate(zip(packed, order[first : first + group])):
            i = first + k
            if i >= WINDOW:
                x, flight[i - WINDOW] = lax.optimization_barrier((x, flight[i - WINDOW]))
            if k == WINDOW and g > 1:
                x, grad = lax.optimization_barrier((x, grad))
            flight.append(swap(x, shift, AXES) if shift else x)
        if g:
            before = firsts[g - 1]
            grad = add(before, asked, flight[before:first], grad, width, rows_dev)
    backs = flight[firsts[-1] :]
    new_table, new_state = update(
        firsts[-1], asked, backs, grad, table.T, state.reshape(1, rows_dev)
    )
    return (new_table.T, new_state.reshape(rows_dev))


def solution(mesh):
    in_specs = (
        P(AXES, None),
        P(AXES),
        P(),
        P(AXES),
        P(AXES, None),
        P(AXES),
        P(AXES),
        P(AXES),
    )
    out_specs = (P(AXES, None), P(AXES))
    return jax.shard_map(
        per_device, mesh=mesh, in_specs=in_specs, out_specs=out_specs, check_vma=False
    )
```

```python
import functools

import jax
import jax.numpy as jnp
from jax import lax
from jax.experimental import pallas as pl
from jax.experimental.pallas import tpu as pltpu
from jax.sharding import PartitionSpec as P

BLK = 128
TAIL = 8
CUTS = (3, 3, 4, 4, 2)
STEPS = (3, 6, 8)
WINDOW = 5
TILE = 256
AXES = ("src", "dst")
F32 = jnp.float32
BF16 = jnp.bfloat16
NT = (((1,), (1,)), ((), ()))


def params(held):
    return pltpu.CompilerParams(vmem_limit_bytes=14 * 1024 * 1024 + held)


MIB = 1024 * 1024


def cost(flops):
    return pl.CostEstimate(flops=flops // 64, bytes_accessed=flops // 32768, transcendentals=0)


def whole():
    return pl.BlockSpec(memory_space=pltpu.VMEM)


def smem():
    return pl.BlockSpec(memory_space=pltpu.SMEM)


def anywhere():
    return pl.BlockSpec(memory_space=pl.ANY)


def select_kernel(asked_ref, blocks_ref, out_ref, sem):
    count = out_ref.shape[0]

    def copy(k):
        return pltpu.make_async_copy(blocks_ref.at[asked_ref[k, 0, 0]], out_ref.at[k], sem)

    def start(k, _):
        copy(k).start()
        return 0

    def wait(k, _):
        copy(k).wait()
        return 0

    lax.fori_loop(0, count, start, 0)
    lax.fori_loop(0, count, wait, 0)


def select(asked, blocks):
    devices = asked.shape[0]
    return pl.pallas_call(
        select_kernel,
        out_shape=jax.ShapeDtypeStruct((devices,) + blocks.shape[1:], blocks.dtype),
        in_specs=[smem(), anywhere()],
        out_specs=anywhere(),
        scratch_shapes=[pltpu.SemaphoreType.DMA],
        compiler_params=params(0),
        name="select",
    )(asked, blocks)


def load_live(live_ref, fetched, rows, sem):
    count = live_ref.shape[0]

    def copy(k):
        lanes = pl.ds(pl.multiple_of(k * BLK, BLK), BLK)
        return pltpu.make_async_copy(fetched.at[live_ref[k]], rows.at[:, lanes], sem)

    def start(k, _):
        copy(k).start()
        return 0

    def wait(k, _):
        copy(k).wait()
        return 0

    lax.fori_loop(0, count, start, 0)
    lax.fori_loop(0, count, wait, 0)


def pick(rows, positions):
    total = rows.shape[1]
    step = min(total, 2048)
    out = None
    for first in range(0, total, step):
        index = lax.broadcasted_iota(jnp.int32, (step, positions.shape[1]), 0) + first
        hot = jnp.where(index == positions, 1.0, 0.0).astype(BF16)
        part = jnp.dot(rows[:, first : first + step], hot, preferred_element_type=F32)
        out = part if out is None else out + part
    return out


def neg_kernel(live_ref, fetched, pos_ref, out_ref, rows, sem):
    load_live(live_ref, fetched, rows, sem)
    out_ref[...] = pick(rows, pos_ref[...]).astype(BF16)


def gather_negs(live, fetched, pos):
    width = fetched.shape[1]
    total = live.shape[0] * BLK
    return pl.pallas_call(
        neg_kernel,
        out_shape=(
            jax.ShapeDtypeStruct((width, pos.shape[1]), BF16),
            jax.ShapeDtypeStruct((width, total), BF16),
        ),
        in_specs=[smem(), anywhere(), whole()],
        out_specs=(whole(), whole()),
        scratch_shapes=[pltpu.SemaphoreType.DMA],
        compiler_params=params(4 * width * total),
        name="gather_negs",
    )(live, fetched, pos)


def edge_kernel(rows, spos, dpos, op_ref, src_ref, dst_ref, gpos_ref):
    source = pick(rows, spos[...])
    target = pick(rows, dpos[...])
    u = source * op_ref[...]
    positive = jnp.sum(u * target, axis=0, keepdims=True)
    gpos_ref[...] = -jax.nn.sigmoid(-positive)
    src_ref[...] = source.astype(BF16)
    dst_ref[...] = target.astype(BF16)


def gather_edges(rows, spos, dpos, operator, tile=1024):
    width, total = rows.shape
    edges = spos.shape[1]
    lane = pl.BlockSpec((1, tile), lambda i: (0, i))
    column = pl.BlockSpec((width, tile), lambda i: (0, i))
    return pl.pallas_call(
        edge_kernel,
        grid=(edges // tile,),
        out_shape=(
            jax.ShapeDtypeStruct((width, edges), BF16),
            jax.ShapeDtypeStruct((width, edges), BF16),
            jax.ShapeDtypeStruct((1, edges), F32),
        ),
        in_specs=[whole(), lane, lane, column],
        out_specs=(column, column, lane),
        compiler_params=params(2 * width * total + 8 * MIB),
        cost_estimate=cost(4 * width * total * edges),
        name="gather_edges",
    )(rows, spos, dpos, operator)


def split(x):
    high = x.astype(BF16)
    return high, (x - high.astype(F32)).astype(BF16)


def score_kernel(groups, *refs):
    negs = refs[:groups]
    src_ref, dst_ref, op_ref, gpos_ref, gs_ref, gd_ref = refs[groups : groups + 6]
    outs = refs[groups + 6 : 2 * groups + 6]
    each = negs[0].shape[1]
    count = groups * each
    wide = jnp.concatenate([n[...] for n in negs], axis=1)
    tall = jnp.concatenate([n[...].T for n in negs], axis=0)
    operator = op_ref[...]
    u = src_ref[...].astype(F32) * operator
    u_half = u.astype(BF16)
    scores = jnp.dot(tall, u_half, preferred_element_type=F32)
    g_neg = (jax.nn.sigmoid(scores) * (1.0 / count)).astype(BF16)
    sums = lax.dot_general(u_half, g_neg, NT, preferred_element_type=F32)
    for g in range(groups):
        outs[g][...] = sums[:, g * each : (g + 1) * each].astype(BF16)
    g_pos = gpos_ref[...]
    grad_u = g_pos * dst_ref[...].astype(F32) + jnp.dot(wide, g_neg, preferred_element_type=F32)
    gs_ref[0], gs_ref[1] = split(grad_u * operator)
    gd_ref[0], gd_ref[1] = split(g_pos * u)


def score(negs, source, target, operator, g_pos):
    groups = len(negs)
    width, each = negs[0].shape
    edges = source.shape[1]
    out = pl.pallas_call(
        functools.partial(score_kernel, groups),
        out_shape=(
            jax.ShapeDtypeStruct((2, width, edges), BF16),
            jax.ShapeDtypeStruct((2, width, edges), BF16),
            *[jax.ShapeDtypeStruct((width, each), BF16)] * groups,
        ),
        in_specs=[whole()] * (groups + 4),
        out_specs=(whole(),) * (groups + 2),
        compiler_params=params(20 * MIB),
        cost_estimate=cost(6 * width * edges * groups * each),
        name="score",
    )(*negs, source, target, operator, g_pos)
    return out[0], out[1], out[2:]


def scatter_kernel(first, gs_ref, gd_ref, spos, dpos, out_ref):
    width, edges = gs_ref.shape[1:]

    def tile(t, _):
        index = lax.broadcasted_iota(jnp.int32, (TILE, edges), 0) + (first + t * TILE)
        both = None
        for grads, pos in ((gs_ref, spos), (gd_ref, dpos)):
            hot = jnp.where(index == pos[...], 1.0, 0.0).astype(BF16)
            part = lax.dot_general(
                grads[...].reshape(2 * width, edges), hot, NT, preferred_element_type=F32
            )
            both = part if both is None else both + part
        out_ref[:, pl.ds(pl.multiple_of(t * TILE, TILE), TILE)] = both[:width] + both[width:]
        return 0

    lax.fori_loop(0, out_ref.shape[1] // TILE, tile, 0)


def scatter(first, after, grads_src, grads_dst, spos, dpos):
    width, edges = grads_src.shape[1:]
    rows = (after - first) * BLK
    return pl.pallas_call(
        functools.partial(scatter_kernel, first * BLK),
        out_shape=jax.ShapeDtypeStruct((width, rows), F32),
        in_specs=[whole(), whole(), whole(), whole()],
        out_specs=whole(),
        compiler_params=params(4 * width * rows),
        cost_estimate=cost(4 * width * rows * edges),
        name="scatter",
    )(grads_src, grads_dst, spos, dpos)


def encode(x, out_ref):
    width = x.shape[0]
    top = jnp.max(jnp.abs(x), axis=0, keepdims=True)
    power = jnp.ceil(jnp.log2(jnp.maximum(top, 1e-30)) + 1e-3)
    code = jnp.round(x * (jnp.exp2(-power) * 32767.0))
    out_ref[:width, :] = code.astype(jnp.int32).astype(jnp.int16)
    tail = jnp.broadcast_to(power, (TAIL, x.shape[1]))
    out_ref[width:, :] = tail.astype(jnp.int32).astype(jnp.int16)


def decode(code, width):
    power = code[width:, :].astype(jnp.int32).astype(F32)[:1]
    return code[:width, :].astype(jnp.int32).astype(F32) * (jnp.exp2(power) * (1.0 / 32767.0))


def pack_kernel(first, bounds, peers, rank_ref, live_ref, npos, *refs):
    chunks, grads = refs[: len(bounds)], refs[len(bounds) : len(bounds) + peers]
    outs, total, slot = refs[len(bounds) + peers : -2], refs[-2], refs[-1]
    total[...] = sum(g[...].astype(F32) for g in grads).astype(BF16)
    for k, out_ref in enumerate(outs):
        alive = live_ref[first + k] > 0
        rank = rank_ref[first + k]

        for chunk, (low, high) in zip(chunks, bounds):

            @pl.when(alive & (rank >= low) & (rank < high))
            def _():
                lanes = pl.ds(pl.multiple_of((rank - low) * BLK, BLK), BLK)
                slot[...] = chunk[:, lanes]

        @pl.when(alive)
        def _():
            index = lax.broadcasted_iota(jnp.int32, (BLK, npos.shape[1]), 0) + rank * BLK
            hot = jnp.where(index == npos[...], 1.0, 0.0).astype(BF16)
            part = lax.dot_general(total[...], hot, NT, preferred_element_type=F32)
            encode(slot[...] + part, out_ref)

        @pl.when(jnp.logical_not(alive))
        def _():
            out_ref[...] = jnp.zeros(out_ref.shape, jnp.int16)


def pack(first, group, rank, live, chunks, bounds, grad_negs, npos):
    width = chunks[0].shape[0]
    return pl.pallas_call(
        functools.partial(pack_kernel, first, tuple(bounds), len(grad_negs)),
        out_shape=(jax.ShapeDtypeStruct((width + TAIL, BLK), jnp.int16),) * group,
        in_specs=[smem(), smem()] + [whole()] * (1 + len(chunks) + len(grad_negs)),
        out_specs=(whole(),) * group,
        scratch_shapes=[
            pltpu.VMEM((width, npos.shape[1]), BF16),
            pltpu.VMEM((width, BLK), F32),
        ],
        compiler_params=params(0),
        cost_estimate=cost(4 * width * BLK * BLK * group),
        name="pack",
    )(rank, live, npos, *chunks, *grad_negs)


def add_kernel(first, fresh, asked_ref, *refs):
    grad = refs[-1]
    backs = refs[: -1 if fresh else -2]
    width = grad.shape[0]
    if fresh:
        grad[...] = jnp.zeros_like(grad)
    for k, back in enumerate(backs):
        lanes = pl.ds(pl.multiple_of(asked_ref[first + k] * BLK, BLK), BLK)
        grad[:, lanes] += decode(back, width)


def add(first, asked, backs, grad, width, rows):
    fresh = grad is None
    extra = [] if fresh else [grad]
    return pl.pallas_call(
        functools.partial(add_kernel, first, fresh),
        out_shape=jax.ShapeDtypeStruct((width, rows), F32),
        in_specs=[smem()] + [whole()] * (len(backs) + len(extra)),
        out_specs=whole(),
        input_output_aliases={} if fresh else {len(backs) + 1: 0},
        compiler_params=params(0),
        cost_estimate=cost(width * BLK * len(backs) * 64),
        name="add",
    )(asked, *backs, *extra)


def update_kernel(first, asked_ref, *refs):
    backs = refs[:-7]
    grad, table_ref, state_ref, table_out, state_out, fresh, sems = refs[-7:]
    width, rows = grad.shape
    for k, back in enumerate(backs):
        lanes = pl.ds(pl.multiple_of(asked_ref[first + k] * BLK, BLK), BLK)
        grad[:, lanes] += decode(back, width)
    span = fresh.shape[1] // sems.shape[0]

    def copy(b):
        lanes = pl.ds(pl.multiple_of(b * span, span), span)
        return pltpu.make_async_copy(fresh.at[:, lanes], table_out.at[:, lanes], sems.at[b])

    for b in range(sems.shape[0]):
        for c in range(b * span, (b + 1) * span, BLK):
            lanes = slice(c, c + BLK)
            g = grad[:, lanes]
            new_state = state_ref[:, lanes] + jnp.sum(g * g, axis=0, keepdims=True) / width
            state_out[:, lanes] = new_state
            fresh[:, lanes] = table_ref[:, lanes] - g * (0.1 / (jnp.sqrt(new_state) + 1e-10))
        copy(b).start()
    for b in range(sems.shape[0]):
        copy(b).wait()


def update(first, asked, backs, grad, table, state, parts=4):
    width, rows = table.shape
    return pl.pallas_call(
        functools.partial(update_kernel, first),
        out_shape=(
            jax.ShapeDtypeStruct((width, rows), F32),
            jax.ShapeDtypeStruct((1, rows), F32),
        ),
        in_specs=[smem()] + [whole()] * (len(backs) + 3),
        out_specs=(anywhere(), whole()),
        scratch_shapes=[pltpu.VMEM((width, rows), F32), pltpu.SemaphoreType.DMA((parts,))],
        compiler_params=params(4 * width * rows),
        cost_estimate=cost(width * rows * 64),
        name="update",
    )(asked, *backs, grad, table, state)


def per_device(table, state, relations, rel_ids, block_list, src_pos, dst_pos, neg_pos):
    devices = lax.axis_size(AXES)
    named = devices // 2
    rows_dev, width = table.shape
    blocks = rows_dev // BLK
    wanted = lax.all_to_all(
        block_list.reshape(devices, 1, 1), AXES, split_axis=0, concat_axis=0, tiled=True
    )
    asked = wanted.reshape(devices)
    own_blocks = table.reshape(blocks, BLK, width).transpose(0, 2, 1).astype(BF16)
    outgoing = select(wanted, own_blocks)
    fetched = lax.all_to_all(outgoing, AXES, split_axis=0, concat_axis=0, tiled=True)
    operator = relations[rel_ids].T

    half = devices // 2
    far, near = list(range(devices - 1, half - 1, -1)), list(range(half - 1, -1, -1))
    lead = devices // 8
    order = far[:lead]
    for f, n in zip(far[lead:], near):
        order += [f, n]
    order += near[half - lead :]
    partners = lax.axis_index(AXES) ^ jnp.array(order, jnp.int32)
    ids = jnp.arange(devices, dtype=jnp.int32)
    seat = partners[:, None] == ids[None, :]
    named_by = jnp.max((src_pos // BLK)[:, None] == ids[None, :], axis=0).astype(jnp.int32)
    alive = jnp.sum(jnp.where(seat, named_by[None, :], 0), axis=1)
    rank = jnp.sum(jnp.where(ids[None, :] < ids[:, None], alive[None, :], 0), axis=1)
    place = jnp.sum(jnp.where(seat, rank[:, None], 0), axis=0)
    slot = jnp.arange(named, dtype=jnp.int32)
    live = jnp.sum(
        jnp.where((rank[None, :] == slot[:, None]) & (alive[None, :] > 0), partners[None, :], 0), axis=1
    )
    asked = jnp.sum(jnp.where(seat, asked[None, :], 0), axis=1)
    sizes = [cut * devices // sum(CUTS) for cut in CUTS]
    firsts = [sum(sizes[:g]) for g in range(len(sizes))]
    steps = [0] + [named * step // STEPS[-1] for step in STEPS]
    bounds = list(zip(steps[:-1], steps[1:]))

    def compact(pos):
        where = jnp.sum(jnp.where((pos // BLK)[:, None] == ids[None, :], place[None, :], 0), axis=1)
        return (where * BLK + pos % BLK).reshape(1, -1)

    spos, dpos, npos = compact(src_pos), compact(dst_pos), compact(neg_pos)
    fetched, operator, live, rank, alive, asked, spos, dpos, npos = lax.optimization_barrier(
        (fetched, operator, live, rank, alive, asked, spos, dpos, npos)
    )

    def swap(x, shift, axis):
        count = lax.axis_size(axis)
        return lax.ppermute(x, axis, [(i, i ^ shift) for i in range(count)])

    peers = lax.axis_size("dst")
    own_negs, rows = gather_negs(live, fetched, npos)
    negs = [own_negs] + [swap(own_negs, shift, "dst") for shift in range(1, peers)]
    source, target, g_pos = gather_edges(rows, spos, dpos, operator)
    grads_src, grads_dst, part_negs = score(negs, source, target, operator, g_pos)
    own_grad = [part_negs[0]] + [swap(part_negs[shift], shift, "dst") for shift in range(1, peers)]
    grad, chunks, flight, queue = None, [], [], []
    for g, (first, group) in enumerate(zip(firsts, sizes)):
        if g < len(bounds):
            edges_at = (spos, dpos)
            if g > 1:
                edges_at, flight[-group] = lax.optimization_barrier((edges_at, flight[-group]))
            chunks.append(scatter(*bounds[g], grads_src, grads_dst, *edges_at))
        packed = pack(first, group, rank, alive, chunks, bounds[: len(chunks)], own_grad, npos)
        for k, (x, shift) in enumerate(zip(packed, order[first : first + group])):
            i = first + k
            if i >= WINDOW:
                x, flight[i - WINDOW] = lax.optimization_barrier((x, flight[i - WINDOW]))
            if k == WINDOW and g > 1:
                x, grad = lax.optimization_barrier((x, grad))
            flight.append(swap(x, shift, AXES) if shift else x)
        if g:
            before = firsts[g - 1]
            grad = add(before, asked, flight[before:first], grad, width, rows_dev)
    backs = flight[firsts[-1] :]
    new_table, new_state = update(
        firsts[-1], asked, backs, grad, table.T, state.reshape(1, rows_dev)
    )
    return (new_table.T, new_state.reshape(rows_dev))


def solution(mesh):
    in_specs = (
        P(AXES, None),
        P(AXES),
        P(),
        P(AXES),
        P(AXES, None),
        P(AXES),
        P(AXES),
        P(AXES),
    )
    out_specs = (P(AXES, None), P(AXES))
    return jax.shard_map(
        per_device, mesh=mesh, in_specs=in_specs, out_specs=out_specs, check_vma=False
    )
```

```python
import functools

import jax
import jax.numpy as jnp
from jax import lax
from jax.experimental import pallas as pl
from jax.experimental.pallas import tpu as pltpu
from jax.sharding import PartitionSpec as P

BLK = 128
TAIL = 8
CUTS = (1, 2, 2, 2, 1)
STEPS = (3, 6, 8)
WINDOW = 5
TILE = 256
AXES = ("src", "dst")
F32 = jnp.float32
BF16 = jnp.bfloat16
NT = (((1,), (1,)), ((), ()))


def params(held):
    return pltpu.CompilerParams(vmem_limit_bytes=14 * 1024 * 1024 + held)


MIB = 1024 * 1024


def cost(flops):
    return pl.CostEstimate(flops=flops // 64, bytes_accessed=flops // 32768, transcendentals=0)


def whole():
    return pl.BlockSpec(memory_space=pltpu.VMEM)


def smem():
    return pl.BlockSpec(memory_space=pltpu.SMEM)


def anywhere():
    return pl.BlockSpec(memory_space=pl.ANY)


def select_kernel(asked_ref, blocks_ref, out_ref, sem):
    count = out_ref.shape[0]

    def copy(k):
        return pltpu.make_async_copy(blocks_ref.at[asked_ref[k, 0, 0]], out_ref.at[k], sem)

    def start(k, _):
        copy(k).start()
        return 0

    def wait(k, _):
        copy(k).wait()
        return 0

    lax.fori_loop(0, count, start, 0)
    lax.fori_loop(0, count, wait, 0)


def select(asked, blocks):
    devices = asked.shape[0]
    return pl.pallas_call(
        select_kernel,
        out_shape=jax.ShapeDtypeStruct((devices,) + blocks.shape[1:], blocks.dtype),
        in_specs=[smem(), anywhere()],
        out_specs=anywhere(),
        scratch_shapes=[pltpu.SemaphoreType.DMA],
        compiler_params=params(0),
        name="select",
    )(asked, blocks)


def load_live(live_ref, fetched, rows, sem):
    count = live_ref.shape[0]

    def copy(k):
        lanes = pl.ds(pl.multiple_of(k * BLK, BLK), BLK)
        return pltpu.make_async_copy(fetched.at[live_ref[k]], rows.at[:, lanes], sem)

    def start(k, _):
        copy(k).start()
        return 0

    def wait(k, _):
        copy(k).wait()
        return 0

    lax.fori_loop(0, count, start, 0)
    lax.fori_loop(0, count, wait, 0)


def pick(rows, positions):
    total = rows.shape[1]
    step = min(total, 2048)
    out = None
    for first in range(0, total, step):
        index = lax.broadcasted_iota(jnp.int32, (step, positions.shape[1]), 0) + first
        hot = jnp.where(index == positions, 1.0, 0.0).astype(BF16)
        part = jnp.dot(rows[:, first : first + step], hot, preferred_element_type=F32)
        out = part if out is None else out + part
    return out


def neg_kernel(live_ref, fetched, pos_ref, out_ref, rows, sem):
    load_live(live_ref, fetched, rows, sem)
    out_ref[...] = pick(rows, pos_ref[...]).astype(BF16)


def gather_negs(live, fetched, pos):
    width = fetched.shape[1]
    total = live.shape[0] * BLK
    return pl.pallas_call(
        neg_kernel,
        out_shape=(
            jax.ShapeDtypeStruct((width, pos.shape[1]), BF16),
            jax.ShapeDtypeStruct((width, total), BF16),
        ),
        in_specs=[smem(), anywhere(), whole()],
        out_specs=(whole(), whole()),
        scratch_shapes=[pltpu.SemaphoreType.DMA],
        compiler_params=params(4 * width * total),
        name="gather_negs",
    )(live, fetched, pos)


def edge_kernel(rows, spos, dpos, op_ref, src_ref, dst_ref, gpos_ref):
    source = pick(rows, spos[...])
    target = pick(rows, dpos[...])
    u = source * op_ref[...]
    positive = jnp.sum(u * target, axis=0, keepdims=True)
    gpos_ref[...] = -jax.nn.sigmoid(-positive)
    src_ref[...] = source.astype(BF16)
    dst_ref[...] = target.astype(BF16)


def gather_edges(rows, spos, dpos, operator, tile=512):
    width, total = rows.shape
    edges = spos.shape[1]
    lane = pl.BlockSpec((1, tile), lambda i: (0, i))
    column = pl.BlockSpec((width, tile), lambda i: (0, i))
    return pl.pallas_call(
        edge_kernel,
        grid=(edges // tile,),
        out_shape=(
            jax.ShapeDtypeStruct((width, edges), BF16),
            jax.ShapeDtypeStruct((width, edges), BF16),
            jax.ShapeDtypeStruct((1, edges), F32),
        ),
        in_specs=[whole(), lane, lane, column],
        out_specs=(column, column, lane),
        compiler_params=params(2 * width * total + 8 * MIB),
        cost_estimate=cost(4 * width * total * edges),
        name="gather_edges",
    )(rows, spos, dpos, operator)


def split(x):
    high = x.astype(BF16)
    return high, (x - high.astype(F32)).astype(BF16)


def score_kernel(groups, *refs):
    negs = refs[:groups]
    src_ref, dst_ref, op_ref, gpos_ref, gs_ref, gd_ref = refs[groups : groups + 6]
    outs = refs[groups + 6 : 2 * groups + 6]
    each = negs[0].shape[1]
    count = groups * each
    wide = jnp.concatenate([n[...] for n in negs], axis=1)
    tall = jnp.concatenate([n[...].T for n in negs], axis=0)
    operator = op_ref[...]
    u = src_ref[...].astype(F32) * operator
    u_half = u.astype(BF16)
    scores = jnp.dot(tall, u_half, preferred_element_type=F32)
    g_neg = (jax.nn.sigmoid(scores) / count).astype(BF16)
    sums = lax.dot_general(u_half, g_neg, NT, preferred_element_type=F32)
    for g in range(groups):
        outs[g][...] = sums[:, g * each : (g + 1) * each].astype(BF16)
    g_pos = gpos_ref[...]
    grad_u = g_pos * dst_ref[...].astype(F32) + jnp.dot(wide, g_neg, preferred_element_type=F32)
    gs_ref[0], gs_ref[1] = split(grad_u * operator)
    gd_ref[0], gd_ref[1] = split(g_pos * u)


def score(negs, source, target, operator, g_pos):
    groups = len(negs)
    width, each = negs[0].shape
    edges = source.shape[1]
    out = pl.pallas_call(
        functools.partial(score_kernel, groups),
        out_shape=(
            jax.ShapeDtypeStruct((2, width, edges), BF16),
            jax.ShapeDtypeStruct((2, width, edges), BF16),
            *[jax.ShapeDtypeStruct((width, each), BF16)] * groups,
        ),
        in_specs=[whole()] * (groups + 4),
        out_specs=(whole(),) * (groups + 2),
        compiler_params=params(20 * MIB),
        cost_estimate=cost(6 * width * edges * groups * each),
        name="score",
    )(*negs, source, target, operator, g_pos)
    return out[0], out[1], out[2:]


def scatter_kernel(first, gs_ref, gd_ref, spos, dpos, out_ref):
    width, edges = gs_ref.shape[1:]

    def tile(t, _):
        index = lax.broadcasted_iota(jnp.int32, (TILE, edges), 0) + (first + t * TILE)
        both = None
        for grads, pos in ((gs_ref, spos), (gd_ref, dpos)):
            hot = jnp.where(index == pos[...], 1.0, 0.0).astype(BF16)
            part = lax.dot_general(
                grads[...].reshape(2 * width, edges), hot, NT, preferred_element_type=F32
            )
            both = part if both is None else both + part
        out_ref[:, pl.ds(pl.multiple_of(t * TILE, TILE), TILE)] = both[:width] + both[width:]
        return 0

    lax.fori_loop(0, out_ref.shape[1] // TILE, tile, 0)


def scatter(first, after, grads_src, grads_dst, spos, dpos):
    width, edges = grads_src.shape[1:]
    rows = (after - first) * BLK
    return pl.pallas_call(
        functools.partial(scatter_kernel, first * BLK),
        out_shape=jax.ShapeDtypeStruct((width, rows), F32),
        in_specs=[whole(), whole(), whole(), whole()],
        out_specs=whole(),
        compiler_params=params(4 * width * rows),
        cost_estimate=cost(4 * width * rows * edges),
        name="scatter",
    )(grads_src, grads_dst, spos, dpos)


def encode(x, out_ref):
    width = x.shape[0]
    top = jnp.max(jnp.abs(x), axis=0, keepdims=True)
    power = jnp.ceil(jnp.log2(jnp.maximum(top, 1e-30)) + 1e-3)
    code = jnp.round(x * (jnp.exp2(-power) * 32767.0))
    out_ref[:width, :] = code.astype(jnp.int32).astype(jnp.int16)
    tail = jnp.broadcast_to(power, (TAIL, x.shape[1]))
    out_ref[width:, :] = tail.astype(jnp.int32).astype(jnp.int16)


def decode(code, width):
    power = code[width:, :].astype(jnp.int32).astype(F32)[:1]
    return code[:width, :].astype(jnp.int32).astype(F32) * (jnp.exp2(power) * (1.0 / 32767.0))


def pack_kernel(first, bounds, peers, rank_ref, live_ref, npos, *refs):
    chunks, grads = refs[: len(bounds)], refs[len(bounds) : len(bounds) + peers]
    outs, total, slot = refs[len(bounds) + peers : -2], refs[-2], refs[-1]
    total[...] = sum(g[...].astype(F32) for g in grads).astype(BF16)
    for k, out_ref in enumerate(outs):
        alive = live_ref[first + k] > 0
        rank = rank_ref[first + k]

        for chunk, (low, high) in zip(chunks, bounds):

            @pl.when(alive & (rank >= low) & (rank < high))
            def _():
                lanes = pl.ds(pl.multiple_of((rank - low) * BLK, BLK), BLK)
                slot[...] = chunk[:, lanes]

        @pl.when(alive)
        def _():
            index = lax.broadcasted_iota(jnp.int32, (BLK, npos.shape[1]), 0) + rank * BLK
            hot = jnp.where(index == npos[...], 1.0, 0.0).astype(BF16)
            part = lax.dot_general(total[...], hot, NT, preferred_element_type=F32)
            encode(slot[...] + part, out_ref)

        @pl.when(jnp.logical_not(alive))
        def _():
            out_ref[...] = jnp.zeros(out_ref.shape, jnp.int16)


def pack(first, group, rank, live, chunks, bounds, grad_negs, npos):
    width = chunks[0].shape[0]
    return pl.pallas_call(
        functools.partial(pack_kernel, first, tuple(bounds), len(grad_negs)),
        out_shape=(jax.ShapeDtypeStruct((width + TAIL, BLK), jnp.int16),) * group,
        in_specs=[smem(), smem()] + [whole()] * (1 + len(chunks) + len(grad_negs)),
        out_specs=(whole(),) * group,
        scratch_shapes=[
            pltpu.VMEM((width, npos.shape[1]), BF16),
            pltpu.VMEM((width, BLK), F32),
        ],
        compiler_params=params(0),
        cost_estimate=cost(4 * width * BLK * BLK * group),
        name="pack",
    )(rank, live, npos, *chunks, *grad_negs)


def add_kernel(first, fresh, asked_ref, *refs):
    grad = refs[-1]
    backs = refs[: -1 if fresh else -2]
    width = grad.shape[0]
    if fresh:
        grad[...] = jnp.zeros_like(grad)
    for k, back in enumerate(backs):
        lanes = pl.ds(pl.multiple_of(asked_ref[first + k] * BLK, BLK), BLK)
        grad[:, lanes] += decode(back, width)


def add(first, asked, backs, grad, width, rows):
    fresh = grad is None
    extra = [] if fresh else [grad]
    return pl.pallas_call(
        functools.partial(add_kernel, first, fresh),
        out_shape=jax.ShapeDtypeStruct((width, rows), F32),
        in_specs=[smem()] + [whole()] * (len(backs) + len(extra)),
        out_specs=whole(),
        input_output_aliases={} if fresh else {len(backs) + 1: 0},
        compiler_params=params(0),
        cost_estimate=cost(width * BLK * len(backs) * 64),
        name="add",
    )(asked, *backs, *extra)


def update_kernel(first, asked_ref, *refs):
    backs = refs[:-7]
    grad, table_ref, state_ref, table_out, state_out, fresh, sems = refs[-7:]
    width, rows = grad.shape
    for k, back in enumerate(backs):
        lanes = pl.ds(pl.multiple_of(asked_ref[first + k] * BLK, BLK), BLK)
        grad[:, lanes] += decode(back, width)
    span = fresh.shape[1] // sems.shape[0]

    def copy(b):
        lanes = pl.ds(pl.multiple_of(b * span, span), span)
        return pltpu.make_async_copy(fresh.at[:, lanes], table_out.at[:, lanes], sems.at[b])

    for b in range(sems.shape[0]):
        for c in range(b * span, (b + 1) * span, BLK):
            lanes = slice(c, c + BLK)
            g = grad[:, lanes]
            new_state = state_ref[:, lanes] + jnp.sum(g * g, axis=0, keepdims=True) / width
            state_out[:, lanes] = new_state
            fresh[:, lanes] = table_ref[:, lanes] - 0.1 * g / (jnp.sqrt(new_state) + 1e-10)
        copy(b).start()
    for b in range(sems.shape[0]):
        copy(b).wait()


def update(first, asked, backs, grad, table, state, parts=4):
    width, rows = table.shape
    return pl.pallas_call(
        functools.partial(update_kernel, first),
        out_shape=(
            jax.ShapeDtypeStruct((width, rows), F32),
            jax.ShapeDtypeStruct((1, rows), F32),
        ),
        in_specs=[smem()] + [whole()] * (len(backs) + 3),
        out_specs=(anywhere(), whole()),
        scratch_shapes=[pltpu.VMEM((width, rows), F32), pltpu.SemaphoreType.DMA((parts,))],
        compiler_params=params(4 * width * rows),
        cost_estimate=cost(width * rows * 64),
        name="update",
    )(asked, *backs, grad, table, state)


def per_device(table, state, relations, rel_ids, block_list, src_pos, dst_pos, neg_pos):
    devices = lax.axis_size(AXES)
    named = devices // 2
    rows_dev, width = table.shape
    blocks = rows_dev // BLK
    wanted = lax.all_to_all(
        block_list.reshape(devices, 1, 1), AXES, split_axis=0, concat_axis=0, tiled=True
    )
    asked = wanted.reshape(devices)
    own_blocks = table.reshape(blocks, BLK, width).transpose(0, 2, 1).astype(BF16)
    outgoing = select(wanted, own_blocks)
    fetched = lax.all_to_all(outgoing, AXES, split_axis=0, concat_axis=0, tiled=True)
    operator = relations[rel_ids].T

    half = devices // 2
    far, near = list(range(devices - 1, half - 1, -1)), list(range(half - 1, -1, -1))
    lead = devices // 8
    order = far[:lead]
    for f, n in zip(far[lead:], near):
        order += [f, n]
    order += near[half - lead :]
    partners = lax.axis_index(AXES) ^ jnp.array(order, jnp.int32)
    ids = jnp.arange(devices, dtype=jnp.int32)
    seat = partners[:, None] == ids[None, :]
    named_by = jnp.max((src_pos // BLK)[:, None] == ids[None, :], axis=0).astype(jnp.int32)
    alive = jnp.sum(jnp.where(seat, named_by[None, :], 0), axis=1)
    rank = jnp.sum(jnp.where(ids[None, :] < ids[:, None], alive[None, :], 0), axis=1)
    place = jnp.sum(jnp.where(seat, rank[:, None], 0), axis=0)
    slot = jnp.arange(named, dtype=jnp.int32)
    live = jnp.sum(
        jnp.where((rank[None, :] == slot[:, None]) & (alive[None, :] > 0), partners[None, :], 0), axis=1
    )
    asked = jnp.sum(jnp.where(seat, asked[None, :], 0), axis=1)
    sizes = [cut * devices // sum(CUTS) for cut in CUTS]
    firsts = [sum(sizes[:g]) for g in range(len(sizes))]
    steps = [0] + [named * step // STEPS[-1] for step in STEPS]
    bounds = list(zip(steps[:-1], steps[1:]))

    def compact(pos):
        where = jnp.sum(jnp.where((pos // BLK)[:, None] == ids[None, :], place[None, :], 0), axis=1)
        return (where * BLK + pos % BLK).reshape(1, -1)

    spos, dpos, npos = compact(src_pos), compact(dst_pos), compact(neg_pos)
    fetched, operator, live, rank, alive, asked, spos, dpos, npos = lax.optimization_barrier(
        (fetched, operator, live, rank, alive, asked, spos, dpos, npos)
    )

    def swap(x, shift, axis):
        count = lax.axis_size(axis)
        return lax.ppermute(x, axis, [(i, i ^ shift) for i in range(count)])

    peers = lax.axis_size("dst")
    own_negs, rows = gather_negs(live, fetched, npos)
    negs = [own_negs] + [swap(own_negs, shift, "dst") for shift in range(1, peers)]
    source, target, g_pos = gather_edges(rows, spos, dpos, operator)
    grads_src, grads_dst, part_negs = score(negs, source, target, operator, g_pos)
    own_grad = [part_negs[0]] + [swap(part_negs[shift], shift, "dst") for shift in range(1, peers)]
    grad, chunks, flight, queue = None, [], [], []
    for g, (first, group) in enumerate(zip(firsts, sizes)):
        if g < len(bounds):
            edges_at = (spos, dpos)
            if g > 1:
                edges_at, flight[-group] = lax.optimization_barrier((edges_at, flight[-group]))
            chunks.append(scatter(*bounds[g], grads_src, grads_dst, *edges_at))
        packed = pack(first, group, rank, alive, chunks, bounds[: len(chunks)], own_grad, npos)
        for k, (x, shift) in enumerate(zip(packed, order[first : first + group])):
            i = first + k
            if i >= WINDOW:
                x, flight[i - WINDOW] = lax.optimization_barrier((x, flight[i - WINDOW]))
            if k == WINDOW and g > 1:
                x, grad = lax.optimization_barrier((x, grad))
            flight.append(swap(x, shift, AXES) if shift else x)
        if g:
            before = firsts[g - 1]
            grad = add(before, asked, flight[before:first], grad, width, rows_dev)
    backs = flight[firsts[-1] :]
    new_table, new_state = update(
        firsts[-1], asked, backs, grad, table.T, state.reshape(1, rows_dev)
    )
    return (new_table.T, new_state.reshape(rows_dev))


def solution(mesh):
    in_specs = (
        P(AXES, None),
        P(AXES),
        P(),
        P(AXES),
        P(AXES, None),
        P(AXES),
        P(AXES),
        P(AXES),
    )
    out_specs = (P(AXES, None), P(AXES))
    return jax.shard_map(
        per_device, mesh=mesh, in_specs=in_specs, out_specs=out_specs, check_vma=False
    )
```

```python
import functools

import jax
import jax.numpy as jnp
from jax import lax
from jax.experimental import pallas as pl
from jax.experimental.pallas import tpu as pltpu
from jax.sharding import PartitionSpec as P

BLK = 128
TAIL = 8
CUTS = (1, 2, 2, 2, 1)
STEPS = (2, 6, 8)
WINDOW = 5
TILE = 256
AXES = ("src", "dst")
F32 = jnp.float32
BF16 = jnp.bfloat16
NT = (((1,), (1,)), ((), ()))


def params(held):
    return pltpu.CompilerParams(vmem_limit_bytes=14 * 1024 * 1024 + held)


MIB = 1024 * 1024


def cost(flops):
    return pl.CostEstimate(flops=flops // 64, bytes_accessed=flops // 32768, transcendentals=0)


def whole():
    return pl.BlockSpec(memory_space=pltpu.VMEM)


def smem():
    return pl.BlockSpec(memory_space=pltpu.SMEM)


def anywhere():
    return pl.BlockSpec(memory_space=pl.ANY)


def select_kernel(asked_ref, blocks_ref, out_ref, sem):
    count = out_ref.shape[0]

    def copy(k):
        return pltpu.make_async_copy(blocks_ref.at[asked_ref[k, 0, 0]], out_ref.at[k], sem)

    def start(k, _):
        copy(k).start()
        return 0

    def wait(k, _):
        copy(k).wait()
        return 0

    lax.fori_loop(0, count, start, 0)
    lax.fori_loop(0, count, wait, 0)


def select(asked, blocks):
    devices = asked.shape[0]
    return pl.pallas_call(
        select_kernel,
        out_shape=jax.ShapeDtypeStruct((devices,) + blocks.shape[1:], blocks.dtype),
        in_specs=[smem(), anywhere()],
        out_specs=anywhere(),
        scratch_shapes=[pltpu.SemaphoreType.DMA],
        compiler_params=params(0),
        name="select",
    )(asked, blocks)


def load_live(live_ref, fetched, rows, sem):
    count = live_ref.shape[0]

    def copy(k):
        lanes = pl.ds(pl.multiple_of(k * BLK, BLK), BLK)
        return pltpu.make_async_copy(fetched.at[live_ref[k]], rows.at[:, lanes], sem)

    def start(k, _):
        copy(k).start()
        return 0

    def wait(k, _):
        copy(k).wait()
        return 0

    lax.fori_loop(0, count, start, 0)
    lax.fori_loop(0, count, wait, 0)


def pick(rows, positions):
    total = rows.shape[1]
    step = min(total, 2048)
    out = None
    for first in range(0, total, step):
        index = lax.broadcasted_iota(jnp.int32, (step, positions.shape[1]), 0) + first
        hot = jnp.where(index == positions, 1.0, 0.0).astype(BF16)
        part = jnp.dot(rows[:, first : first + step], hot, preferred_element_type=F32)
        out = part if out is None else out + part
    return out


def neg_kernel(live_ref, fetched, pos_ref, out_ref, rows, sem):
    load_live(live_ref, fetched, rows, sem)
    out_ref[...] = pick(rows, pos_ref[...]).astype(BF16)


def gather_negs(live, fetched, pos):
    width = fetched.shape[1]
    total = live.shape[0] * BLK
    return pl.pallas_call(
        neg_kernel,
        out_shape=(
            jax.ShapeDtypeStruct((width, pos.shape[1]), BF16),
            jax.ShapeDtypeStruct((width, total), BF16),
        ),
        in_specs=[smem(), anywhere(), whole()],
        out_specs=(whole(), whole()),
        scratch_shapes=[pltpu.SemaphoreType.DMA],
        compiler_params=params(4 * width * total),
        name="gather_negs",
    )(live, fetched, pos)


def edge_kernel(rows, spos, dpos, op_ref, src_ref, dst_ref, gpos_ref):
    source = pick(rows, spos[...])
    target = pick(rows, dpos[...])
    u = source * op_ref[...]
    positive = jnp.sum(u * target, axis=0, keepdims=True)
    gpos_ref[...] = -jax.nn.sigmoid(-positive)
    src_ref[...] = source.astype(BF16)
    dst_ref[...] = target.astype(BF16)


def gather_edges(rows, spos, dpos, operator, tile=512):
    width, total = rows.shape
    edges = spos.shape[1]
    lane = pl.BlockSpec((1, tile), lambda i: (0, i))
    column = pl.BlockSpec((width, tile), lambda i: (0, i))
    return pl.pallas_call(
        edge_kernel,
        grid=(edges // tile,),
        out_shape=(
            jax.ShapeDtypeStruct((width, edges), BF16),
            jax.ShapeDtypeStruct((width, edges), BF16),
            jax.ShapeDtypeStruct((1, edges), F32),
        ),
        in_specs=[whole(), lane, lane, column],
        out_specs=(column, column, lane),
        compiler_params=params(2 * width * total + 8 * MIB),
        cost_estimate=cost(4 * width * total * edges),
        name="gather_edges",
    )(rows, spos, dpos, operator)


def split(x):
    high = x.astype(BF16)
    return high, (x - high.astype(F32)).astype(BF16)


def score_kernel(groups, *refs):
    negs = refs[:groups]
    src_ref, dst_ref, op_ref, gpos_ref, gs_ref, gd_ref = refs[groups : groups + 6]
    outs = refs[groups + 6 : 2 * groups + 6]
    each = negs[0].shape[1]
    count = groups * each
    wide = jnp.concatenate([n[...] for n in negs], axis=1)
    tall = jnp.concatenate([n[...].T for n in negs], axis=0)
    operator = op_ref[...]
    u = src_ref[...].astype(F32) * operator
    u_half = u.astype(BF16)
    scores = jnp.dot(tall, u_half, preferred_element_type=F32)
    g_neg = (jax.nn.sigmoid(scores) / count).astype(BF16)
    sums = lax.dot_general(u_half, g_neg, NT, preferred_element_type=F32)
    for g in range(groups):
        outs[g][...] = sums[:, g * each : (g + 1) * each].astype(BF16)
    g_pos = gpos_ref[...]
    grad_u = g_pos * dst_ref[...].astype(F32) + jnp.dot(wide, g_neg, preferred_element_type=F32)
    gs_ref[0], gs_ref[1] = split(grad_u * operator)
    gd_ref[0], gd_ref[1] = split(g_pos * u)


def score(negs, source, target, operator, g_pos):
    groups = len(negs)
    width, each = negs[0].shape
    edges = source.shape[1]
    out = pl.pallas_call(
        functools.partial(score_kernel, groups),
        out_shape=(
            jax.ShapeDtypeStruct((2, width, edges), BF16),
            jax.ShapeDtypeStruct((2, width, edges), BF16),
            *[jax.ShapeDtypeStruct((width, each), BF16)] * groups,
        ),
        in_specs=[whole()] * (groups + 4),
        out_specs=(whole(),) * (groups + 2),
        compiler_params=params(20 * MIB),
        cost_estimate=cost(6 * width * edges * groups * each),
        name="score",
    )(*negs, source, target, operator, g_pos)
    return out[0], out[1], out[2:]


def scatter_kernel(first, gs_ref, gd_ref, spos, dpos, out_ref):
    width, edges = gs_ref.shape[1:]

    def tile(t, _):
        index = lax.broadcasted_iota(jnp.int32, (TILE, edges), 0) + (first + t * TILE)
        both = None
        for grads, pos in ((gs_ref, spos), (gd_ref, dpos)):
            hot = jnp.where(index == pos[...], 1.0, 0.0).astype(BF16)
            part = lax.dot_general(
                grads[...].reshape(2 * width, edges), hot, NT, preferred_element_type=F32
            )
            both = part if both is None else both + part
        out_ref[:, pl.ds(pl.multiple_of(t * TILE, TILE), TILE)] = both[:width] + both[width:]
        return 0

    lax.fori_loop(0, out_ref.shape[1] // TILE, tile, 0)


def scatter(first, after, grads_src, grads_dst, spos, dpos):
    width, edges = grads_src.shape[1:]
    rows = (after - first) * BLK
    return pl.pallas_call(
        functools.partial(scatter_kernel, first * BLK),
        out_shape=jax.ShapeDtypeStruct((width, rows), F32),
        in_specs=[whole(), whole(), whole(), whole()],
        out_specs=whole(),
        compiler_params=params(4 * width * rows),
        cost_estimate=cost(4 * width * rows * edges),
        name="scatter",
    )(grads_src, grads_dst, spos, dpos)


def encode(x, out_ref):
    width = x.shape[0]
    top = jnp.max(jnp.abs(x), axis=0, keepdims=True)
    power = jnp.ceil(jnp.log2(jnp.maximum(top, 1e-30)) + 1e-3)
    code = jnp.round(x * (jnp.exp2(-power) * 32767.0))
    out_ref[:width, :] = code.astype(jnp.int32).astype(jnp.int16)
    tail = jnp.broadcast_to(power, (TAIL, x.shape[1]))
    out_ref[width:, :] = tail.astype(jnp.int32).astype(jnp.int16)


def decode(code, width):
    power = code[width:, :].astype(jnp.int32).astype(F32)[:1]
    return code[:width, :].astype(jnp.int32).astype(F32) * (jnp.exp2(power) * (1.0 / 32767.0))


def pack_kernel(first, bounds, peers, rank_ref, live_ref, npos, *refs):
    chunks, grads = refs[: len(bounds)], refs[len(bounds) : len(bounds) + peers]
    outs, total, slot = refs[len(bounds) + peers : -2], refs[-2], refs[-1]
    width = slot.shape[0]
    total[:width], total[width:] = split(sum(g[...].astype(F32) for g in grads))
    for k, out_ref in enumerate(outs):
        alive = live_ref[first + k] > 0
        rank = rank_ref[first + k]

        for chunk, (low, high) in zip(chunks, bounds):

            @pl.when(alive & (rank >= low) & (rank < high))
            def _():
                lanes = pl.ds(pl.multiple_of((rank - low) * BLK, BLK), BLK)
                slot[...] = chunk[:, lanes]

        @pl.when(alive)
        def _():
            index = lax.broadcasted_iota(jnp.int32, (BLK, npos.shape[1]), 0) + rank * BLK
            hot = jnp.where(index == npos[...], 1.0, 0.0).astype(BF16)
            both = lax.dot_general(total[...], hot, NT, preferred_element_type=F32)
            encode(slot[...] + (both[:width] + both[width:]), out_ref)

        @pl.when(jnp.logical_not(alive))
        def _():
            out_ref[...] = jnp.zeros(out_ref.shape, jnp.int16)


def pack(first, group, rank, live, chunks, bounds, grad_negs, npos):
    width = chunks[0].shape[0]
    return pl.pallas_call(
        functools.partial(pack_kernel, first, tuple(bounds), len(grad_negs)),
        out_shape=(jax.ShapeDtypeStruct((width + TAIL, BLK), jnp.int16),) * group,
        in_specs=[smem(), smem()] + [whole()] * (1 + len(chunks) + len(grad_negs)),
        out_specs=(whole(),) * group,
        scratch_shapes=[
            pltpu.VMEM((2 * width, npos.shape[1]), BF16),
            pltpu.VMEM((width, BLK), F32),
        ],
        compiler_params=params(0),
        cost_estimate=cost(4 * width * BLK * BLK * group),
        name="pack",
    )(rank, live, npos, *chunks, *grad_negs)


def add_kernel(first, fresh, asked_ref, *refs):
    grad = refs[-1]
    backs = refs[: -1 if fresh else -2]
    width = grad.shape[0]
    if fresh:
        grad[...] = jnp.zeros_like(grad)
    for k, back in enumerate(backs):
        lanes = pl.ds(pl.multiple_of(asked_ref[first + k] * BLK, BLK), BLK)
        grad[:, lanes] += decode(back, width)


def add(first, asked, backs, grad, width, rows):
    fresh = grad is None
    extra = [] if fresh else [grad]
    return pl.pallas_call(
        functools.partial(add_kernel, first, fresh),
        out_shape=jax.ShapeDtypeStruct((width, rows), F32),
        in_specs=[smem()] + [whole()] * (len(backs) + len(extra)),
        out_specs=whole(),
        input_output_aliases={} if fresh else {len(backs) + 1: 0},
        compiler_params=params(0),
        cost_estimate=cost(width * BLK * len(backs) * 64),
        name="add",
    )(asked, *backs, *extra)


def update_kernel(first, asked_ref, *refs):
    backs = refs[:-7]
    grad, table_ref, state_ref, table_out, state_out, fresh, sems = refs[-7:]
    width, rows = grad.shape
    for k, back in enumerate(backs):
        lanes = pl.ds(pl.multiple_of(asked_ref[first + k] * BLK, BLK), BLK)
        grad[:, lanes] += decode(back, width)
    span = fresh.shape[1] // sems.shape[0]

    def copy(b):
        lanes = pl.ds(pl.multiple_of(b * span, span), span)
        return pltpu.make_async_copy(fresh.at[:, lanes], table_out.at[:, lanes], sems.at[b])

    for b in range(sems.shape[0]):
        for c in range(b * span, (b + 1) * span, BLK):
            lanes = slice(c, c + BLK)
            g = grad[:, lanes]
            new_state = state_ref[:, lanes] + jnp.sum(g * g, axis=0, keepdims=True) / width
            state_out[:, lanes] = new_state
            fresh[:, lanes] = table_ref[:, lanes] - 0.1 * g / (jnp.sqrt(new_state) + 1e-10)
        copy(b).start()
    for b in range(sems.shape[0]):
        copy(b).wait()


def update(first, asked, backs, grad, table, state, parts=4):
    width, rows = table.shape
    return pl.pallas_call(
        functools.partial(update_kernel, first),
        out_shape=(
            jax.ShapeDtypeStruct((width, rows), F32),
            jax.ShapeDtypeStruct((1, rows), F32),
        ),
        in_specs=[smem()] + [whole()] * (len(backs) + 3),
        out_specs=(anywhere(), whole()),
        scratch_shapes=[pltpu.VMEM((width, rows), F32), pltpu.SemaphoreType.DMA((parts,))],
        compiler_params=params(4 * width * rows),
        cost_estimate=cost(width * rows * 64),
        name="update",
    )(asked, *backs, grad, table, state)


def per_device(table, state, relations, rel_ids, block_list, src_pos, dst_pos, neg_pos):
    devices = lax.axis_size(AXES)
    named = devices // 2
    rows_dev, width = table.shape
    blocks = rows_dev // BLK
    wanted = lax.all_to_all(
        block_list.reshape(devices, 1, 1), AXES, split_axis=0, concat_axis=0, tiled=True
    )
    asked = wanted.reshape(devices)
    own_blocks = table.reshape(blocks, BLK, width).transpose(0, 2, 1).astype(BF16)
    outgoing = select(wanted, own_blocks)
    fetched = lax.all_to_all(outgoing, AXES, split_axis=0, concat_axis=0, tiled=True)
    operator = relations[rel_ids].T

    half = devices // 2
    far, near = list(range(devices - 1, half - 1, -1)), list(range(half - 1, -1, -1))
    lead = devices // 8
    order = far[:lead]
    for f, n in zip(far[lead:], near):
        order += [f, n]
    order += near[half - lead :]
    partners = lax.axis_index(AXES) ^ jnp.array(order, jnp.int32)
    ids = jnp.arange(devices, dtype=jnp.int32)
    seat = partners[:, None] == ids[None, :]
    named_by = jnp.max((src_pos // BLK)[:, None] == ids[None, :], axis=0).astype(jnp.int32)
    alive = jnp.sum(jnp.where(seat, named_by[None, :], 0), axis=1)
    rank = jnp.sum(jnp.where(ids[None, :] < ids[:, None], alive[None, :], 0), axis=1)
    place = jnp.sum(jnp.where(seat, rank[:, None], 0), axis=0)
    slot = jnp.arange(named, dtype=jnp.int32)
    live = jnp.sum(
        jnp.where((rank[None, :] == slot[:, None]) & (alive[None, :] > 0), partners[None, :], 0), axis=1
    )
    asked = jnp.sum(jnp.where(seat, asked[None, :], 0), axis=1)
    sizes = [cut * devices // sum(CUTS) for cut in CUTS]
    firsts = [sum(sizes[:g]) for g in range(len(sizes))]
    steps = [0] + [named * step // STEPS[-1] for step in STEPS]
    bounds = list(zip(steps[:-1], steps[1:]))

    def compact(pos):
        where = jnp.sum(jnp.where((pos // BLK)[:, None] == ids[None, :], place[None, :], 0), axis=1)
        return (where * BLK + pos % BLK).reshape(1, -1)

    spos, dpos, npos = compact(src_pos), compact(dst_pos), compact(neg_pos)
    fetched, operator, live, rank, alive, asked, spos, dpos, npos = lax.optimization_barrier(
        (fetched, operator, live, rank, alive, asked, spos, dpos, npos)
    )

    def swap(x, shift, axis):
        count = lax.axis_size(axis)
        return lax.ppermute(x, axis, [(i, i ^ shift) for i in range(count)])

    peers = lax.axis_size("dst")
    own_negs, rows = gather_negs(live, fetched, npos)
    negs = [own_negs] + [swap(own_negs, shift, "dst") for shift in range(1, peers)]
    source, target, g_pos = gather_edges(rows, spos, dpos, operator)
    grads_src, grads_dst, part_negs = score(negs, source, target, operator, g_pos)
    own_grad = [part_negs[0]] + [swap(part_negs[shift], shift, "dst") for shift in range(1, peers)]
    grad, chunks, flight, queue = None, [], [], []
    for g, (first, group) in enumerate(zip(firsts, sizes)):
        if g < len(bounds):
            edges_at = (spos, dpos)
            if g > 1:
                edges_at, flight[-group] = lax.optimization_barrier((edges_at, flight[-group]))
            chunks.append(scatter(*bounds[g], grads_src, grads_dst, *edges_at))
        packed = pack(first, group, rank, alive, chunks, bounds[: len(chunks)], own_grad, npos)
        for k, (x, shift) in enumerate(zip(packed, order[first : first + group])):
            i = first + k
            if i >= WINDOW:
                x, flight[i - WINDOW] = lax.optimization_barrier((x, flight[i - WINDOW]))
            if k == WINDOW and g > 1:
                x, grad = lax.optimization_barrier((x, grad))
            flight.append(swap(x, shift, AXES) if shift else x)
        if g:
            before = firsts[g - 1]
            grad = add(before, asked, flight[before:first], grad, width, rows_dev)
    backs = flight[firsts[-1] :]
    new_table, new_state = update(
        firsts[-1], asked, backs, grad, table.T, state.reshape(1, rows_dev)
    )
    return (new_table.T, new_state.reshape(rows_dev))


def solution(mesh):
    in_specs = (
        P(AXES, None),
        P(AXES),
        P(),
        P(AXES),
        P(AXES, None),
        P(AXES),
        P(AXES),
        P(AXES),
    )
    out_specs = (P(AXES, None), P(AXES))
    return jax.shard_map(
        per_device, mesh=mesh, in_specs=in_specs, out_specs=out_specs, check_vma=False
    )
```
